32 devices in a mesh: groups: 2 (over y), space: 8 (over z, x), dp: 2 (over core).
Axes of the slice: x: 2, y: 2, z: 4, core: 2. Of those that a mesh axis runs over, the one named last changes fastest.
Arguments:
- features: bfloat16 [4, 16, 8, 8, 512], P(('groups', 'dp'), 'space'), parts along dimension 0, may hold values from -6 to 6
- cotangent: bfloat16 [4, 16, 8, 8, 512], P(('groups', 'dp'), 'space'), parts along dimension 0, may hold values from -6 to 6
- kernel: bfloat16 [3, 3, 3, 64, 64], replicated, may hold values from -0.15625 to 0.15625
- neighbours: int32 [4, 16, 6], P(('groups', 'dp'), 'space'), parts along dimension 0, may hold values from -1 to 15, as said below
Outputs:
- response: bfloat16 [4, 16, 8, 8, 512], P(('groups', 'dp'), 'space'), parts along dimension 0
- feature_grad: bfloat16 [4, 16, 8, 8, 512], P(('groups', 'dp'), 'space'), parts along dimension 0
- kernel_grad: float32 [6, 3, 3, 64, 64], P('groups'), parts along dimension 0
The draws below stay inside these ranges and needn't reach their ends.
There are 2 independent parts, one for each index of `groups`. The reference program is written for one: setup_inputs(seed, part) draws one part's arguments, and reference() takes and returns one part's arrays. A program takes and returns all parts, laid end to end along the dimension named above; an argument that names none is the same for every part. Nothing has to cross between parts.
Inputs may be any that keep to these rules, and one draw needn't show every extreme that they name: `neighbours`: the active bricks lie on a lattice of 3 by 8 by 4 bricks. Tile t sits at position p = t + 2: it covers lattice row p // 4 of the first dimension, rows 2 * (p % 4) to 2 * (p % 4) + 1 of the second and all rows of the third; it holds exactly 2 active bricks, in slots 2 * t to 2 * t + 1, listed by second then third lattice coordinate. In each realization one third-dimension row z is drawn, and every tile holds the bricks at z in its first and in its last second-dimension row; its other bricks are drawn at random. Directions are first dimension down, up, second down, up, third down, up; the relation is symmetric (if brick u is the up neighbour of s, s is the down neighbour of u), and -1 marks a neighbour that is inactive or outside the lattice.
All inputs are finite; a program needn't handle non-finite values.
Results may differ from the reference program's by a relative error of at most 0.0045.
Values may be sent and summed in bfloat16 or wider, within the bound.
No kernel may reach another device: no remote copies, remote signals or barrier semaphores. Data moves between devices by JAX's collectives and lax.ppermute only.
A program may use at most 64 MiB of HBM per device.

```python
import math
import jax
import jax.numpy as jnp
from jax import lax

CHANNELS = 64
BRICK = 8
DEPTH_BRICKS = 4
TILES_Y = 4
BRICKS_DEV = 2
BRICKS = 16
REALIZATIONS = 2


def draw_neighbours(key, part):
    tile_count = BRICKS // BRICKS_DEV
    lattice_x = tile_count // TILES_Y + 1
    lattice_y = TILES_Y * BRICKS_DEV
    places = DEPTH_BRICKS * BRICKS_DEV
    keys_all = jax.random.split(key, REALIZATIONS * tile_count)
    spine_depth = jax.random.randint(jax.random.fold_in(key, 7), (REALIZATIONS,), 0, DEPTH_BRICKS).astype(jnp.int32)
    spine_all = jnp.repeat(spine_depth, tile_count)
    place_ids = jnp.arange(places, dtype=jnp.int32)

    def choose(sub_key, spine_z):
        priority = jax.random.permutation(sub_key, places).astype(jnp.int32)
        first_spine = spine_z
        last_spine = (BRICKS_DEV - 1) * DEPTH_BRICKS + spine_z
        forced = (place_ids == first_spine) | (place_ids == last_spine)
        priority = jnp.where(forced, -1, priority)
        order = jnp.argsort(priority, stable=True).astype(jnp.int32)
        return jnp.sort(order[:BRICKS_DEV])
    chosen = jax.vmap(choose)(keys_all, spine_all).reshape(REALIZATIONS, tile_count, BRICKS_DEV).astype(jnp.int32)
    tile_ids = jnp.arange(tile_count, dtype=jnp.int32)
    placed = tile_ids + TILES_Y // 2
    coord_x = jnp.broadcast_to((placed // TILES_Y)[None, :, None], chosen.shape)
    coord_y = (placed % TILES_Y * BRICKS_DEV)[None, :, None] + chosen // DEPTH_BRICKS
    coord_z = chosen % DEPTH_BRICKS
    slot_grid = jnp.broadcast_to(jnp.arange(BRICKS, dtype=jnp.int32).reshape(1, tile_count, BRICKS_DEV), chosen.shape)
    cells_total = lattice_x * lattice_y * DEPTH_BRICKS

    def linear(along_x, along_y, along_z):
        return (along_x * lattice_y + along_y) * DEPTH_BRICKS + along_z

    def per_realization(first_c, second_c, third_c, slot_part):
        table = jnp.full((cells_total,), -1, jnp.int32).at[linear(first_c, second_c, third_c).ravel()].set(slot_part.ravel())
        columns = []
        for step_x, step_y, step_z in ((-1, 0, 0), (1, 0, 0), (0, -1, 0), (0, 1, 0), (0, 0, -1), (0, 0, 1)):
            near_x = first_c + step_x
            near_y = second_c + step_y
            near_z = third_c + step_z
            inside = (near_x >= 0) & (near_x < lattice_x) & (near_y >= 0) & (near_y < lattice_y) & (near_z >= 0) & (near_z < DEPTH_BRICKS)
            found = table[jnp.where(inside, linear(near_x, near_y, near_z), 0)]
            columns.append(jnp.where(inside, found, -1).ravel())
        return jnp.stack(columns, axis=-1)
    return jax.vmap(per_realization)(coord_x, coord_y, coord_z, slot_grid).astype(jnp.int32)


def level_of(key, extent, cuts, smallest, top_value):
    factor_of, own = 1.0, jax.random.fold_in(key, 6)
    for position, parts in cuts:
        draws = jnp.exp(jax.random.uniform(jax.random.fold_in(own, position), (parts,), jnp.float32, smallest / len(cuts), top_value / len(cuts)))
        factor_of = factor_of * jnp.repeat(draws, extent[position] // parts).reshape([-1 if axis == position else 1 for axis in range(len(extent))])
    return factor_of


def gaussian(own_key, shape, width, most, pieces=(), kind=jnp.bfloat16):
    entries = width * jax.random.normal(own_key, shape, jnp.float32)
    if pieces:
        entries = entries * level_of(own_key, shape, pieces, -0.22, 0.18)
    return jnp.clip(entries, -most, most).astype(kind)


def setup_inputs(seed: int = 0, part: int = 0) -> dict:
    arg_keys = jax.random.split(jax.random.key(seed), 5)
    part_keys = jax.random.split(jax.random.fold_in(arg_keys[4], part), 5)
    return {
        "features": gaussian(part_keys[0], (REALIZATIONS, BRICKS, BRICK, BRICK, BRICK * CHANNELS), 1.0, 6.0, ((0, 2), (1, 8))),
        "cotangent": gaussian(part_keys[1], (REALIZATIONS, BRICKS, BRICK, BRICK, BRICK * CHANNELS), 1.0, 6.0, ((0, 2), (1, 8))),
        "kernel": gaussian(arg_keys[2], (3, 3, 3, CHANNELS, CHANNELS), (27 * CHANNELS) ** -0.5, 0.15625),
        "neighbours": draw_neighbours(jax.random.fold_in(jax.random.fold_in(arg_keys[4], part), 71), part),
    }


def pick_rows(values, slots):
    present = slots >= 0
    picked = jnp.take(values, jnp.where(present, slots, 0).astype(jnp.int32), axis=0)
    shape_tail = (1,) * (values.ndim - 1)
    return jnp.where(present.reshape((-1,) + shape_tail), picked, jnp.zeros_like(picked))

def extend(volume, slots):
    for axis_dim, columns in zip((1, 2, 3), ((0, 1), (2, 3), (4, 5))):
        length = volume.shape[axis_dim]
        upper_face = lax.slice_in_dim(volume, length - 1, length, axis=axis_dim)
        lower_face = lax.slice_in_dim(volume, 0, 1, axis=axis_dim)
        below = pick_rows(upper_face, slots[:, columns[0]])
        above = pick_rows(lower_face, slots[:, columns[1]])
        volume = jnp.concatenate([below, volume, above], axis=axis_dim)
    return volume

def reference(features, cotangent, kernel, neighbours):
    kernel_wide = kernel.astype(jnp.float32)

    def single(inputs):
        volume_in, cotangent_in, slots = inputs
        volume_wide = volume_in.reshape(BRICKS, BRICK, BRICK, BRICK, CHANNELS).astype(jnp.float32)
        seed_grad = cotangent_in.reshape(BRICKS, BRICK, BRICK, BRICK, CHANNELS).astype(jnp.float32)

        def forward(volume, weights):
            return lax.conv_general_dilated(extend(volume, slots), weights, (1, 1, 1), 'VALID', dimension_numbers=('NDHWC', 'DHWIO', 'NDHWC'), precision=lax.Precision.HIGHEST)
        output, pullback = jax.vjp(forward, volume_wide, kernel_wide)
        volume_grad, weight_grad = pullback(seed_grad)
        shaped = (BRICKS, BRICK, BRICK, BRICK * CHANNELS)
        return (output.astype(jnp.bfloat16).reshape(shaped), volume_grad.astype(jnp.bfloat16).reshape(shaped), weight_grad)
    response, feature_grad, weight_parts = lax.map(single, (features, cotangent, neighbours))
    scale_factor = 1.0 / math.sqrt(REALIZATIONS * BRICKS * BRICK ** 3)
    kernel_grad = lax.optimization_barrier(jnp.sum(weight_parts, axis=0)) * scale_factor
    return (response, feature_grad, kernel_grad)
```

```python
import functools
import math

import jax
import jax.numpy as jnp
import numpy as np
from jax import lax
from jax.experimental import pallas as pl
from jax.experimental.pallas import tpu as pltpu
from jax.sharding import PartitionSpec as P

TILES_Y = 4
F32 = jnp.float32
BF16 = jnp.bfloat16


def step_y(tile, sign, tiles):
    column = (tile + TILES_Y // 2) % TILES_Y + sign
    near = tile + sign
    return near if 0 <= column < TILES_Y and 0 <= near < tiles else None


def step_x(tile, sign, tiles):
    near = tile + sign * TILES_Y
    return near if 0 <= near < tiles else None


def path(tile, first, second, tiles):
    for axis, sign in (first, second):
        tile = None if tile is None else (step_x if axis == "x" else step_y)(tile, sign, tiles)
    return tile


def rounds(edges):
    found = []
    for edge in edges:
        for one in found:
            if edge[0] not in one and edge[1] not in one:
                break
        else:
            one = {}
            found.append(one)
        one[edge[0]] = (edge[1], edge[2])
        one[edge[1]] = (edge[0], edge[3])
    return found


def make_plan(tiles):
    along_x, along_y, corners = [], [], []
    for tile in range(tiles):
        up = step_x(tile, 1, tiles)
        if up is not None:
            along_x.append((tile, up, (1,), (0,)))
        up = step_y(tile, 1, tiles)
        if up is not None:
            along_y.append((tile, up, (1,), (0,)))
        for sign in (-1, 1):
            column = (tile + TILES_Y // 2) % TILES_Y + sign
            far = tile + TILES_Y + sign
            if not 0 <= column < TILES_Y or far >= tiles:
                continue
            x_up, x_down, y_to, y_back = ("x", 1), ("x", -1), ("y", sign), ("y", -sign)
            here = (path(tile, y_to, x_up, tiles) == far, path(tile, x_up, y_to, tiles) == far)
            there = (path(far, y_back, x_down, tiles) == tile, path(far, x_down, y_back, tiles) == tile)
            if any(here) or any(there):
                side = int(sign > 0)
                corners.append((tile, far, (2 + side, *map(int, here)), (1 - side, *map(int, there))))
    plan = [rounds(along_x), rounds(along_y), rounds(corners)]
    table = []
    for tile in range(tiles):
        row = []
        for kind, width in zip(plan, (1, 1, 3)):
            for one in kind:
                row.extend(one[tile][1] if tile in one else (-1,) + (0,) * (width - 1))
        table.append(row)
    pairs = [[[(tile, one[tile][0]) for tile in sorted(one)] for one in kind] for kind in plan]
    return pairs, np.asarray(table, np.int32)


class Roles:
    def __init__(self, table_ref, counts):
        self.row = lax.axis_index("space")
        self.table, self.counts = table_ref, counts

    def x(self, number):
        return self.table[self.row, number]

    def y(self, number):
        return self.table[self.row, self.counts[0] + number]

    def corner(self, number, field):
        return self.table[self.row, self.counts[0] + self.counts[1] + 3 * number + field]


def faces_kernel(counts, table_ref, f_ref, c_ref, *out_refs):
    roles = Roles(table_ref, counts)
    edge = f_ref.shape[1]
    x_refs = out_refs[: counts[0]]
    y_refs = out_refs[counts[0] : counts[0] + counts[1]]
    corner_refs = out_refs[counts[0] + counts[1] :]
    for number, out in enumerate(x_refs):
        plane = jnp.where(roles.x(number) == 1, edge - 1, 0)
        for source, ref in enumerate((f_ref, c_ref)):
            for brick in range(2):
                out[source, brick] = ref[brick, plane]
    rows = []
    for ref in (f_ref, c_ref):
        low = ref[0].astype(F32)[:, 0, :]
        high = ref[1].astype(F32)[:, edge - 1, :]
        rows.append((low, high))
    for number, out in enumerate(y_refs):
        up = roles.y(number) == 1
        for source, (low, high) in enumerate(rows):
            out[source] = jnp.where(up, high, low).astype(BF16)
    for number, out in enumerate(corner_refs):
        slot = roles.corner(number, 0)
        for source, (low, high) in enumerate(rows):
            at_low = jnp.where(slot >= 2, low[edge - 1 : edge], low[0:1])
            at_high = jnp.where(slot >= 2, high[edge - 1 : edge], high[0:1])
            line = jnp.where(slot % 2 == 1, at_high, at_low)
            out[source] = jnp.broadcast_to(line, out.shape[1:]).astype(BF16)


def padded(x, channels):
    zeros = jnp.zeros(x.shape[:-1] + (2 * channels,), F32)
    return pltpu.roll(jnp.concatenate([x, zeros], axis=-1), channels, x.ndim - 1)


def masked(keep, x):
    return jnp.where(keep, x, jnp.zeros_like(x))


def weights_kernel(kernel_ref, forward_ref, backward_ref, wide):
    channels = kernel_ref.shape[-1]
    wide[...] = jnp.zeros_like(wide)
    wide[:, :, :channels] = kernel_ref[...].astype(F32)
    for tap in range(9):
        plain = [wide[3 * tap + d] for d in range(3)]
        moved = [pltpu.roll(x, channels, 1) for x in plain]
        steps = (plain[0], plain[1] + moved[0], plain[2] + moved[1], moved[2])
        for number, block in enumerate(steps):
            forward_ref[tap, channels * number : channels * (number + 1), :] = block.astype(BF16)
        last = 8 - tap
        lanes = 2 * channels
        backward_ref[last, :channels, :lanes] = (plain[2] + moved[1]).astype(BF16)
        backward_ref[last, :channels, lanes:] = plain[0].astype(BF16)
        backward_ref[last, channels:, :lanes] = moved[2].astype(BF16)
        backward_ref[last, channels:, lanes:] = (plain[1] + moved[0]).astype(BF16)


def kernel_grad_kernel(counts, channels, table_ref, link_ref, f_ref, c_ref, *refs):
    roles = Roles(table_ref, counts)
    x_refs = refs[: counts[0]]
    y_refs = refs[counts[0] : counts[0] + counts[1]]
    keep_ref, send_ref, wide, tall, packed = refs[counts[0] + counts[1] :]
    bricks, edge, _, width = f_ref.shape
    rows = edge * edge
    wide[:, edge : edge + rows, :] = padded(f_ref[...].astype(F32).reshape(bricks, rows, width), channels)
    for side in range(2):
        start = side * (edge + rows)
        plane = jnp.zeros((bricks, edge, width), F32)
        for number, ref in enumerate(x_refs):
            plane = jnp.where(roles.x(number) == side, ref[0].astype(F32), plane)
        plane = padded(plane, channels)
        for brick in range(bricks):
            wide[brick, start : start + edge, :] = masked(link_ref[brick, side] >= 0, plane[brick])
    own = c_ref[...].astype(F32)
    tall[:, :, edge : 2 * edge, :] = own
    tall[1, :, edge - 1 : edge, :] = masked(link_ref[1, 2] >= 0, own[0, :, edge - 1 :, :])
    tall[0, :, 2 * edge : 2 * edge + 1, :] = masked(link_ref[0, 3] >= 0, own[1, :, 0:1, :])
    for side in range(2):
        row = jnp.zeros((edge, width), F32)
        for number, ref in enumerate(y_refs):
            row = jnp.where(roles.y(number) == side, ref[1].astype(F32), row)
        at = 2 * edge if side else edge - 1
        tall[side, :, at : at + 1, :] = masked(link_ref[side, 2 + side] >= 0, row)[:, None, :]
    lanes = 2 * channels
    pairs = width // lanes
    right = []
    for col in range(3):
        value = tall[:, :, edge + 1 - col : 2 * edge + 1 - col, :].reshape(bricks * rows, width).astype(BF16)
        right.append(jnp.concatenate([value[:, lanes * k : lanes * (k + 1)] for k in range(pairs)], axis=0))
    right = jnp.concatenate(right, axis=1)
    low = lax.broadcasted_iota(jnp.int32, (3 * channels // 2, lanes), 1) < channels
    half = 3 * channels // 2
    for row in range(3):
        value = wide[:, edge * row : edge * row + rows, :].reshape(bricks * rows, -1).astype(BF16)
        left = jnp.concatenate([value[:, lanes * k : lanes * (k + 2)] for k in range(pairs)], axis=0)
        grad = lax.dot_general(left, right, (((0,), (0,)), ((), ())), preferred_element_type=F32)
        for col in range(3):
            block = grad[:, lanes * col : lanes * (col + 1)]
            moved = pltpu.roll(block, channels, 1)
            first = block[:half] + moved[channels : channels + half]
            second = moved[half : 2 * half] + block[channels + half :]
            at = half * (3 * row + col)
            packed[at : at + half, :] = jnp.where(low, first, second)
    count = keep_ref.shape[0]
    core = lax.axis_index("dp")
    keep_ref[...] = packed[pl.ds(pl.multiple_of(core * count, 8), count), :]
    send_ref[...] = packed[pl.ds(pl.multiple_of((1 - core) * count, 8), count), :]


def conv_kernel(counts, channels, source, table_ref, link_ref, v_ref, weight_ref, *refs):
    roles = Roles(table_ref, counts)
    x_refs = refs[: counts[0]]
    y_refs = refs[counts[0] : counts[0] + counts[1]]
    corner_refs = refs[counts[0] + counts[1] : sum(counts)]
    out_ref, ext = refs[sum(counts) :]
    bricks, edge, _, width = v_ref.shape
    rows = edge * edge
    first, last = edge, 2 * edge - 1
    ext[:, 1 : edge + 1, first : last + 1, :] = padded(v_ref[...].astype(F32), channels)
    for side in range(2):
        plane = jnp.zeros((bricks, edge, width), F32)
        for number, ref in enumerate(x_refs):
            plane = jnp.where(roles.x(number) == side, ref[source].astype(F32), plane)
        plane = padded(plane, channels)
        for brick in range(bricks):
            ext[brick, side * (edge + 1), first : last + 1, :] = masked(link_ref[brick, side] >= 0, plane[brick])
    for side in range(2):
        row = jnp.zeros((edge, width), F32)
        for number, ref in enumerate(y_refs):
            row = jnp.where(roles.y(number) == side, ref[source].astype(F32), row)
        at = last + 1 if side else first - 1
        row = masked(link_ref[side, 2 + side] >= 0, padded(row, channels))
        ext[side, 1 : edge + 1, at : at + 1, :] = row[:, None, :]
        for across in range(2):
            line = jnp.zeros((1, width), F32)
            for number, ref in enumerate(corner_refs):
                hit = (roles.corner(number, 0) == 2 * across + side) & (roles.corner(number, 1 + source) == 1)
                line = jnp.where(hit, ref[source, 0:1].astype(F32), line)
            ext[side, across * (edge + 1), at : at + 1, :] = padded(line, channels)
    ext[1, :, first - 1 : first, :] = masked(link_ref[1, 2] >= 0, ext[0, :, last : last + 1, :])
    ext[0, :, last + 1 : last + 2, :] = masked(link_ref[0, 3] >= 0, ext[1, :, first : first + 1, :])
    lanes = 2 * channels
    pairs = width // lanes
    total = jnp.zeros((pairs * bricks * rows, lanes), F32)
    contract = 0 if source == 0 else 1
    for col in range(3):
        for row in range(3):
            value = ext[:, row : row + edge, first - 1 + col : last + col, :]
            value = value.reshape(bricks * rows, -1).astype(BF16)
            left = jnp.concatenate([value[:, lanes * k : lanes * (k + 2)] for k in range(pairs)], axis=0)
            total = total + lax.dot_general(
                left, weight_ref[3 * row + col], (((1,), (contract,)), ((), ())), preferred_element_type=F32
            )
    for k in range(pairs):
        out_ref[:, lanes * k : lanes * (k + 1)] = total[bricks * rows * k : bricks * rows * (k + 1)].astype(BF16)


def unpack_kernel(factor, own_ref, other_ref, out_ref, packed):
    count = own_ref.shape[0]
    core = lax.axis_index("dp")
    packed[pl.ds(pl.multiple_of(core * count, 8), count), :] = own_ref[...] * factor
    packed[pl.ds(pl.multiple_of((1 - core) * count, 8), count), :] = other_ref[...] * factor
    taps, rows, channels = out_ref.shape
    half = rows // 2
    for tap in range(taps):
        block = packed[half * tap : half * (tap + 1), :]
        out_ref[tap, :half, :] = block[:, :channels]
        out_ref[tap, half:, :] = pltpu.roll(block, channels, 1)[:, :channels]


VMEM = pl.BlockSpec(memory_space=pltpu.VMEM)
SMEM = pl.BlockSpec(memory_space=pltpu.SMEM)


def call(kernel, in_specs, out_shapes, scratch=(), flops=0, name=None):
    several = isinstance(out_shapes, list)
    return pl.pallas_call(
        kernel,
        in_specs=in_specs,
        out_specs=[VMEM] * len(out_shapes) if several else VMEM,
        out_shape=out_shapes,
        scratch_shapes=list(scratch),
        compiler_params=pltpu.CompilerParams(vmem_limit_bytes=24 * 2**20),
        cost_estimate=pl.CostEstimate(flops=flops, bytes_accessed=2**20, transcendentals=0),
        name=name,
    )


def body(tiles, features, cotangent, kernel, neighbours):
    pairs, table = make_plan(tiles)
    counts = tuple(len(kind) for kind in pairs)
    table = jnp.asarray(table)
    bricks, edge = features.shape[1:3]
    width = features.shape[-1]
    channels = kernel.shape[-1]
    rows = edge * edge
    lanes = 2 * channels
    shape = jax.ShapeDtypeStruct
    f = features.reshape(bricks, edge, edge, width)
    c = cotangent.reshape(bricks, edge, edge, width)
    links = neighbours.reshape(bricks, 6)

    face_shapes = [(2, bricks, edge, width)] * counts[0] + [(2, edge, width)] * counts[1] + [(2, 8, width)] * counts[2]
    faces = call(
        functools.partial(faces_kernel, counts),
        [SMEM, VMEM, VMEM],
        [shape(s, BF16) for s in face_shapes],
        name="faces",
    )(table, f, c)
    flat_pairs = [one for kind in pairs for one in kind]
    near = counts[0] + counts[1]
    got = [lax.ppermute(x, "space", one) for x, one in zip(faces[:near], flat_pairs)]
    forward, backward = call(
        weights_kernel,
        [VMEM],
        [shape((9, 4 * channels, lanes), BF16), shape((9, lanes, 4 * channels), BF16)],
        [pltpu.VMEM((27, channels, lanes), F32)],
        name="weights",
    )(kernel.reshape(27, channels, channels))

    count = 27 * channels * channels // lanes // 2
    keep, send = call(
        functools.partial(kernel_grad_kernel, counts, channels),
        [SMEM, SMEM, VMEM, VMEM] + [VMEM] * near,
        [shape((count, lanes), F32)] * 2,
        [
            pltpu.VMEM((bricks, rows + 2 * edge, width + lanes), F32),
            pltpu.VMEM((bricks, edge, 3 * edge, width), F32),
            pltpu.VMEM((2 * count, lanes), F32),
        ],
        flops=2 * 768 * 384 * 512,
        name="kernel_grad",
    )(table, links, f, c, *got)

    swap = [(0, 1), (1, 0)]
    part = keep + lax.ppermute(send, "dp", swap)
    got += [lax.ppermute(x, "space", one) for x, one in zip(faces[near:], flat_pairs[near:])]

    def conv(source, x, weight):
        return call(
            functools.partial(conv_kernel, counts, channels, source),
            [SMEM, SMEM, VMEM, VMEM] + [VMEM] * len(got),
            shape((bricks * rows, width), BF16),
            [pltpu.VMEM((bricks, edge + 2, 3 * edge, width + lanes), F32)],
            flops=2 * 512 * 256 * 128 * 9,
            name="response" if source == 0 else "feature_grad",
        )(table, links, x, weight, *got)

    response = conv(0, f, forward).reshape(features.shape)
    feature_grad = conv(1, c, backward).reshape(features.shape)
    steps = tiles.bit_length() - 1
    wire = BF16 if steps <= 3 else F32
    for number in range(steps):
        mine = lax.optimization_barrier(part.astype(wire))
        theirs = lax.ppermute(mine, "space", [(i, i ^ (1 << number)) for i in range(tiles)])
        part = mine.astype(F32) + theirs.astype(F32)
    other = lax.ppermute(part, "dp", swap)
    cells = bricks * tiles * lax.axis_size("dp") * edge**3
    kernel_grad = call(
        functools.partial(unpack_kernel, 1.0 / math.sqrt(cells)),
        [VMEM, VMEM],
        shape((9, 3 * channels, channels), F32),
        [pltpu.VMEM((2 * count, lanes), F32)],
        name="unpack",
    )(part, other).reshape(kernel.shape)
    return response, feature_grad, kernel_grad


def solution(mesh):
    bricks_spec = P(("groups", "dp"), "space", None, None, None)
    return jax.shard_map(
        functools.partial(body, mesh.shape["space"]),
        mesh=mesh,
        in_specs=(bricks_spec, bricks_spec, P(), P(("groups", "dp"), "space", None)),
        out_specs=(bricks_spec, bricks_spec, P("groups", None, None, None, None)),
        check_vma=False,
    )
```

```python
import functools
import math

import jax
import jax.numpy as jnp
from jax import lax
from jax.experimental import pallas as pl
from jax.experimental.pallas import tpu as pltpu
from jax.sharding import PartitionSpec as P

TILES_Y = 4
F32 = jnp.float32
BF16 = jnp.bfloat16


def step_y(tile, sign, tiles):
    column = (tile + TILES_Y // 2) % TILES_Y + sign
    near = tile + sign
    return near if 0 <= column < TILES_Y and 0 <= near < tiles else None


def step_x(tile, sign, tiles):
    near = tile + sign * TILES_Y
    return near if 0 <= near < tiles else None


def rounds(edges):
    found = []
    for low, high in edges:
        for one in found:
            if low not in one and high not in one:
                break
        else:
            one = {}
            found.append(one)
        one[low] = (high, 1)
        one[high] = (low, 0)
    return found


def detours(tiles):
    found = []
    for tile in range(tiles):
        for across in range(2):
            for along in range(2):
                sender = step_y(tile, 2 * along - 1, tiles)
                if sender is None or step_x(sender, 2 * across - 1, tiles) is None:
                    continue
                if step_x(tile, 2 * across - 1, tiles) is not None:
                    continue
                for one in found:
                    if all(hop[0] != sender and hop[1] != tile for hop in one):
                        break
                else:
                    one = []
                    found.append(one)
                one.append((sender, tile, across, along))
    return found


def make_plan(tiles):
    def edges(step):
        return [(tile, step(tile, 1, tiles)) for tile in range(tiles) if step(tile, 1, tiles) is not None]

    along_x, along_y, hops = rounds(edges(step_x)), rounds(edges(step_y)), detours(tiles)
    pairs = [[[(tile, one[tile][0]) for tile in sorted(one)] for one in kind] for kind in (along_x, along_y)]
    pairs.append([[hop[:2] for hop in one] for one in hops])
    roles = [[{tile: one[tile][1] for tile in one} for one in kind] for kind in (along_x, along_y)]
    roles.append([{hop[0]: (hop[2], 1 - hop[3]) for hop in one} for one in hops])
    roles.append([{hop[1]: hop[2:] for hop in one} for one in hops])
    return pairs, roles


class Roles:
    def __init__(self, roles, tiles):
        self.roles, self.tiles = roles, tiles
        self.counts = [len(kind) for kind in roles[:3]]
        self.tile = lax.axis_index("space")

    def any(self, kind, number, test):
        words = []
        for start in range(0, self.tiles, 32):
            here = [t for t in range(start, min(start + 32, self.tiles)) if t in self.roles[kind][number]]
            word = sum(1 << (t - start) for t in here if test(self.roles[kind][number][t]))
            words.append(word - (1 << 32) if word >> 31 else word)
        word = jnp.int32(words[0])
        for number, other in enumerate(words[1:], 1):
            word = jnp.where(self.tile // 32 == number, jnp.int32(other), word)
        return (lax.shift_right_logical(word, self.tile % 32) & 1) == 1

    def side(self, kind, number, side):
        return self.any(kind, number, lambda role: role == side)

    def linked(self, side):
        found = jnp.bool_(False)
        for number in range(self.counts[1]):
            found = found | self.side(1, number, side)
        return found


def masked(keep, x):
    return jnp.where(keep, x, jnp.zeros_like(x))


def faces_kernel(roles, tiles, f_hbm, c_hbm, link_hbm, *refs):
    roles = Roles(roles, tiles)
    counts = roles.counts
    x_refs = refs[: counts[0]]
    y_refs = refs[counts[0] : counts[0] + counts[1]]
    f_ref, c_ref, link_ref, arrived = refs[counts[0] + counts[1] :]
    copies = [
        pltpu.make_async_copy(f_hbm, f_ref, arrived.at[0]),
        pltpu.make_async_copy(c_hbm, c_ref, arrived.at[1]),
        pltpu.make_async_copy(link_hbm, link_ref, arrived.at[2]),
    ]
    for copy in copies:
        copy.start()
    for copy in copies:
        copy.wait()
    edge = f_ref.shape[1]
    linked = [[link_ref[brick, way] >= 0 for way in range(4)] for brick in range(2)]
    for number, out in enumerate(x_refs):
        up = roles.side(0, number, 1)
        plane = jnp.where(up, edge - 1, 0)
        for brick in range(2):
            keep = jnp.where(up, linked[brick][1], linked[brick][0])
            for source, ref in enumerate((f_ref, c_ref)):
                out[source, brick] = masked(keep, ref[brick, plane])
    rows = []
    for ref in (f_ref, c_ref):
        low = ref[0].astype(F32)[:, 0, :]
        high = ref[1].astype(F32)[:, edge - 1, :]
        rows.append((low, high))
    for number, out in enumerate(y_refs):
        up = roles.side(1, number, 1)
        keep = jnp.where(up, linked[1][3], linked[0][2])
        for source, (low, high) in enumerate(rows):
            out[source] = masked(keep, jnp.where(up, high, low)).astype(BF16)


def padded(x, channels):
    zeros = jnp.zeros(x.shape[:-1] + (2 * channels,), F32)
    return pltpu.roll(jnp.concatenate([x, zeros], axis=-1), channels, x.ndim - 1)


def weights_kernel(kernel_ref, forward_ref, backward_ref, wide):
    channels = kernel_ref.shape[-1]
    wide[...] = jnp.zeros_like(wide)
    wide[:, :, :channels] = kernel_ref[...].astype(F32)
    for tap in range(9):
        plain = [wide[3 * tap + d] for d in range(3)]
        moved = [pltpu.roll(x, channels, 1) for x in plain]
        steps = (plain[0], plain[1] + moved[0], plain[2] + moved[1], moved[2])
        for number, block in enumerate(steps):
            forward_ref[tap, channels * number : channels * (number + 1), :] = block.astype(BF16)
        last = 8 - tap
        lanes = 2 * channels
        backward_ref[last, :channels, :lanes] = (plain[2] + moved[1]).astype(BF16)
        backward_ref[last, :channels, lanes:] = plain[0].astype(BF16)
        backward_ref[last, channels:, :lanes] = moved[2].astype(BF16)
        backward_ref[last, channels:, lanes:] = (plain[1] + moved[0]).astype(BF16)


def store_line(lines, number, line):
    lanes = lines.shape[1]
    each = line.shape[1] // lanes
    for k in range(each):
        lines[each * number + k : each * number + k + 1, :] = line[:, lanes * k : lanes * (k + 1)]


def load_line(rows, number, each):
    return jnp.concatenate([rows[each * number + k : each * number + k + 1] for k in range(each)], axis=1)


def kernel_grad_kernel(roles, tiles, channels, f_ref, c_ref, *refs):
    roles = Roles(roles, tiles)
    counts = roles.counts
    x_refs = refs[: counts[0]]
    y_refs = refs[counts[0] : counts[0] + counts[1]]
    near = counts[0] + counts[1]
    keep_ref, send_ref = refs[near : near + 2]
    line_refs = refs[near + 2 : near + 2 + counts[0]]
    hop_refs = refs[near + 2 + counts[0] : near + 2 + counts[0] + counts[2]]
    wide, tall, packed, lines = refs[near + 2 + counts[0] + counts[2] :]
    bricks, edge, _, width = f_ref.shape
    rows = edge * edge
    wide[:, edge : edge + rows, :] = padded(f_ref[...].astype(F32).reshape(bricks, rows, width), channels)
    planes = []
    for side in range(2):
        start = side * (edge + rows)
        plane = jnp.zeros((bricks, edge, width), F32)
        for number, ref in enumerate(x_refs):
            plane = jnp.where(roles.side(0, number, side), ref[0].astype(F32), plane)
        planes.append(plane)
        plane = padded(plane, channels)
        for brick in range(bricks):
            wide[brick, start : start + edge, :] = plane[brick]
    own = c_ref[...].astype(F32)
    tall[:, :, edge : 2 * edge, :] = own
    tall[1, :, edge - 1 : edge, :] = own[0, :, edge - 1 :, :]
    tall[0, :, 2 * edge : 2 * edge + 1, :] = own[1, :, 0:1, :]
    halo = {}
    for side in range(2):
        for source in range(2):
            row = jnp.zeros((edge, width), F32)
            for number, ref in enumerate(y_refs):
                row = jnp.where(roles.side(1, number, side), ref[source].astype(F32), row)
            halo[source, side] = row
        at = 2 * edge if side else edge - 1
        tall[side, :, at : at + 1, :] = halo[1, side][:, None, :]
    lanes = 2 * channels
    pairs = width // lanes
    right = []
    for col in range(3):
        value = tall[:, :, edge + 1 - col : 2 * edge + 1 - col, :].reshape(bricks * rows, width).astype(BF16)
        right.append(jnp.concatenate([value[:, lanes * k : lanes * (k + 1)] for k in range(pairs)], axis=0))
    right = jnp.concatenate(right, axis=1)
    low = lax.broadcasted_iota(jnp.int32, (3 * channels // 2, lanes), 1) < channels
    half = 3 * channels // 2
    for row in range(3):
        value = wide[:, edge * row : edge * row + rows, :].reshape(bricks * rows, -1).astype(BF16)
        left = jnp.concatenate([value[:, lanes * k : lanes * (k + 2)] for k in range(pairs)], axis=0)
        grad = lax.dot_general(left, right, (((0,), (0,)), ((), ())), preferred_element_type=F32)
        for col in range(3):
            block = grad[:, lanes * col : lanes * (col + 1)]
            moved = pltpu.roll(block, channels, 1)
            first = block[:half] + moved[channels : channels + half]
            second = moved[half : 2 * half] + block[channels + half :]
            at = half * (3 * row + col)
            packed[at : at + half, :] = jnp.where(low, first, second)
    for number, out in enumerate(line_refs):
        up = roles.side(0, number, 1)
        for (source, side), row in halo.items():
            store_line(lines, 2 * source + side, jnp.where(up, row[edge - 1 : edge], row[0:1]))
        out[...] = lines[...].astype(BF16)
    for number, out in enumerate(hop_refs):
        line = jnp.zeros((1, width), F32)
        for across in range(2):
            for side in range(2):
                at = (edge - 1) * side
                hit = roles.any(2, number, lambda role: role == (across, side))
                line = jnp.where(hit, planes[across][side, at : at + 1, :], line)
        store_line(lines, 0, line)
        out[...] = lines[...].astype(BF16)
    count = keep_ref.shape[0]
    core = lax.axis_index("dp")
    keep_ref[...] = packed[pl.ds(pl.multiple_of(core * count, 8), count), :]
    send_ref[...] = packed[pl.ds(pl.multiple_of((1 - core) * count, 8), count), :]


def conv_kernel(roles, tiles, channels, source, v_ref, *refs):
    roles = Roles(roles, tiles)
    counts = roles.counts
    x_refs = refs[: counts[0]]
    y_refs = refs[counts[0] : counts[0] + counts[1]]
    near = counts[0] + counts[1]
    line_refs = refs[near : near + counts[0]]
    hop_refs = refs[near + counts[0] : near + counts[0] + counts[2]]
    weight_ref, out_ref, ext = refs[near + counts[0] + counts[2] :]
    bricks, edge, _, width = v_ref.shape
    rows = edge * edge
    first, last = edge, 2 * edge - 1
    ext[:, 1 : edge + 1, first : last + 1, :] = padded(v_ref[...].astype(F32), channels)
    for side in range(2):
        plane = jnp.zeros((bricks, edge, width), F32)
        for number, ref in enumerate(x_refs):
            plane = jnp.where(roles.side(0, number, side), ref[source].astype(F32), plane)
        plane = padded(plane, channels)
        for brick in range(bricks):
            ext[brick, side * (edge + 1), first : last + 1, :] = plane[brick]
    each = width // line_refs[0].shape[1]
    arrived = [ref[ref.shape[0] - 4 * each :, :].astype(F32) for ref in line_refs]
    hops = [load_line(ref[...].astype(F32), 0, each) for ref in hop_refs]
    for side in range(2):
        row = jnp.zeros((edge, width), F32)
        for number, ref in enumerate(y_refs):
            row = jnp.where(roles.side(1, number, side), ref[source].astype(F32), row)
        at = last + 1 if side else first - 1
        row = padded(row, channels)
        ext[side, 1 : edge + 1, at : at + 1, :] = row[:, None, :]
        for across in range(2):
            line = jnp.zeros((1, width), F32)
            for number, value in enumerate(arrived):
                line = jnp.where(roles.side(0, number, across), load_line(value, 2 * source + side, each), line)
            if source == 0:
                line = masked(roles.linked(side), line)
                for number, value in enumerate(hops):
                    line = jnp.where(roles.any(3, number, lambda role: role == (across, side)), value, line)
            ext[side, across * (edge + 1), at : at + 1, :] = padded(line, channels)
    ext[1, :, first - 1 : first, :] = ext[0, :, last : last + 1, :]
    ext[0, :, last + 1 : last + 2, :] = ext[1, :, first : first + 1, :]
    lanes = 2 * channels
    pairs = width // lanes
    total = jnp.zeros((pairs * bricks * rows, lanes), F32)
    contract = 0 if source == 0 else 1
    for col in range(3):
        for row in range(3):
            value = ext[:, row : row + edge, first - 1 + col : last + col, :]
            value = value.reshape(bricks * rows, -1).astype(BF16)
            left = jnp.concatenate([value[:, lanes * k : lanes * (k + 2)] for k in range(pairs)], axis=0)
            total = total + lax.dot_general(
                left, weight_ref[3 * row + col], (((1,), (contract,)), ((), ())), preferred_element_type=F32
            )
    for k in range(pairs):
        out_ref[:, lanes * k : lanes * (k + 1)] = total[bricks * rows * k : bricks * rows * (k + 1)].astype(BF16)


def unpack_kernel(factor, own_ref, other_ref, out_ref, packed):
    count = own_ref.shape[0]
    core = lax.axis_index("dp")
    packed[pl.ds(pl.multiple_of(core * count, 8), count), :] = own_ref[...] * factor
    packed[pl.ds(pl.multiple_of((1 - core) * count, 8), count), :] = other_ref[...] * factor
    taps, rows, channels = out_ref.shape
    half = rows // 2
    for tap in range(taps):
        block = packed[half * tap : half * (tap + 1), :]
        out_ref[tap, :half, :] = block[:, :channels]
        out_ref[tap, half:, :] = pltpu.roll(block, channels, 1)[:, :channels]


VMEM = pl.BlockSpec(memory_space=pltpu.VMEM)
HBM = pl.BlockSpec(memory_space=pltpu.HBM)


def call(kernel, in_specs, out_shapes, scratch=(), flops=0, name=None, vmem=24 * 2**20):
    several = isinstance(out_shapes, list)
    return pl.pallas_call(
        kernel,
        in_specs=in_specs,
        out_specs=[VMEM] * len(out_shapes) if several else VMEM,
        out_shape=out_shapes,
        scratch_shapes=list(scratch),
        compiler_params=pltpu.CompilerParams(vmem_limit_bytes=vmem),
        cost_estimate=pl.CostEstimate(flops=flops, bytes_accessed=2**20, transcendentals=0),
        name=name,
    )


def body(tiles, features, cotangent, kernel, neighbours):
    pairs, roles = make_plan(tiles)
    counts = [len(kind) for kind in pairs]
    bricks, edge = features.shape[1:3]
    width = features.shape[-1]
    channels = kernel.shape[-1]
    rows = edge * edge
    lanes = 2 * channels
    shape = jax.ShapeDtypeStruct
    f = features.reshape(bricks, edge, edge, width)
    c = cotangent.reshape(bricks, edge, edge, width)
    links = neighbours.reshape(bricks, 6)

    near = counts[0] + counts[1]
    face_shapes = [(2, bricks, edge, width)] * counts[0] + [(2, edge, width)] * counts[1]
    faces = call(
        functools.partial(faces_kernel, roles, tiles),
        [HBM, HBM, HBM],
        [shape(s, BF16) for s in face_shapes],
        [
            pltpu.VMEM(f.shape, BF16),
            pltpu.VMEM(c.shape, BF16),
            pltpu.SMEM(links.shape, jnp.int32),
            pltpu.SemaphoreType.DMA((3,)),
        ],
        name="faces",
        vmem=None,
    )(f, c, links)
    got = [lax.ppermute(x, "space", one) for x, one in zip(faces, pairs[0] + pairs[1])]
    count = 27 * channels * channels // lanes // 2
    line_rows = 4 * width // lanes
    keep, send, *lines = call(
        functools.partial(kernel_grad_kernel, roles, tiles, channels),
        [VMEM, VMEM] + [VMEM] * near,
        [shape((count, lanes), F32)] * 2 + [shape((line_rows, lanes), BF16)] * (counts[0] + counts[2]),
        [
            pltpu.VMEM((bricks, rows + 2 * edge, width + lanes), F32),
            pltpu.VMEM((bricks, edge, 3 * edge, width), F32),
            pltpu.VMEM((2 * count, lanes), F32),
            pltpu.VMEM((line_rows, lanes), F32),
        ],
        flops=2 * 768 * 384 * 512,
        name="kernel_grad",
    )(f, c, *got)

    forward, backward = call(
        weights_kernel,
        [VMEM],
        [shape((9, 4 * channels, lanes), BF16), shape((9, lanes, 4 * channels), BF16)],
        [pltpu.VMEM((27, channels, lanes), F32)],
        name="weights",
    )(kernel.reshape(27, channels, channels))

    def conv(source, x, weight):
        return call(
            functools.partial(conv_kernel, roles, tiles, channels, source),
            [VMEM] * (2 + len(got)),
            shape((bricks * rows, width), BF16),
            [pltpu.VMEM((bricks, edge + 2, 3 * edge, width + lanes), F32)],
            flops=2 * 512 * 256 * 128 * 9,
            name="response" if source == 0 else "feature_grad",
        )(x, *got, weight)

    swap = [(0, 1), (1, 0)]
    part = keep + lax.ppermute(send, "dp", swap)
    steps = [[(i, i ^ (1 << bit)) for i in range(tiles)] for bit in range(tiles.bit_length() - 1)]
    wire = BF16 if len(steps) <= 3 else F32
    joined = len(pairs[0]) == 1 and pairs[0][0] in steps and wire == BF16
    if joined:
        steps.sort(key=lambda step: step != pairs[0][0])
    hops = [lax.ppermute(x, "space", one) for x, one in zip(lines[counts[0] :], pairs[2])]
    lines = lines[: counts[0]]
    if not joined:
        got += [lax.ppermute(x, "space", one) for x, one in zip(lines, pairs[0])]
    for number, step in enumerate(steps):
        mine = part.astype(wire)
        if number == 0 and joined:
            mine = lax.optimization_barrier(jnp.concatenate([mine, lines[0]], axis=0))
        if number == 1:
            mine, hops, forward, backward = lax.optimization_barrier((mine, hops, forward, backward))
            got += hops
            response = conv(0, f, forward)
            feature_grad = conv(1, c, backward)
        elif number == 2:
            mine, response = lax.optimization_barrier((mine, response))
        else:
            mine = lax.optimization_barrier(mine)
        theirs = lax.ppermute(mine, "space", step)
        if number == 0 and joined:
            got.append(theirs)
            mine, theirs = mine[:count], theirs[:count]
        part = mine.astype(F32) + theirs.astype(F32)
    part, feature_grad = lax.optimization_barrier((part, feature_grad))
    response, feature_grad = (x.reshape(features.shape) for x in (response, feature_grad))
    other = lax.ppermute(part, "dp", swap)
    cells = bricks * tiles * lax.axis_size("dp") * edge**3
    kernel_grad = call(
        functools.partial(unpack_kernel, 1.0 / math.sqrt(cells)),
        [VMEM, VMEM],
        shape((9, 3 * channels, channels), F32),
        [pltpu.VMEM((2 * count, lanes), F32)],
        name="unpack",
    )(part, other).reshape(kernel.shape)
    return response, feature_grad, kernel_grad


def solution(mesh):
    bricks_spec = P(("groups", "dp"), "space", None, None, None)
    return jax.shard_map(
        functools.partial(body, mesh.shape["space"]),
        mesh=mesh,
        in_specs=(bricks_spec, bricks_spec, P(), P(("groups", "dp"), "space", None)),
        out_specs=(bricks_spec, bricks_spec, P("groups", None, None, None, None)),
        check_vma=False,
    )
```

```python
import functools
import math

import jax
import jax.numpy as jnp
from jax import lax
from jax.experimental import pallas as pl
from jax.experimental.pallas import tpu as pltpu
from jax.sharding import PartitionSpec as P

TILES_Y = 4
F32 = jnp.float32
BF16 = jnp.bfloat16


def step_y(tile, sign, tiles):
    column = (tile + TILES_Y // 2) % TILES_Y + sign
    near = tile + sign
    return near if 0 <= column < TILES_Y and 0 <= near < tiles else None


def step_x(tile, sign, tiles):
    near = tile + sign * TILES_Y
    return near if 0 <= near < tiles else None


def rounds(edges):
    found = []
    for low, high in edges:
        for one in found:
            if low not in one and high not in one:
                break
        else:
            one = {}
            found.append(one)
        one[low] = (high, 1)
        one[high] = (low, 0)
    return found


def detours(tiles):
    found = []
    for tile in range(tiles):
        for across in range(2):
            for along in range(2):
                sender = step_y(tile, 2 * along - 1, tiles)
                if sender is None or step_x(sender, 2 * across - 1, tiles) is None:
                    continue
                if step_x(tile, 2 * across - 1, tiles) is not None:
                    continue
                for one in found:
                    if all(hop[0] != sender and hop[1] != tile for hop in one):
                        break
                else:
                    one = []
                    found.append(one)
                one.append((sender, tile, across, along))
    return found


def completed(pairs, tiles):
    idle = [tile for tile in range(tiles) if all(tile != a for a, _ in pairs) and all(tile != b for _, b in pairs)]
    near = [tile for tile in idle if tile ^ 1 in idle]
    rest = [tile for tile in idle if tile ^ 1 not in idle]
    pairs = pairs + [(tile, tile ^ 1) for tile in near]
    for low, high in zip(rest[::2], rest[1::2]):
        pairs = pairs + [(low, high), (high, low)]
    return sorted(pairs)


def make_plan(tiles):
    def edges(step):
        return [(tile, step(tile, 1, tiles)) for tile in range(tiles) if step(tile, 1, tiles) is not None]

    along_x, along_y, hops = rounds(edges(step_x)), rounds(edges(step_y)), detours(tiles)
    pairs = [[[(tile, one[tile][0]) for tile in sorted(one)] for one in kind] for kind in (along_x, along_y)]
    pairs.append([[hop[:2] for hop in one] for one in hops])
    pairs = [[completed(one, tiles) for one in kind] for kind in pairs]
    roles = [[{tile: one[tile][1] for tile in one} for one in kind] for kind in (along_x, along_y)]
    roles.append([{hop[0]: (hop[2], 1 - hop[3]) for hop in one} for one in hops])
    roles.append([{hop[1]: hop[2:] for hop in one} for one in hops])
    return pairs, roles


class Roles:
    def __init__(self, roles, tiles):
        self.roles, self.tiles = roles, tiles
        self.counts = [len(kind) for kind in roles[:3]]
        self.tile = lax.axis_index("space")

    def any(self, kind, number, test):
        words = []
        for start in range(0, self.tiles, 32):
            here = [t for t in range(start, min(start + 32, self.tiles)) if t in self.roles[kind][number]]
            word = sum(1 << (t - start) for t in here if test(self.roles[kind][number][t]))
            words.append(word - (1 << 32) if word >> 31 else word)
        word = jnp.int32(words[0])
        for number, other in enumerate(words[1:], 1):
            word = jnp.where(self.tile // 32 == number, jnp.int32(other), word)
        return (lax.shift_right_logical(word, self.tile % 32) & 1) == 1

    def side(self, kind, number, side):
        return self.any(kind, number, lambda role: role == side)

    def linked(self, side):
        found = jnp.bool_(False)
        for number in range(self.counts[1]):
            found = found | self.side(1, number, side)
        return found


def masked(keep, x):
    return jnp.where(keep, x, jnp.zeros_like(x))


def faces_kernel(roles, tiles, f_hbm, c_hbm, link_hbm, *refs):
    roles = Roles(roles, tiles)
    counts = roles.counts
    x_refs = refs[: counts[0]]
    y_refs = refs[counts[0] : counts[0] + counts[1]]
    f_ref, c_ref, link_ref, arrived = refs[counts[0] + counts[1] :]
    copies = [
        pltpu.make_async_copy(f_hbm, f_ref, arrived.at[0]),
        pltpu.make_async_copy(c_hbm, c_ref, arrived.at[1]),
        pltpu.make_async_copy(link_hbm, link_ref, arrived.at[2]),
    ]
    for copy in copies:
        copy.start()
    for copy in copies:
        copy.wait()
    edge = f_ref.shape[1]
    linked = [[link_ref[brick, way] >= 0 for way in range(4)] for brick in range(2)]
    for number, out in enumerate(x_refs):
        up = roles.side(0, number, 1)
        plane = jnp.where(up, edge - 1, 0)
        for brick in range(2):
            keep = jnp.where(up, linked[brick][1], linked[brick][0])
            for source, ref in enumerate((f_ref, c_ref)):
                out[source, brick] = masked(keep, ref[brick, plane])
    rows = []
    for ref in (f_ref, c_ref):
        low = ref[0].astype(F32)[:, 0, :]
        high = ref[1].astype(F32)[:, edge - 1, :]
        rows.append((low, high))
    for number, out in enumerate(y_refs):
        up = roles.side(1, number, 1)
        keep = jnp.where(up, linked[1][3], linked[0][2])
        for source, (low, high) in enumerate(rows):
            out[source] = masked(keep, jnp.where(up, high, low)).astype(BF16)


def padded(x, channels):
    zeros = jnp.zeros(x.shape[:-1] + (2 * channels,), F32)
    return pltpu.roll(jnp.concatenate([x, zeros], axis=-1), channels, x.ndim - 1)


def weights_kernel(kernel_ref, forward_ref, backward_ref, wide):
    channels = kernel_ref.shape[-1]
    wide[...] = jnp.zeros_like(wide)
    wide[:, :, :channels] = kernel_ref[...].astype(F32)
    for tap in range(9):
        plain = [wide[3 * tap + d] for d in range(3)]
        moved = [pltpu.roll(x, channels, 1) for x in plain]
        steps = (plain[0], plain[1] + moved[0], plain[2] + moved[1], moved[2])
        for number, block in enumerate(steps):
            forward_ref[tap, channels * number : channels * (number + 1), :] = block.astype(BF16)
        last = 8 - tap
        lanes = 2 * channels
        backward_ref[last, :channels, :lanes] = (plain[2] + moved[1]).astype(BF16)
        backward_ref[last, :channels, lanes:] = plain[0].astype(BF16)
        backward_ref[last, channels:, :lanes] = moved[2].astype(BF16)
        backward_ref[last, channels:, lanes:] = (plain[1] + moved[0]).astype(BF16)


def store_line(lines, number, line):
    lanes = lines.shape[1]
    each = line.shape[1] // lanes
    for k in range(each):
        lines[each * number + k : each * number + k + 1, :] = line[:, lanes * k : lanes * (k + 1)]


def load_line(rows, number, each):
    return jnp.concatenate([rows[each * number + k : each * number + k + 1] for k in range(each)], axis=1)


def kernel_grad_kernel(roles, tiles, channels, f_ref, c_ref, *refs):
    roles = Roles(roles, tiles)
    counts = roles.counts
    x_refs = refs[: counts[0]]
    y_refs = refs[counts[0] : counts[0] + counts[1]]
    near = counts[0] + counts[1]
    keep_ref, send_ref = refs[near : near + 2]
    line_refs = refs[near + 2 : near + 2 + counts[0]]
    hop_refs = refs[near + 2 + counts[0] : near + 2 + counts[0] + counts[2]]
    wide, tall, packed, lines = refs[near + 2 + counts[0] + counts[2] :]
    bricks, edge, _, width = f_ref.shape
    rows = edge * edge
    wide[:, edge : edge + rows, :] = padded(f_ref[...].astype(F32).reshape(bricks, rows, width), channels)
    planes = []
    for side in range(2):
        start = side * (edge + rows)
        plane = jnp.zeros((bricks, edge, width), F32)
        for number, ref in enumerate(x_refs):
            plane = jnp.where(roles.side(0, number, side), ref[0].astype(F32), plane)
        planes.append(plane)
        plane = padded(plane, channels)
        for brick in range(bricks):
            wide[brick, start : start + edge, :] = plane[brick]
    own = c_ref[...].astype(F32)
    tall[:, :, edge : 2 * edge, :] = own
    tall[1, :, edge - 1 : edge, :] = own[0, :, edge - 1 :, :]
    tall[0, :, 2 * edge : 2 * edge + 1, :] = own[1, :, 0:1, :]
    halo = {}
    for side in range(2):
        for source in range(2):
            row = jnp.zeros((edge, width), F32)
            for number, ref in enumerate(y_refs):
                row = jnp.where(roles.side(1, number, side), ref[source].astype(F32), row)
            halo[source, side] = row
        at = 2 * edge if side else edge - 1
        tall[side, :, at : at + 1, :] = halo[1, side][:, None, :]
    lanes = 2 * channels
    pairs = width // lanes
    right = []
    for col in range(3):
        value = tall[:, :, edge + 1 - col : 2 * edge + 1 - col, :].reshape(bricks * rows, width).astype(BF16)
        right.append(jnp.concatenate([value[:, lanes * k : lanes * (k + 1)] for k in range(pairs)], axis=0))
    right = jnp.concatenate(right, axis=1)
    low = lax.broadcasted_iota(jnp.int32, (3 * channels // 2, lanes), 1) < channels
    half = 3 * channels // 2
    for row in range(3):
        value = wide[:, edge * row : edge * row + rows, :].reshape(bricks * rows, -1).astype(BF16)
        left = jnp.concatenate([value[:, lanes * k : lanes * (k + 2)] for k in range(pairs)], axis=0)
        grad = lax.dot_general(left, right, (((0,), (0,)), ((), ())), preferred_element_type=F32)
        for col in range(3):
            block = grad[:, lanes * col : lanes * (col + 1)]
            moved = pltpu.roll(block, channels, 1)
            first = block[:half] + moved[channels : channels + half]
            second = moved[half : 2 * half] + block[channels + half :]
            at = half * (3 * row + col)
            packed[at : at + half, :] = jnp.where(low, first, second)
    for number, out in enumerate(line_refs):
        up = roles.side(0, number, 1)
        for (source, side), row in halo.items():
            store_line(lines, 2 * source + side, jnp.where(up, row[edge - 1 : edge], row[0:1]))
        out[...] = lines[...].astype(BF16)
    for number, out in enumerate(hop_refs):
        line = jnp.zeros((1, width), F32)
        for across in range(2):
            for side in range(2):
                at = (edge - 1) * side
                hit = roles.any(2, number, lambda role: role == (across, side))
                line = jnp.where(hit, planes[across][side, at : at + 1, :], line)
        store_line(lines, 0, line)
        out[...] = lines[...].astype(BF16)
    count = keep_ref.shape[0]
    core = lax.axis_index("dp")
    keep_ref[...] = packed[pl.ds(pl.multiple_of(core * count, 8), count), :]
    send_ref[...] = packed[pl.ds(pl.multiple_of((1 - core) * count, 8), count), :]


def conv_kernel(roles, tiles, channels, source, ways, v_ref, *refs):
    roles = Roles(roles, tiles)
    counts = roles.counts
    x_refs = refs[: counts[0]]
    y_refs = refs[counts[0] : counts[0] + counts[1]]
    near = counts[0] + counts[1]
    hops_at = near + counts[0] * ways
    line_refs = refs[near:hops_at]
    hop_refs = refs[hops_at : hops_at + counts[2]]
    weight_ref, out_ref, ext = refs[hops_at + counts[2] :]
    bricks, edge, _, width = v_ref.shape
    rows = edge * edge
    first, last = edge, 2 * edge - 1
    ext[:, 1 : edge + 1, first : last + 1, :] = padded(v_ref[...].astype(F32), channels)
    for side in range(2):
        plane = jnp.zeros((bricks, edge, width), F32)
        for number, ref in enumerate(x_refs):
            plane = jnp.where(roles.side(0, number, side), ref[source].astype(F32), plane)
        plane = padded(plane, channels)
        for brick in range(bricks):
            ext[brick, side * (edge + 1), first : last + 1, :] = plane[brick]
    each = width // line_refs[0].shape[1]
    arrived = [ref[ref.shape[0] - 4 * each :, :].astype(F32) for ref in line_refs]
    if ways == 2:
        first_core = lax.axis_index("dp") == 0
        arrived = [jnp.where(first_core, *arrived)]
    hops = [load_line(ref[...].astype(F32), 0, each) for ref in hop_refs]
    for side in range(2):
        row = jnp.zeros((edge, width), F32)
        for number, ref in enumerate(y_refs):
            row = jnp.where(roles.side(1, number, side), ref[source].astype(F32), row)
        at = last + 1 if side else first - 1
        row = padded(row, channels)
        ext[side, 1 : edge + 1, at : at + 1, :] = row[:, None, :]
        for across in range(2):
            line = jnp.zeros((1, width), F32)
            for number, value in enumerate(arrived):
                line = jnp.where(roles.side(0, number, across), load_line(value, 2 * source + side, each), line)
            if source == 0:
                line = masked(roles.linked(side), line)
                for number, value in enumerate(hops):
                    line = jnp.where(roles.any(3, number, lambda role: role == (across, side)), value, line)
            ext[side, across * (edge + 1), at : at + 1, :] = padded(line, channels)
    ext[1, :, first - 1 : first, :] = ext[0, :, last : last + 1, :]
    ext[0, :, last + 1 : last + 2, :] = ext[1, :, first : first + 1, :]
    lanes = 2 * channels
    pairs = width // lanes
    total = jnp.zeros((pairs * bricks * rows, lanes), F32)
    contract = 0 if source == 0 else 1
    for col in range(3):
        for row in range(3):
            value = ext[:, row : row + edge, first - 1 + col : last + col, :]
            value = value.reshape(bricks * rows, -1).astype(BF16)
            left = jnp.concatenate([value[:, lanes * k : lanes * (k + 2)] for k in range(pairs)], axis=0)
            total = total + lax.dot_general(
                left, weight_ref[3 * row + col], (((1,), (contract,)), ((), ())), preferred_element_type=F32
            )
    for k in range(pairs):
        out_ref[:, lanes * k : lanes * (k + 1)] = total[bricks * rows * k : bricks * rows * (k + 1)].astype(BF16)


def unpack_kernel(factor, own_ref, other_ref, out_ref, packed):
    count = own_ref.shape[0]
    core = lax.axis_index("dp")
    packed[pl.ds(pl.multiple_of(core * count, 8), count), :] = own_ref[...] * factor
    packed[pl.ds(pl.multiple_of((1 - core) * count, 8), count), :] = other_ref[...] * factor
    taps, rows, channels = out_ref.shape
    half = rows // 2
    for tap in range(taps):
        block = packed[half * tap : half * (tap + 1), :]
        out_ref[tap, :half, :] = block[:, :channels]
        out_ref[tap, half:, :] = pltpu.roll(block, channels, 1)[:, :channels]


VMEM = pl.BlockSpec(memory_space=pltpu.VMEM)
HBM = pl.BlockSpec(memory_space=pltpu.HBM)


def call(kernel, in_specs, out_shapes, scratch=(), flops=0, name=None, vmem=24 * 2**20):
    several = isinstance(out_shapes, list)
    return pl.pallas_call(
        kernel,
        in_specs=in_specs,
        out_specs=[VMEM] * len(out_shapes) if several else VMEM,
        out_shape=out_shapes,
        scratch_shapes=list(scratch),
        compiler_params=pltpu.CompilerParams(vmem_limit_bytes=vmem),
        cost_estimate=pl.CostEstimate(flops=flops, bytes_accessed=2**20, transcendentals=0),
        name=name,
    )


def body(tiles, features, cotangent, kernel, neighbours):
    pairs, roles = make_plan(tiles)
    counts = [len(kind) for kind in pairs]
    bricks, edge = features.shape[1:3]
    width = features.shape[-1]
    channels = kernel.shape[-1]
    rows = edge * edge
    lanes = 2 * channels
    shape = jax.ShapeDtypeStruct
    f = features.reshape(bricks, edge, edge, width)
    c = cotangent.reshape(bricks, edge, edge, width)
    links = neighbours.reshape(bricks, 6)

    near = counts[0] + counts[1]
    face_shapes = [(2, bricks, edge, width)] * counts[0] + [(2, edge, width)] * counts[1]
    faces = call(
        functools.partial(faces_kernel, roles, tiles),
        [HBM, HBM, HBM],
        [shape(s, BF16) for s in face_shapes],
        [
            pltpu.VMEM(f.shape, BF16),
            pltpu.VMEM(c.shape, BF16),
            pltpu.SMEM(links.shape, jnp.int32),
            pltpu.SemaphoreType.DMA((3,)),
        ],
        name="faces",
        vmem=None,
    )(f, c, links)
    got = [lax.ppermute(x, "space", one) for x, one in zip(faces, pairs[0] + pairs[1])]
    count = 27 * channels * channels // lanes // 2
    line_rows = 4 * width // lanes
    keep, send, *lines = call(
        functools.partial(kernel_grad_kernel, roles, tiles, channels),
        [VMEM, VMEM] + [VMEM] * near,
        [shape((count, lanes), F32)] * 2 + [shape((line_rows, lanes), BF16)] * (counts[0] + counts[2]),
        [
            pltpu.VMEM((bricks, rows + 2 * edge, width + lanes), F32),
            pltpu.VMEM((bricks, edge, 3 * edge, width), F32),
            pltpu.VMEM((2 * count, lanes), F32),
            pltpu.VMEM((line_rows, lanes), F32),
        ],
        flops=2 * 768 * 384 * 512,
        name="kernel_grad",
    )(f, c, *got)

    forward, backward = call(
        weights_kernel,
        [VMEM],
        [shape((9, 4 * channels, lanes), BF16), shape((9, lanes, 4 * channels), BF16)],
        [pltpu.VMEM((27, channels, lanes), F32)],
        name="weights",
    )(kernel.reshape(27, channels, channels))

    def conv(source, x, weight):
        return call(
            functools.partial(conv_kernel, roles, tiles, channels, source, ready),
            [VMEM] * (2 + len(got)),
            shape((bricks * rows, width), BF16),
            [pltpu.VMEM((bricks, edge + 2, 3 * edge, width + lanes), F32)],
            flops=2 * 512 * 256 * 128 * 9,
            name="response" if source == 0 else "feature_grad",
        )(x, *got, weight)

    cores = lax.axis_size("dp")
    swap = [(0, 1), (1, 0)]
    part = keep + lax.ppermute(send, "dp", swap)
    bits = [1 << number for number in range(tiles.bit_length() - 1)]
    orders = [bits, bits]
    wire = BF16 if len(bits) <= 3 else F32
    shared = [bit for bit in bits if pairs[0] == [[(i, i ^ bit) for i in range(tiles)]]]
    joined = bool(shared) and len(bits) == 3
    if joined:
        first, last = (bit for bit in bits if bit not in shared)
        orders = [shared + [first, last], [last] + shared + [first]]
    hops = [lax.ppermute(x, "space", one) for x, one in zip(lines[counts[0] :], pairs[2])]
    lines = lines[: counts[0]]
    if not joined:
        got += [lax.ppermute(x, "space", one) for x, one in zip(lines, pairs[0])]
    ready = 2 if joined else 1
    for number in range(len(bits)):
        step = [
            (tile * cores + core, (tile ^ order[number]) * cores + core)
            for tile in range(tiles)
            for core, order in enumerate(orders)
        ]
        mine = part.astype(wire)
        carries = joined and number < ready
        if carries:
            mine = jnp.concatenate([mine, lines[0]], axis=0)
        if number == 1:
            mine, hops, forward, backward = lax.optimization_barrier((mine, hops, forward, backward))
        else:
            mine = lax.optimization_barrier(mine)
        if number == ready:
            got += hops
            response = conv(0, f, forward)
            feature_grad = conv(1, c, backward)
        theirs = lax.ppermute(mine, ("space", "dp"), step)
        if carries:
            got.append(theirs)
            mine, theirs = mine[:count], theirs[:count]
        part = mine.astype(F32) + theirs.astype(F32)
    part, response = lax.optimization_barrier((part, response))
    other = lax.ppermute(part, "dp", swap)
    other, feature_grad = lax.optimization_barrier((other, feature_grad))
    response, feature_grad = (x.reshape(features.shape) for x in (response, feature_grad))
    cells = bricks * tiles * lax.axis_size("dp") * edge**3
    kernel_grad = call(
        functools.partial(unpack_kernel, 1.0 / math.sqrt(cells)),
        [VMEM, VMEM],
        shape((9, 3 * channels, channels), F32),
        [pltpu.VMEM((2 * count, lanes), F32)],
        name="unpack",
    )(part, other).reshape(kernel.shape)
    return response, feature_grad, kernel_grad


def solution(mesh):
    bricks_spec = P(("groups", "dp"), "space", None, None, None)
    return jax.shard_map(
        functools.partial(body, mesh.shape["space"]),
        mesh=mesh,
        in_specs=(bricks_spec, bricks_spec, P(), P(("groups", "dp"), "space", None)),
        out_specs=(bricks_spec, bricks_spec, P("groups", None, None, None, None)),
        check_vma=False,
    )
```

```python
import functools
import math

import jax
import jax.numpy as jnp
from jax import lax
from jax.experimental import pallas as pl
from jax.experimental.pallas import tpu as pltpu
from jax.sharding import PartitionSpec as P

TILES_Y = 4
F32 = jnp.float32
BF16 = jnp.bfloat16


def step_y(tile, sign, tiles):
    column = (tile + TILES_Y // 2) % TILES_Y + sign
    near = tile + sign
    return near if 0 <= column < TILES_Y and 0 <= near < tiles else None


def step_x(tile, sign, tiles):
    near = tile + sign * TILES_Y
    return near if 0 <= near < tiles else None


def rounds(edges):
    found = []
    for low, high in edges:
        for one in found:
            if low not in one and high not in one:
                break
        else:
            one = {}
            found.append(one)
        one[low] = (high, 1)
        one[high] = (low, 0)
    return found


def detours(tiles):
    found = []
    for tile in range(tiles):
        for across in range(2):
            for along in range(2):
                sender = step_y(tile, 2 * along - 1, tiles)
                if sender is None or step_x(sender, 2 * across - 1, tiles) is None:
                    continue
                if step_x(tile, 2 * across - 1, tiles) is not None:
                    continue
                for one in found:
                    if all(hop[0] != sender and hop[1] != tile for hop in one):
                        break
                else:
                    one = []
                    found.append(one)
                one.append((sender, tile, across, along))
    return found


def completed(pairs, tiles):
    idle = [tile for tile in range(tiles) if all(tile != a for a, _ in pairs) and all(tile != b for _, b in pairs)]
    near = [tile for tile in idle if tile ^ 1 in idle]
    rest = [tile for tile in idle if tile ^ 1 not in idle]
    pairs = pairs + [(tile, tile ^ 1) for tile in near]
    for low, high in zip(rest[::2], rest[1::2]):
        pairs = pairs + [(low, high), (high, low)]
    return sorted(pairs)


def make_plan(tiles):
    def edges(step):
        return [(tile, step(tile, 1, tiles)) for tile in range(tiles) if step(tile, 1, tiles) is not None]

    along_x, along_y, hops = rounds(edges(step_x)), rounds(edges(step_y)), detours(tiles)
    pairs = [[[(tile, one[tile][0]) for tile in sorted(one)] for one in kind] for kind in (along_x, along_y)]
    pairs.append([[hop[:2] for hop in one] for one in hops])
    pairs = [[completed(one, tiles) for one in kind] for kind in pairs]
    roles = [[{tile: one[tile][1] for tile in one} for one in kind] for kind in (along_x, along_y)]
    roles.append([{hop[0]: (hop[2], 1 - hop[3]) for hop in one} for one in hops])
    roles.append([{hop[1]: hop[2:] for hop in one} for one in hops])
    return pairs, roles


class Roles:
    def __init__(self, roles, tiles):
        self.roles, self.tiles = roles, tiles
        self.counts = [len(kind) for kind in roles[:3]]
        self.tile = lax.axis_index("space")

    def any(self, kind, number, test):
        words = []
        for start in range(0, self.tiles, 32):
            here = [t for t in range(start, min(start + 32, self.tiles)) if t in self.roles[kind][number]]
            word = sum(1 << (t - start) for t in here if test(self.roles[kind][number][t]))
            words.append(word - (1 << 32) if word >> 31 else word)
        word = jnp.int32(words[0])
        for number, other in enumerate(words[1:], 1):
            word = jnp.where(self.tile // 32 == number, jnp.int32(other), word)
        return (lax.shift_right_logical(word, self.tile % 32) & 1) == 1

    def side(self, kind, number, side):
        return self.any(kind, number, lambda role: role == side)

    def linked(self, side):
        found = jnp.bool_(False)
        for number in range(self.counts[1]):
            found = found | self.side(1, number, side)
        return found


def masked(keep, x):
    return jnp.where(keep, x, jnp.zeros_like(x))


def x_faces_kernel(roles, tiles, f_hbm, c_hbm, link_hbm, *refs):
    roles = Roles(roles, tiles)
    *x_refs, flag_ref, link_ref, arrived = refs
    edge = f_hbm.shape[1]
    copies = [pltpu.make_async_copy(link_hbm, link_ref, arrived.at[0])]
    for number, out in enumerate(x_refs):
        plane = jnp.where(roles.side(0, number, 1), edge - 1, 0)
        for source, ref in enumerate((f_hbm, c_hbm)):
            for brick in range(2):
                at = arrived.at[len(copies)]
                copies.append(pltpu.make_async_copy(ref.at[brick, plane], out.at[source, brick], at))
    for copy in copies:
        copy.start()
    for copy in copies:
        copy.wait()
    linked = [[link_ref[brick, way] >= 0 for way in range(4)] for brick in range(2)]
    for number, out in enumerate(x_refs):
        up = roles.side(0, number, 1)
        for brick in range(2):

            @pl.when(jnp.logical_not(jnp.where(up, linked[brick][1], linked[brick][0])))
            def _():
                out[:, brick] = jnp.zeros_like(out[:, brick])

    for row, flag in enumerate((linked[0][2], linked[1][3])):
        flag_ref[8 * row : 8 * row + 8, :] = jnp.full((8, flag_ref.shape[1]), jnp.where(flag, 1.0, 0.0), F32)


def y_faces_kernel(roles, tiles, f_ref, c_ref, flag_ref, *y_refs):
    roles = Roles(roles, tiles)
    edge = f_ref.shape[1]
    rows = []
    for ref in (f_ref, c_ref):
        low = ref[0].astype(F32)[:, 0, :] * flag_ref[:8]
        high = ref[1].astype(F32)[:, edge - 1, :] * flag_ref[8:]
        rows.append((low, high))
    for number, out in enumerate(y_refs):
        up = roles.side(1, number, 1)
        for source, (low, high) in enumerate(rows):
            out[source] = jnp.where(up, high, low).astype(BF16)


def padded(x, channels):
    zeros = jnp.zeros(x.shape[:-1] + (2 * channels,), F32)
    return pltpu.roll(jnp.concatenate([x, zeros], axis=-1), channels, x.ndim - 1)


def weights_kernel(kernel_ref, forward_ref, backward_ref, wide):
    channels = kernel_ref.shape[-1]
    wide[...] = jnp.zeros_like(wide)
    wide[:, :, :channels] = kernel_ref[...].astype(F32)
    for tap in range(9):
        plain = [wide[3 * tap + d] for d in range(3)]
        moved = [pltpu.roll(x, channels, 1) for x in plain]
        steps = (plain[0], plain[1] + moved[0], plain[2] + moved[1], moved[2])
        for number, block in enumerate(steps):
            forward_ref[tap, channels * number : channels * (number + 1), :] = block.astype(BF16)
        last = 8 - tap
        lanes = 2 * channels
        backward_ref[last, :channels, :lanes] = (plain[2] + moved[1]).astype(BF16)
        backward_ref[last, :channels, lanes:] = plain[0].astype(BF16)
        backward_ref[last, channels:, :lanes] = moved[2].astype(BF16)
        backward_ref[last, channels:, lanes:] = (plain[1] + moved[0]).astype(BF16)


def store_line(lines, number, line):
    lanes = lines.shape[1]
    each = line.shape[1] // lanes
    for k in range(each):
        lines[each * number + k : each * number + k + 1, :] = line[:, lanes * k : lanes * (k + 1)]


def load_line(rows, number, each):
    return jnp.concatenate([rows[each * number + k : each * number + k + 1] for k in range(each)], axis=1)


def kernel_grad_kernel(roles, tiles, channels, f_ref, c_ref, *refs):
    roles = Roles(roles, tiles)
    counts = roles.counts
    x_refs = refs[: counts[0]]
    y_refs = refs[counts[0] : counts[0] + counts[1]]
    near = counts[0] + counts[1]
    keep_ref, send_ref = refs[near : near + 2]
    line_refs = refs[near + 2 : near + 2 + counts[0]]
    hop_refs = refs[near + 2 + counts[0] : near + 2 + counts[0] + counts[2]]
    wide, tall, packed, lines = refs[near + 2 + counts[0] + counts[2] :]
    bricks, edge, _, width = f_ref.shape
    rows = edge * edge
    wide[:, edge : edge + rows, :] = padded(f_ref[...].astype(F32).reshape(bricks, rows, width), channels)
    planes = []
    for side in range(2):
        start = side * (edge + rows)
        plane = jnp.zeros((bricks, edge, width), F32)
        for number, ref in enumerate(x_refs):
            plane = jnp.where(roles.side(0, number, side), ref[0].astype(F32), plane)
        planes.append(plane)
        plane = padded(plane, channels)
        for brick in range(bricks):
            wide[brick, start : start + edge, :] = plane[brick]
    own = c_ref[...].astype(F32)
    tall[:, :, edge : 2 * edge, :] = own
    tall[1, :, edge - 1 : edge, :] = own[0, :, edge - 1 :, :]
    tall[0, :, 2 * edge : 2 * edge + 1, :] = own[1, :, 0:1, :]
    halo = {}
    for side in range(2):
        for source in range(2):
            row = jnp.zeros((edge, width), F32)
            for number, ref in enumerate(y_refs):
                row = jnp.where(roles.side(1, number, side), ref[source].astype(F32), row)
            halo[source, side] = row
        at = 2 * edge if side else edge - 1
        tall[side, :, at : at + 1, :] = halo[1, side][:, None, :]
    lanes = 2 * channels
    pairs = width // lanes
    right = []
    for col in range(3):
        value = tall[:, :, edge + 1 - col : 2 * edge + 1 - col, :].reshape(bricks * rows, width).astype(BF16)
        right.append(jnp.concatenate([value[:, lanes * k : lanes * (k + 1)] for k in range(pairs)], axis=0))
    right = jnp.concatenate(right, axis=1)
    low = lax.broadcasted_iota(jnp.int32, (3 * channels // 2, lanes), 1) < channels
    half = 3 * channels // 2
    for row in range(3):
        value = wide[:, edge * row : edge * row + rows, :].reshape(bricks * rows, -1).astype(BF16)
        left = jnp.concatenate([value[:, lanes * k : lanes * (k + 2)] for k in range(pairs)], axis=0)
        grad = lax.dot_general(left, right, (((0,), (0,)), ((), ())), preferred_element_type=F32)
        for col in range(3):
            block = grad[:, lanes * col : lanes * (col + 1)]
            moved = pltpu.roll(block, channels, 1)
            first = block[:half] + moved[channels : channels + half]
            second = moved[half : 2 * half] + block[channels + half :]
            at = half * (3 * row + col)
            packed[at : at + half, :] = jnp.where(low, first, second)
    for number, out in enumerate(line_refs):
        up = roles.side(0, number, 1)
        for (source, side), row in halo.items():
            store_line(lines, 2 * source + side, jnp.where(up, row[edge - 1 : edge], row[0:1]))
        out[...] = lines[...].astype(BF16)
    for number, out in enumerate(hop_refs):
        line = jnp.zeros((1, width), F32)
        for across in range(2):
            for side in range(2):
                at = (edge - 1) * side
                hit = roles.any(2, number, lambda role: role == (across, side))
                line = jnp.where(hit, planes[across][side, at : at + 1, :], line)
        store_line(lines, 0, line)
        out[...] = lines[...].astype(BF16)
    count = keep_ref.shape[0]
    core = lax.axis_index("dp")
    keep_ref[...] = packed[pl.ds(pl.multiple_of(core * count, 8), count), :]
    send_ref[...] = packed[pl.ds(pl.multiple_of((1 - core) * count, 8), count), :]


def conv_kernel(roles, tiles, channels, source, ways, v_ref, *refs):
    roles = Roles(roles, tiles)
    counts = roles.counts
    x_refs = refs[: counts[0]]
    y_refs = refs[counts[0] : counts[0] + counts[1]]
    near = counts[0] + counts[1]
    hops_at = near + counts[0] * ways
    line_refs = refs[near:hops_at]
    hop_refs = refs[hops_at : hops_at + counts[2]]
    weight_ref, out_ref, ext = refs[hops_at + counts[2] :]
    bricks, edge, _, width = v_ref.shape
    rows = edge * edge
    first, last = edge, 2 * edge - 1
    ext[:, 1 : edge + 1, first : last + 1, :] = padded(v_ref[...].astype(F32), channels)
    for side in range(2):
        plane = jnp.zeros((bricks, edge, width), F32)
        for number, ref in enumerate(x_refs):
            plane = jnp.where(roles.side(0, number, side), ref[source].astype(F32), plane)
        plane = padded(plane, channels)
        for brick in range(bricks):
            ext[brick, side * (edge + 1), first : last + 1, :] = plane[brick]
    each = width // line_refs[0].shape[1]
    arrived = [ref[ref.shape[0] - 4 * each :, :].astype(F32) for ref in line_refs]
    if ways == 2:
        first_core = lax.axis_index("dp") == 0
        arrived = [jnp.where(first_core, *arrived)]
    hops = [load_line(ref[...].astype(F32), 0, each) for ref in hop_refs]
    for side in range(2):
        row = jnp.zeros((edge, width), F32)
        for number, ref in enumerate(y_refs):
            row = jnp.where(roles.side(1, number, side), ref[source].astype(F32), row)
        at = last + 1 if side else first - 1
        row = padded(row, channels)
        ext[side, 1 : edge + 1, at : at + 1, :] = row[:, None, :]
        for across in range(2):
            line = jnp.zeros((1, width), F32)
            for number, value in enumerate(arrived):
                line = jnp.where(roles.side(0, number, across), load_line(value, 2 * source + side, each), line)
            if source == 0:
                line = masked(roles.linked(side), line)
                for number, value in enumerate(hops):
                    line = jnp.where(roles.any(3, number, lambda role: role == (across, side)), value, line)
            ext[side, across * (edge + 1), at : at + 1, :] = padded(line, channels)
    ext[1, :, first - 1 : first, :] = ext[0, :, last : last + 1, :]
    ext[0, :, last + 1 : last + 2, :] = ext[1, :, first : first + 1, :]
    lanes = 2 * channels
    pairs = width // lanes
    total = jnp.zeros((pairs * bricks * rows, lanes), F32)
    contract = 0 if source == 0 else 1
    for col in range(3):
        for row in range(3):
            value = ext[:, row : row + edge, first - 1 + col : last + col, :]
            value = value.reshape(bricks * rows, -1).astype(BF16)
            left = jnp.concatenate([value[:, lanes * k : lanes * (k + 2)] for k in range(pairs)], axis=0)
            total = total + lax.dot_general(
                left, weight_ref[3 * row + col], (((1,), (contract,)), ((), ())), preferred_element_type=F32
            )
    for k in range(pairs):
        out_ref[:, lanes * k : lanes * (k + 1)] = total[bricks * rows * k : bricks * rows * (k + 1)].astype(BF16)


def unpack_kernel(factor, own_ref, other_ref, out_hbm, out_ref, sent):
    count = own_ref.shape[0]
    first_half = lax.axis_index("dp") == 0
    taps, rows, channels = out_ref.shape
    half = rows // 2

    def packed(start, stop):
        pieces = []
        for low, ref, other in ((0, own_ref, other_ref), (count, other_ref, own_ref)):
            here = slice(max(start - low, 0), min(stop - low, count))
            if here.start < here.stop:
                pieces.append(jnp.where(first_half, ref[here], other[here]))
        return jnp.concatenate(pieces, axis=0) * factor

    copies = []
    for tap in range(taps):
        block = packed(half * tap, half * (tap + 1))
        out_ref[tap, :half, :] = block[:, :channels]
        out_ref[tap, half:, :] = pltpu.roll(block, channels, 1)[:, :channels]
        copies.append(pltpu.make_async_copy(out_ref.at[tap], out_hbm.at[tap], sent.at[tap]))
        copies[-1].start()
    for copy in copies:
        copy.wait()


VMEM = pl.BlockSpec(memory_space=pltpu.VMEM)
HBM = pl.BlockSpec(memory_space=pltpu.HBM)


def call(kernel, in_specs, out_shapes, scratch=(), flops=0, name=None, vmem=24 * 2**20, out=None):
    several = isinstance(out_shapes, list)
    return pl.pallas_call(
        kernel,
        in_specs=in_specs,
        out_specs=[VMEM] * len(out_shapes) if several else (out or VMEM),
        out_shape=out_shapes,
        scratch_shapes=list(scratch),
        compiler_params=pltpu.CompilerParams(vmem_limit_bytes=vmem),
        cost_estimate=pl.CostEstimate(flops=flops, bytes_accessed=2**20, transcendentals=0),
        name=name,
    )


def body(tiles, features, cotangent, kernel, neighbours):
    pairs, roles = make_plan(tiles)
    counts = [len(kind) for kind in pairs]
    bricks, edge = features.shape[1:3]
    width = features.shape[-1]
    channels = kernel.shape[-1]
    rows = edge * edge
    lanes = 2 * channels
    shape = jax.ShapeDtypeStruct
    f = features.reshape(bricks, edge, edge, width)
    c = cotangent.reshape(bricks, edge, edge, width)
    links = neighbours.reshape(bricks, 6)

    near = counts[0] + counts[1]
    *faces, flags = call(
        functools.partial(x_faces_kernel, roles, tiles),
        [HBM, HBM, HBM],
        [pltpu.VMEM((2, bricks, edge, width), BF16)] * counts[0] + [pltpu.VMEM((16, width), F32)],
        [pltpu.SMEM(links.shape, jnp.int32), pltpu.SemaphoreType.DMA((4 * counts[0] + 1,))],
        name="x_faces",
        vmem=None,
    )(f, c, links)
    got = [lax.ppermute(x, "space", one) for x, one in zip(faces, pairs[0])]
    faces = call(
        functools.partial(y_faces_kernel, roles, tiles),
        [VMEM] * 3,
        [pltpu.VMEM((2, edge, width), BF16)] * counts[1],
        name="y_faces",
    )(f, c, flags)
    got += [lax.ppermute(x, "space", one) for x, one in zip(faces, pairs[1])]
    count = 27 * channels * channels // lanes // 2
    line_rows = 4 * width // lanes
    keep, send, *lines = call(
        functools.partial(kernel_grad_kernel, roles, tiles, channels),
        [VMEM, VMEM] + [VMEM] * near,
        [shape((count, lanes), F32)] * 2 + [shape((line_rows, lanes), BF16)] * (counts[0] + counts[2]),
        [
            pltpu.VMEM((bricks, rows + 2 * edge, width + lanes), F32),
            pltpu.VMEM((bricks, edge, 3 * edge, width), F32),
            pltpu.VMEM((2 * count, lanes), F32),
            pltpu.VMEM((line_rows, lanes), F32),
        ],
        flops=2 * 768 * 384 * 512,
        name="kernel_grad",
    )(f, c, *got)

    forward, backward = call(
        weights_kernel,
        [VMEM],
        [shape((9, 4 * channels, lanes), BF16), shape((9, lanes, 4 * channels), BF16)],
        [pltpu.VMEM((27, channels, lanes), F32)],
        name="weights",
    )(kernel.reshape(27, channels, channels))

    def conv(source, x, weight):
        return call(
            functools.partial(conv_kernel, roles, tiles, channels, source, ready),
            [VMEM] * (2 + len(got)),
            shape((bricks * rows, width), BF16),
            [pltpu.VMEM((bricks, edge + 2, 3 * edge, width + lanes), F32)],
            flops=2 * 512 * 256 * 128 * 9,
            name="response" if source == 0 else "feature_grad",
        )(x, *got, weight)

    cores = lax.axis_size("dp")
    swap = [(0, 1), (1, 0)]
    part = keep + lax.ppermute(send, "dp", swap)
    bits = [1 << number for number in range(tiles.bit_length() - 1)]
    orders = [bits, bits]
    wire = BF16 if len(bits) <= 3 else F32
    shared = [bit for bit in bits if pairs[0] == [[(i, i ^ bit) for i in range(tiles)]]]
    joined = bool(shared) and len(bits) == 3
    if joined:
        first, last = (bit for bit in bits if bit not in shared)
        orders = [shared + [first, last], [last] + shared + [first]]
    hops = [lax.ppermute(x, "space", one) for x, one in zip(lines[counts[0] :], pairs[2])]
    lines = lines[: counts[0]]
    if not joined:
        got += [lax.ppermute(x, "space", one) for x, one in zip(lines, pairs[0])]
    ready = 2 if joined else 1
    for number in range(len(bits)):
        step = [
            (tile * cores + core, (tile ^ order[number]) * cores + core)
            for tile in range(tiles)
            for core, order in enumerate(orders)
        ]
        mine = part.astype(wire)
        carries = joined and number < ready
        if carries:
            mine = jnp.concatenate([mine, lines[0]], axis=0)
        if number == 1:
            mine, hops, forward, backward = lax.optimization_barrier((mine, hops, forward, backward))
        else:
            mine = lax.optimization_barrier(mine)
        if number == ready:
            got += hops
            response = conv(0, f, forward)
            feature_grad = conv(1, c, backward)
        theirs = lax.ppermute(mine, ("space", "dp"), step)
        if carries:
            got.append(theirs)
            mine, theirs = mine[:count], theirs[:count]
        part = mine.astype(F32) + theirs.astype(F32)
    part, response = lax.optimization_barrier((part, response))
    other = lax.ppermute(part, "dp", swap)
    other, feature_grad = lax.optimization_barrier((other, feature_grad))
    response, feature_grad = (x.reshape(features.shape) for x in (response, feature_grad))
    cells = bricks * tiles * lax.axis_size("dp") * edge**3
    kernel_grad = call(
        functools.partial(unpack_kernel, 1.0 / math.sqrt(cells)),
        [VMEM, VMEM],
        shape((9, 3 * channels, channels), F32),
        [pltpu.VMEM((9, 3 * channels, channels), F32), pltpu.SemaphoreType.DMA((9,))],
        name="unpack",
        out=HBM,
    )(part, other).reshape(kernel.shape)
    return response, feature_grad, kernel_grad


def solution(mesh):
    bricks_spec = P(("groups", "dp"), "space", None, None, None)
    return jax.shard_map(
        functools.partial(body, mesh.shape["space"]),
        mesh=mesh,
        in_specs=(bricks_spec, bricks_spec, P(), P(("groups", "dp"), "space", None)),
        out_specs=(bricks_spec, bricks_spec, P("groups", None, None, None, None)),
        check_vma=False,
    )
```

```python
import functools
import math

import jax
import jax.numpy as jnp
from jax import lax
from jax.experimental import pallas as pl
from jax.experimental.pallas import tpu as pltpu
from jax.sharding import PartitionSpec as P

TILES_Y = 4
F32 = jnp.float32
BF16 = jnp.bfloat16


def step_y(tile, sign, tiles):
    column = (tile + TILES_Y // 2) % TILES_Y + sign
    near = tile + sign
    return near if 0 <= column < TILES_Y and 0 <= near < tiles else None


def step_x(tile, sign, tiles):
    near = tile + sign * TILES_Y
    return near if 0 <= near < tiles else None


def rounds(edges):
    found = []
    for low, high in edges:
        for one in found:
            if low not in one and high not in one:
                break
        else:
            one = {}
            found.append(one)
        one[low] = (high, 1)
        one[high] = (low, 0)
    return found


def detours(tiles):
    found = []
    for tile in range(tiles):
        for across in range(2):
            for along in range(2):
                sender = step_y(tile, 2 * along - 1, tiles)
                if sender is None or step_x(sender, 2 * across - 1, tiles) is None:
                    continue
                if step_x(tile, 2 * across - 1, tiles) is not None:
                    continue
                for one in found:
                    if all(hop[0] != sender and hop[1] != tile for hop in one):
                        break
                else:
                    one = []
                    found.append(one)
                one.append((sender, tile, across, along))
    return found


def completed(pairs, tiles):
    idle = [tile for tile in range(tiles) if all(tile != a for a, _ in pairs) and all(tile != b for _, b in pairs)]
    active = [(2 * a + core, 2 * b + core) for a, b in pairs for core in range(2)]
    return sorted(active + [(2 * tile + core, 2 * tile + 1 - core) for tile in idle for core in range(2)])


def make_plan(tiles):
    def edges(step):
        return [(tile, step(tile, 1, tiles)) for tile in range(tiles) if step(tile, 1, tiles) is not None]

    along_x, along_y, hops = rounds(edges(step_x)), rounds(edges(step_y)), detours(tiles)
    pairs = [[[(tile, one[tile][0]) for tile in sorted(one)] for one in kind] for kind in (along_x, along_y)]
    pairs.append([[hop[:2] for hop in one] for one in hops])
    meetings = pairs[0]
    pairs = [[completed(one, tiles) for one in kind] for kind in pairs]
    roles = [[{tile: one[tile][1] for tile in one} for one in kind] for kind in (along_x, along_y)]
    roles.append([{hop[0]: (hop[2], 1 - hop[3]) for hop in one} for one in hops])
    roles.append([{hop[1]: hop[2:] for hop in one} for one in hops])
    return pairs, roles, meetings


class Roles:
    def __init__(self, roles, tiles):
        self.roles, self.tiles = roles, tiles
        self.counts = [len(kind) for kind in roles[:3]]
        self.tile = lax.axis_index("space")

    def any(self, kind, number, test):
        words = []
        for start in range(0, self.tiles, 32):
            here = [t for t in range(start, min(start + 32, self.tiles)) if t in self.roles[kind][number]]
            word = sum(1 << (t - start) for t in here if test(self.roles[kind][number][t]))
            words.append(word - (1 << 32) if word >> 31 else word)
        word = jnp.int32(words[0])
        for number, other in enumerate(words[1:], 1):
            word = jnp.where(self.tile // 32 == number, jnp.int32(other), word)
        return (lax.shift_right_logical(word, self.tile % 32) & 1) == 1

    def side(self, kind, number, side):
        return self.any(kind, number, lambda role: role == side)

    def linked(self, side):
        found = jnp.bool_(False)
        for number in range(self.counts[1]):
            found = found | self.side(1, number, side)
        return found


def masked(keep, x):
    return jnp.where(keep, x, jnp.zeros_like(x))


def x_faces_kernel(roles, tiles, f_hbm, c_hbm, link_hbm, *refs):
    roles = Roles(roles, tiles)
    *x_refs, flag_ref, link_ref, arrived = refs
    edge = f_hbm.shape[1]
    copies = [pltpu.make_async_copy(link_hbm, link_ref, arrived.at[0])]
    for number, out in enumerate(x_refs):
        plane = jnp.where(roles.side(0, number, 1), edge - 1, 0)
        for source, ref in enumerate((f_hbm, c_hbm)):
            for brick in range(2):
                at = arrived.at[len(copies)]
                copies.append(pltpu.make_async_copy(ref.at[brick, plane], out.at[source, brick], at))
    for copy in copies:
        copy.start()
    for copy in copies:
        copy.wait()
    linked = [[link_ref[brick, way] >= 0 for way in range(4)] for brick in range(2)]
    for number, out in enumerate(x_refs):
        up = roles.side(0, number, 1)
        for brick in range(2):

            @pl.when(jnp.logical_not(jnp.where(up, linked[brick][1], linked[brick][0])))
            def _():
                out[:, brick] = jnp.zeros_like(out[:, brick])

    for row, flag in enumerate((linked[0][2], linked[1][3])):
        flag_ref[8 * row : 8 * row + 8, :] = jnp.full((8, flag_ref.shape[1]), jnp.where(flag, 1.0, 0.0), F32)


def y_faces_kernel(roles, tiles, f_ref, c_ref, flag_ref, *y_refs):
    roles = Roles(roles, tiles)
    edge = f_ref.shape[1]
    rows = []
    for ref in (f_ref, c_ref):
        low = ref[0].astype(F32)[:, 0, :] * flag_ref[:8]
        high = ref[1].astype(F32)[:, edge - 1, :] * flag_ref[8:]
        rows.append((low, high))
    for number, out in enumerate(y_refs):
        up = roles.side(1, number, 1)
        for source, (low, high) in enumerate(rows):
            out[source] = jnp.where(up, high, low).astype(BF16)


def padded(x, channels):
    zeros = jnp.zeros(x.shape[:-1] + (2 * channels,), F32)
    return pltpu.roll(jnp.concatenate([x, zeros], axis=-1), channels, x.ndim - 1)


def weights_kernel(kernel_ref, forward_ref, backward_ref, wide):
    channels = kernel_ref.shape[-1]
    wide[...] = jnp.zeros_like(wide)
    wide[:, :, :channels] = kernel_ref[...].astype(F32)
    for tap in range(9):
        plain = [wide[3 * tap + d] for d in range(3)]
        moved = [pltpu.roll(x, channels, 1) for x in plain]
        steps = (plain[0], plain[1] + moved[0], plain[2] + moved[1], moved[2])
        for number, block in enumerate(steps):
            forward_ref[tap, channels * number : channels * (number + 1), :] = block.astype(BF16)
        last = 8 - tap
        lanes = 2 * channels
        backward_ref[last, :channels, :lanes] = (plain[2] + moved[1]).astype(BF16)
        backward_ref[last, :channels, lanes:] = plain[0].astype(BF16)
        backward_ref[last, channels:, :lanes] = moved[2].astype(BF16)
        backward_ref[last, channels:, lanes:] = (plain[1] + moved[0]).astype(BF16)


def store_line(lines, number, line):
    lanes = lines.shape[1]
    each = line.shape[1] // lanes
    for k in range(each):
        lines[each * number + k : each * number + k + 1, :] = line[:, lanes * k : lanes * (k + 1)]


def load_line(rows, number, each):
    return jnp.concatenate([rows[each * number + k : each * number + k + 1] for k in range(each)], axis=1)


def kernel_grad_kernel(roles, tiles, channels, f_ref, c_ref, *refs):
    roles = Roles(roles, tiles)
    counts = roles.counts
    x_refs = refs[: counts[0]]
    y_refs = refs[counts[0] : counts[0] + counts[1]]
    near = counts[0] + counts[1]
    keep_ref, send_ref = refs[near : near + 2]
    line_refs = refs[near + 2 : near + 2 + counts[0]]
    hop_refs = refs[near + 2 + counts[0] : near + 2 + counts[0] + counts[2]]
    wide, tall, packed, lines = refs[near + 2 + counts[0] + counts[2] :]
    bricks, edge, _, width = f_ref.shape
    rows = edge * edge
    wide[:, edge : edge + rows, :] = padded(f_ref[...].astype(F32).reshape(bricks, rows, width), channels)
    planes = []
    for side in range(2):
        start = side * (edge + rows)
        plane = jnp.zeros((bricks, edge, width), F32)
        for number, ref in enumerate(x_refs):
            plane = jnp.where(roles.side(0, number, side), ref[0].astype(F32), plane)
        planes.append(plane)
        plane = padded(plane, channels)
        for brick in range(bricks):
            wide[brick, start : start + edge, :] = plane[brick]
    own = c_ref[...].astype(F32)
    tall[:, :, edge : 2 * edge, :] = own
    tall[1, :, edge - 1 : edge, :] = own[0, :, edge - 1 :, :]
    tall[0, :, 2 * edge : 2 * edge + 1, :] = own[1, :, 0:1, :]
    halo = {}
    for side in range(2):
        for source in range(2):
            row = jnp.zeros((edge, width), F32)
            for number, ref in enumerate(y_refs):
                row = jnp.where(roles.side(1, number, side), ref[source].astype(F32), row)
            halo[source, side] = row
        at = 2 * edge if side else edge - 1
        tall[side, :, at : at + 1, :] = halo[1, side][:, None, :]
    lanes = 2 * channels
    pairs = width // lanes
    right = []
    for col in range(3):
        value = tall[:, :, edge + 1 - col : 2 * edge + 1 - col, :].reshape(bricks * rows, width).astype(BF16)
        right.append(jnp.concatenate([value[:, lanes * k : lanes * (k + 1)] for k in range(pairs)], axis=0))
    right = jnp.concatenate(right, axis=1)
    low = lax.broadcasted_iota(jnp.int32, (3 * channels // 2, lanes), 1) < channels
    half = 3 * channels // 2
    left = []
    for row in range(3):
        value = wide[:, edge * row : edge * row + rows, :].reshape(bricks * rows, -1).astype(BF16)
        left.append(jnp.concatenate([value[:, lanes * k : lanes * (k + 2)] for k in range(pairs)], axis=0))
    left = jnp.concatenate(left, axis=1)
    every = lax.dot_general(left, right, (((0,), (0,)), ((), ())), preferred_element_type=F32)
    for row in range(3):
        grad = every[2 * lanes * row : 2 * lanes * (row + 1)]
        for col in range(3):
            block = grad[:, lanes * col : lanes * (col + 1)]
            moved = pltpu.roll(block, channels, 1)
            first = block[:half] + moved[channels : channels + half]
            second = moved[half : 2 * half] + block[channels + half :]
            at = half * (3 * row + col)
            packed[at : at + half, :] = jnp.where(low, first, second)
    for number, out in enumerate(line_refs):
        up = roles.side(0, number, 1)
        for (source, side), row in halo.items():
            store_line(lines, 2 * source + side, jnp.where(up, row[edge - 1 : edge], row[0:1]))
        out[...] = lines[...].astype(BF16)
    for number, out in enumerate(hop_refs):
        line = jnp.zeros((1, width), F32)
        for across in range(2):
            for side in range(2):
                at = (edge - 1) * side
                hit = roles.any(2, number, lambda role: role == (across, side))
                line = jnp.where(hit, planes[across][side, at : at + 1, :], line)
        store_line(lines, 0, line)
        out[...] = lines[...].astype(BF16)
    count = keep_ref.shape[0]
    core = lax.axis_index("dp")
    keep_ref[...] = packed[pl.ds(pl.multiple_of(core * count, 8), count), :]
    send_ref[...] = packed[pl.ds(pl.multiple_of((1 - core) * count, 8), count), :]


def conv_kernel(roles, tiles, channels, source, ways, v_ref, *refs):
    roles = Roles(roles, tiles)
    counts = roles.counts
    x_refs = refs[: counts[0]]
    y_refs = refs[counts[0] : counts[0] + counts[1]]
    near = counts[0] + counts[1]
    hops_at = near + counts[0] * ways
    line_refs = refs[near:hops_at]
    hop_refs = refs[hops_at : hops_at + counts[2]]
    weight_ref, out_ref, ext = refs[hops_at + counts[2] :]
    bricks, edge, _, width = v_ref.shape
    rows = edge * edge
    first, last = edge, 2 * edge - 1
    ext[:, 1 : edge + 1, first : last + 1, :] = padded(v_ref[...].astype(F32), channels)
    for side in range(2):
        plane = jnp.zeros((bricks, edge, width), F32)
        for number, ref in enumerate(x_refs):
            plane = jnp.where(roles.side(0, number, side), ref[source].astype(F32), plane)
        plane = padded(plane, channels)
        for brick in range(bricks):
            ext[brick, side * (edge + 1), first : last + 1, :] = plane[brick]
    each = width // line_refs[0].shape[1]
    arrived = [ref[ref.shape[0] - 4 * each :, :].astype(F32) for ref in line_refs]
    if ways == 2:
        first_core = lax.axis_index("dp") == 0
        arrived = [jnp.where(first_core, *arrived)]
    hops = [load_line(ref[...].astype(F32), 0, each) for ref in hop_refs]
    for side in range(2):
        row = jnp.zeros((edge, width), F32)
        for number, ref in enumerate(y_refs):
            row = jnp.where(roles.side(1, number, side), ref[source].astype(F32), row)
        at = last + 1 if side else first - 1
        row = padded(row, channels)
        ext[side, 1 : edge + 1, at : at + 1, :] = row[:, None, :]
        for across in range(2):
            line = jnp.zeros((1, width), F32)
            for number, value in enumerate(arrived):
                line = jnp.where(roles.side(0, number, across), load_line(value, 2 * source + side, each), line)
            if source == 0:
                line = masked(roles.linked(side), line)
                for number, value in enumerate(hops):
                    line = jnp.where(roles.any(3, number, lambda role: role == (across, side)), value, line)
            ext[side, across * (edge + 1), at : at + 1, :] = padded(line, channels)
    ext[1, :, first - 1 : first, :] = ext[0, :, last : last + 1, :]
    ext[0, :, last + 1 : last + 2, :] = ext[1, :, first : first + 1, :]
    lanes = 2 * channels
    pairs = width // lanes
    total = jnp.zeros((pairs * bricks * rows, lanes), F32)
    contract = 0 if source == 0 else 1
    for col in range(3):
        for row in range(3):
            value = ext[:, row : row + edge, first - 1 + col : last + col, :]
            value = value.reshape(bricks * rows, -1).astype(BF16)
            left = jnp.concatenate([value[:, lanes * k : lanes * (k + 2)] for k in range(pairs)], axis=0)
            total = total + lax.dot_general(
                left, weight_ref[3 * row + col], (((1,), (contract,)), ((), ())), preferred_element_type=F32
            )
    for k in range(pairs):
        out_ref[:, lanes * k : lanes * (k + 1)] = total[bricks * rows * k : bricks * rows * (k + 1)].astype(BF16)


def unpack_kernel(factor, own_ref, other_ref, out_hbm, out_ref, sent):
    count = own_ref.shape[0]
    first_half = lax.axis_index("dp") == 0
    taps, rows, channels = out_ref.shape
    half = rows // 2

    def packed(start, stop):
        pieces = []
        for low, ref, other in ((0, own_ref, other_ref), (count, other_ref, own_ref)):
            here = slice(max(start - low, 0), min(stop - low, count))
            if here.start < here.stop:
                pieces.append(jnp.where(first_half, ref[here], other[here]))
        return jnp.concatenate(pieces, axis=0) * factor

    copies = []
    for tap in range(taps):
        block = packed(half * tap, half * (tap + 1))
        out_ref[tap, :half, :] = block[:, :channels]
        out_ref[tap, half:, :] = pltpu.roll(block, channels, 1)[:, :channels]
        copies.append(pltpu.make_async_copy(out_ref.at[tap], out_hbm.at[tap], sent.at[tap]))
        copies[-1].start()
    for copy in copies:
        copy.wait()


VMEM = pl.BlockSpec(memory_space=pltpu.VMEM)
HBM = pl.BlockSpec(memory_space=pltpu.HBM)


def call(kernel, in_specs, out_shapes, scratch=(), flops=0, name=None, vmem=24 * 2**20, out=None):
    several = isinstance(out_shapes, list)
    return pl.pallas_call(
        kernel,
        in_specs=in_specs,
        out_specs=[VMEM] * len(out_shapes) if several else (out or VMEM),
        out_shape=out_shapes,
        scratch_shapes=list(scratch),
        compiler_params=pltpu.CompilerParams(vmem_limit_bytes=vmem),
        cost_estimate=pl.CostEstimate(flops=flops, bytes_accessed=2**20, transcendentals=0),
        name=name,
    )


def body(tiles, features, cotangent, kernel, neighbours):
    pairs, roles, meetings = make_plan(tiles)
    counts = [len(kind) for kind in pairs]
    bricks, edge = features.shape[1:3]
    width = features.shape[-1]
    channels = kernel.shape[-1]
    rows = edge * edge
    lanes = 2 * channels
    shape = jax.ShapeDtypeStruct
    f = features.reshape(bricks, edge, edge, width)
    c = cotangent.reshape(bricks, edge, edge, width)
    links = neighbours.reshape(bricks, 6)

    near = counts[0] + counts[1]
    *faces, flags = call(
        functools.partial(x_faces_kernel, roles, tiles),
        [HBM, HBM, HBM],
        [pltpu.VMEM((2, bricks, edge, width), BF16)] * counts[0] + [pltpu.VMEM((16, width), F32)],
        [pltpu.SMEM(links.shape, jnp.int32), pltpu.SemaphoreType.DMA((4 * counts[0] + 1,))],
        name="x_faces",
        vmem=None,
    )(f, c, links)
    got = [lax.ppermute(x, ("space", "dp"), one) for x, one in zip(faces, pairs[0])]
    faces = call(
        functools.partial(y_faces_kernel, roles, tiles),
        [VMEM] * 3,
        [pltpu.VMEM((2, edge, width), BF16)] * counts[1],
        name="y_faces",
    )(f, c, flags)
    got += [lax.ppermute(x, ("space", "dp"), one) for x, one in zip(faces, pairs[1])]
    count = 27 * channels * channels // lanes // 2
    line_rows = 4 * width // lanes
    keep, send, *lines = call(
        functools.partial(kernel_grad_kernel, roles, tiles, channels),
        [VMEM, VMEM] + [VMEM] * near,
        [shape((count, lanes), F32)] * 2 + [shape((line_rows, lanes), BF16)] * (counts[0] + counts[2]),
        [
            pltpu.VMEM((bricks, rows + 2 * edge, width + lanes), F32),
            pltpu.VMEM((bricks, edge, 3 * edge, width), F32),
            pltpu.VMEM((2 * count, lanes), F32),
            pltpu.VMEM((line_rows, lanes), F32),
        ],
        flops=2 * 768 * 384 * 512,
        name="kernel_grad",
    )(f, c, *got)

    forward, backward = call(
        weights_kernel,
        [VMEM],
        [shape((9, 4 * channels, lanes), BF16), shape((9, lanes, 4 * channels), BF16)],
        [pltpu.VMEM((27, channels, lanes), F32)],
        name="weights",
    )(kernel.reshape(27, channels, channels))

    def conv(source, x, weight):
        return call(
            functools.partial(conv_kernel, roles, tiles, channels, source, ready),
            [VMEM] * (2 + len(got)),
            shape((bricks * rows, width), BF16),
            [pltpu.VMEM((bricks, edge + 2, 3 * edge, width + lanes), F32)],
            flops=2 * 512 * 256 * 128 * 9,
            name="response" if source == 0 else "feature_grad",
        )(x, *got, weight)

    cores = lax.axis_size("dp")
    swap = [(0, 1), (1, 0)]
    part = keep + lax.ppermute(send, "dp", swap)
    bits = [1 << number for number in range(tiles.bit_length() - 1)]
    orders = [bits, bits]
    wire = BF16 if len(bits) <= 3 else F32
    shared = [bit for bit in bits if meetings == [[(i, i ^ bit) for i in range(tiles)]]]
    joined = bool(shared) and len(bits) == 3
    if joined:
        first, last = (bit for bit in bits if bit not in shared)
        orders = [shared + [first, last], [last] + shared + [first]]
    hops = [lax.ppermute(x, ("space", "dp"), one) for x, one in zip(lines[counts[0] :], pairs[2])]
    lines = lines[: counts[0]]
    if not joined:
        got += [lax.ppermute(x, ("space", "dp"), one) for x, one in zip(lines, pairs[0])]
    ready = 2 if joined else 1
    for number in range(len(bits)):
        step = [
            (tile * cores + core, (tile ^ order[number]) * cores + core)
            for tile in range(tiles)
            for core, order in enumerate(orders)
        ]
        mine = part.astype(wire)
        carries = joined and number < ready
        if carries:
            mine = jnp.concatenate([mine, lines[0]], axis=0)
        if number == 1:
            mine, hops, forward, backward = lax.optimization_barrier((mine, hops, forward, backward))
        else:
            mine = lax.optimization_barrier(mine)
        if number == ready:
            got += hops
            response = conv(0, f, forward)
            feature_grad = conv(1, c, backward)
        theirs = lax.ppermute(mine, ("space", "dp"), step)
        if carries:
            got.append(theirs)
            mine, theirs = mine[:count], theirs[:count]
        part = mine.astype(F32) + theirs.astype(F32)
    part, response = lax.optimization_barrier((part, response))
    other = lax.ppermute(part, "dp", swap)
    other, feature_grad = lax.optimization_barrier((other, feature_grad))
    response, feature_grad = (x.reshape(features.shape) for x in (response, feature_grad))
    cells = bricks * tiles * lax.axis_size("dp") * edge**3
    kernel_grad = call(
        functools.partial(unpack_kernel, 1.0 / math.sqrt(cells)),
        [VMEM, VMEM],
        shape((9, 3 * channels, channels), F32),
        [pltpu.VMEM((9, 3 * channels, channels), F32), pltpu.SemaphoreType.DMA((9,))],
        name="unpack",
        out=HBM,
    )(part, other).reshape(kernel.shape)
    return response, feature_grad, kernel_grad


def solution(mesh):
    bricks_spec = P(("groups", "dp"), "space", None, None, None)
    return jax.shard_map(
        functools.partial(body, mesh.shape["space"]),
        mesh=mesh,
        in_specs=(bricks_spec, bricks_spec, P(), P(("groups", "dp"), "space", None)),
        out_specs=(bricks_spec, bricks_spec, P("groups", None, None, None, None)),
        check_vma=False,
    )
```

```python
import functools
import math

import jax
import jax.numpy as jnp
from jax import lax
from jax.experimental import pallas as pl
from jax.experimental.pallas import tpu as pltpu
from jax.sharding import PartitionSpec as P

TILES_Y = 4
F32 = jnp.float32
BF16 = jnp.bfloat16


def step_y(tile, sign, tiles):
    column = (tile + TILES_Y // 2) % TILES_Y + sign
    near = tile + sign
    return near if 0 <= column < TILES_Y and 0 <= near < tiles else None


def step_x(tile, sign, tiles):
    near = tile + sign * TILES_Y
    return near if 0 <= near < tiles else None


def rounds(edges):
    found = []
    for low, high in edges:
        for one in found:
            if low not in one and high not in one:
                break
        else:
            one = {}
            found.append(one)
        one[low] = (high, 1)
        one[high] = (low, 0)
    return found


def detours(tiles):
    found = []
    for tile in range(tiles):
        for across in range(2):
            for along in range(2):
                sender = step_y(tile, 2 * along - 1, tiles)
                if sender is None or step_x(sender, 2 * across - 1, tiles) is None:
                    continue
                if step_x(tile, 2 * across - 1, tiles) is not None:
                    continue
                for one in found:
                    if all(hop[0] != sender and hop[1] != tile for hop in one):
                        break
                else:
                    one = []
                    found.append(one)
                one.append((sender, tile, across, along))
    return found


def completed(pairs, tiles):
    idle = [tile for tile in range(tiles) if all(tile != a for a, _ in pairs) and all(tile != b for _, b in pairs)]
    active = [(2 * a + core, 2 * b + core) for a, b in pairs for core in range(2)]
    return sorted(active + [(2 * tile + core, 2 * tile + 1 - core) for tile in idle for core in range(2)])


def make_plan(tiles):
    def edges(step):
        return [(tile, step(tile, 1, tiles)) for tile in range(tiles) if step(tile, 1, tiles) is not None]

    along_x, along_y, hops = rounds(edges(step_x)), rounds(edges(step_y)), detours(tiles)
    pairs = [[[(tile, one[tile][0]) for tile in sorted(one)] for one in kind] for kind in (along_x, along_y)]
    pairs.append([[hop[:2] for hop in one] for one in hops])
    meetings = pairs[0]
    pairs = [[completed(one, tiles) for one in kind] for kind in pairs]
    roles = [[{tile: one[tile][1] for tile in one} for one in kind] for kind in (along_x, along_y)]
    roles.append([{hop[0]: (hop[2], 1 - hop[3]) for hop in one} for one in hops])
    roles.append([{hop[1]: hop[2:] for hop in one} for one in hops])
    return pairs, roles, meetings


class Roles:
    def __init__(self, roles, tiles):
        self.roles, self.tiles = roles, tiles
        self.counts = [len(kind) for kind in roles[:3]]
        self.tile = lax.axis_index("space")

    def any(self, kind, number, test):
        words = []
        for start in range(0, self.tiles, 32):
            here = [t for t in range(start, min(start + 32, self.tiles)) if t in self.roles[kind][number]]
            word = sum(1 << (t - start) for t in here if test(self.roles[kind][number][t]))
            words.append(word - (1 << 32) if word >> 31 else word)
        word = jnp.int32(words[0])
        for number, other in enumerate(words[1:], 1):
            word = jnp.where(self.tile // 32 == number, jnp.int32(other), word)
        return (lax.shift_right_logical(word, self.tile % 32) & 1) == 1

    def side(self, kind, number, side):
        return self.any(kind, number, lambda role: role == side)

    def linked(self, side):
        found = jnp.bool_(False)
        for number in range(self.counts[1]):
            found = found | self.side(1, number, side)
        return found


def half_of(tile, core):
    for shift in (16, 8, 4, 2, 1):
        tile = tile ^ (tile >> shift)
    return core ^ (tile & 1)


def my_half():
    return half_of(lax.axis_index("space"), lax.axis_index("dp"))


def masked(keep, x):
    return jnp.where(keep, x, jnp.zeros_like(x))


def x_faces_kernel(roles, tiles, f_hbm, c_hbm, link_hbm, *refs):
    roles = Roles(roles, tiles)
    *x_refs, flag_ref, link_ref, arrived = refs
    edge = f_hbm.shape[1]
    copies = [pltpu.make_async_copy(link_hbm, link_ref, arrived.at[0])]
    for number, out in enumerate(x_refs):
        plane = jnp.where(roles.side(0, number, 1), edge - 1, 0)
        for source, ref in enumerate((f_hbm, c_hbm)):
            for brick in range(2):
                at = arrived.at[len(copies)]
                copies.append(pltpu.make_async_copy(ref.at[brick, plane], out.at[source, brick], at))
    for copy in copies:
        copy.start()
    for copy in copies:
        copy.wait()
    linked = [[link_ref[brick, way] >= 0 for way in range(4)] for brick in range(2)]
    for number, out in enumerate(x_refs):
        up = roles.side(0, number, 1)
        for brick in range(2):

            @pl.when(jnp.logical_not(jnp.where(up, linked[brick][1], linked[brick][0])))
            def _():
                out[:, brick] = jnp.zeros_like(out[:, brick])

    for row, flag in enumerate((linked[0][2], linked[1][3])):
        flag_ref[8 * row : 8 * row + 8, :] = jnp.full((8, flag_ref.shape[1]), jnp.where(flag, 1.0, 0.0), F32)


def y_faces_kernel(roles, tiles, f_ref, c_ref, flag_ref, *y_refs):
    roles = Roles(roles, tiles)
    edge = f_ref.shape[1]
    rows = []
    for ref in (f_ref, c_ref):
        low = ref[0].astype(F32)[:, 0, :] * flag_ref[:8]
        high = ref[1].astype(F32)[:, edge - 1, :] * flag_ref[8:]
        rows.append((low, high))
    for number, out in enumerate(y_refs):
        up = roles.side(1, number, 1)
        for source, (low, high) in enumerate(rows):
            out[source] = jnp.where(up, high, low).astype(BF16)


def padded(x, channels):
    zeros = jnp.zeros(x.shape[:-1] + (2 * channels,), F32)
    return pltpu.roll(jnp.concatenate([x, zeros], axis=-1), channels, x.ndim - 1)


def weights_kernel(kernel_ref, forward_ref, backward_ref, wide):
    channels = kernel_ref.shape[-1]
    wide[...] = jnp.zeros_like(wide)
    wide[:, :, :channels] = kernel_ref[...].astype(F32)
    for tap in range(9):
        plain = [wide[3 * tap + d] for d in range(3)]
        moved = [pltpu.roll(x, channels, 1) for x in plain]
        steps = (plain[0], plain[1] + moved[0], plain[2] + moved[1], moved[2])
        for number, block in enumerate(steps):
            forward_ref[tap, channels * number : channels * (number + 1), :] = block.astype(BF16)
        last = 8 - tap
        lanes = 2 * channels
        backward_ref[last, :channels, :lanes] = (plain[2] + moved[1]).astype(BF16)
        backward_ref[last, :channels, lanes:] = plain[0].astype(BF16)
        backward_ref[last, channels:, :lanes] = moved[2].astype(BF16)
        backward_ref[last, channels:, lanes:] = (plain[1] + moved[0]).astype(BF16)


def store_line(lines, number, line):
    lanes = lines.shape[1]
    each = line.shape[1] // lanes
    for k in range(each):
        lines[each * number + k : each * number + k + 1, :] = line[:, lanes * k : lanes * (k + 1)]


def load_line(rows, number, each):
    return jnp.concatenate([rows[each * number + k : each * number + k + 1] for k in range(each)], axis=1)


def kernel_grad_kernel(roles, tiles, channels, joined, f_ref, c_ref, *refs):
    roles = Roles(roles, tiles)
    counts = roles.counts
    x_refs = refs[: counts[0]]
    y_refs = refs[counts[0] : counts[0] + counts[1]]
    near = counts[0] + counts[1]
    keep_ref, send_ref = refs[near : near + 2]
    hops_at = near + 2 + (0 if joined else counts[0])
    line_refs = refs[near + 2 : hops_at]
    hop_refs = refs[hops_at : hops_at + counts[2]]
    wide, tall, packed, lines = refs[hops_at + counts[2] :]
    count = keep_ref.shape[0]
    bricks, edge, _, width = f_ref.shape
    rows = edge * edge
    wide[:, edge : edge + rows, :] = padded(f_ref[...].astype(F32).reshape(bricks, rows, width), channels)
    planes = []
    for side in range(2):
        start = side * (edge + rows)
        plane = jnp.zeros((bricks, edge, width), F32)
        for number, ref in enumerate(x_refs):
            plane = jnp.where(roles.side(0, number, side), ref[0].astype(F32), plane)
        planes.append(plane)
        plane = padded(plane, channels)
        for brick in range(bricks):
            wide[brick, start : start + edge, :] = plane[brick]
    own = c_ref[...].astype(F32)
    tall[:, :, edge : 2 * edge, :] = own
    tall[1, :, edge - 1 : edge, :] = own[0, :, edge - 1 :, :]
    tall[0, :, 2 * edge : 2 * edge + 1, :] = own[1, :, 0:1, :]
    halo = {}
    for side in range(2):
        for source in range(2):
            row = jnp.zeros((edge, width), F32)
            for number, ref in enumerate(y_refs):
                row = jnp.where(roles.side(1, number, side), ref[source].astype(F32), row)
            halo[source, side] = row
        at = 2 * edge if side else edge - 1
        tall[side, :, at : at + 1, :] = halo[1, side][:, None, :]
    lanes = 2 * channels
    pairs = width // lanes
    right = []
    for col in range(3):
        value = tall[:, :, edge + 1 - col : 2 * edge + 1 - col, :].reshape(bricks * rows, width).astype(BF16)
        right.append(jnp.concatenate([value[:, lanes * k : lanes * (k + 1)] for k in range(pairs)], axis=0))
    right = jnp.concatenate(right, axis=1)
    low = lax.broadcasted_iota(jnp.int32, (3 * channels // 2, lanes), 1) < channels
    half = 3 * channels // 2
    left = []
    for row in range(3):
        value = wide[:, edge * row : edge * row + rows, :].reshape(bricks * rows, -1).astype(BF16)
        left.append(jnp.concatenate([value[:, lanes * k : lanes * (k + 2)] for k in range(pairs)], axis=0))
    left = jnp.concatenate(left, axis=1)
    every = lax.dot_general(left, right, (((0,), (0,)), ((), ())), preferred_element_type=F32)
    for row in range(3):
        grad = every[2 * lanes * row : 2 * lanes * (row + 1)]
        for col in range(3):
            block = grad[:, lanes * col : lanes * (col + 1)]
            moved = pltpu.roll(block, channels, 1)
            first = block[:half] + moved[channels : channels + half]
            second = moved[half : 2 * half] + block[channels + half :]
            at = half * (3 * row + col)
            packed[at : at + half, :] = jnp.where(low, first, second)
    for number in range(counts[0]):
        up = roles.side(0, number, 1)
        for (source, side), row in halo.items():
            store_line(lines, 2 * source + side, jnp.where(up, row[edge - 1 : edge], row[0:1]))
        if joined:
            send_ref[count:, :] = lines[...]
        else:
            line_refs[number][...] = lines[...].astype(BF16)
    for number, out in enumerate(hop_refs):
        line = jnp.zeros((1, width), F32)
        for across in range(2):
            for side in range(2):
                at = (edge - 1) * side
                hit = roles.any(2, number, lambda role: role == (across, side))
                line = jnp.where(hit, planes[across][side, at : at + 1, :], line)
        store_line(lines, 0, line)
        out[...] = lines[...].astype(BF16)
    own = my_half()
    keep_ref[...] = packed[pl.ds(pl.multiple_of(own * count, 8), count), :]
    send_ref[:count, :] = packed[pl.ds(pl.multiple_of((1 - own) * count, 8), count), :]


def conv_kernel(roles, tiles, channels, source, ways, v_ref, *refs):
    roles = Roles(roles, tiles)
    counts = roles.counts
    x_refs = refs[: counts[0]]
    y_refs = refs[counts[0] : counts[0] + counts[1]]
    near = counts[0] + counts[1]
    hops_at = near + counts[0] * ways
    line_refs = refs[near:hops_at]
    hop_refs = refs[hops_at : hops_at + counts[2]]
    weight_ref, out_ref, ext = refs[hops_at + counts[2] :]
    bricks, edge, _, width = v_ref.shape
    rows = edge * edge
    first, last = edge, 2 * edge - 1
    ext[:, 1 : edge + 1, first : last + 1, :] = padded(v_ref[...].astype(F32), channels)
    for side in range(2):
        plane = jnp.zeros((bricks, edge, width), F32)
        for number, ref in enumerate(x_refs):
            plane = jnp.where(roles.side(0, number, side), ref[source].astype(F32), plane)
        plane = padded(plane, channels)
        for brick in range(bricks):
            ext[brick, side * (edge + 1), first : last + 1, :] = plane[brick]
    each = width // line_refs[0].shape[1]
    arrived = [ref[ref.shape[0] - 4 * each :, :].astype(F32) for ref in line_refs]
    if ways == 2:
        arrived = [jnp.where(my_half() == 1, *arrived)]
    hops = [load_line(ref[...].astype(F32), 0, each) for ref in hop_refs]
    for side in range(2):
        row = jnp.zeros((edge, width), F32)
        for number, ref in enumerate(y_refs):
            row = jnp.where(roles.side(1, number, side), ref[source].astype(F32), row)
        at = last + 1 if side else first - 1
        row = padded(row, channels)
        ext[side, 1 : edge + 1, at : at + 1, :] = row[:, None, :]
        for across in range(2):
            line = jnp.zeros((1, width), F32)
            for number, value in enumerate(arrived):
                line = jnp.where(roles.side(0, number, across), load_line(value, 2 * source + side, each), line)
            if source == 0:
                line = masked(roles.linked(side), line)
                for number, value in enumerate(hops):
                    line = jnp.where(roles.any(3, number, lambda role: role == (across, side)), value, line)
            ext[side, across * (edge + 1), at : at + 1, :] = padded(line, channels)
    ext[1, :, first - 1 : first, :] = ext[0, :, last : last + 1, :]
    ext[0, :, last + 1 : last + 2, :] = ext[1, :, first : first + 1, :]
    lanes = 2 * channels
    pairs = width // lanes
    total = jnp.zeros((pairs * bricks * rows, lanes), F32)
    contract = 0 if source == 0 else 1
    for col in range(3):
        for row in range(3):
            value = ext[:, row : row + edge, first - 1 + col : last + col, :]
            value = value.reshape(bricks * rows, -1).astype(BF16)
            left = jnp.concatenate([value[:, lanes * k : lanes * (k + 2)] for k in range(pairs)], axis=0)
            total = total + lax.dot_general(
                left, weight_ref[3 * row + col], (((1,), (contract,)), ((), ())), preferred_element_type=F32
            )
    for k in range(pairs):
        out_ref[:, lanes * k : lanes * (k + 1)] = total[bricks * rows * k : bricks * rows * (k + 1)].astype(BF16)


def unpack_kernel(factor, own_ref, other_ref, out_hbm, out_ref, sent):
    count = own_ref.shape[0]
    first_half = my_half() == 0
    taps, rows, channels = out_ref.shape
    half = rows // 2

    def packed(start, stop):
        pieces = []
        for low, ref, other in ((0, own_ref, other_ref), (count, other_ref, own_ref)):
            here = slice(max(start - low, 0), min(stop - low, count))
            if here.start < here.stop:
                pieces.append(jnp.where(first_half, ref[here], other[here]))
        return jnp.concatenate(pieces, axis=0) * factor

    copies = []
    for tap in range(taps):
        block = packed(half * tap, half * (tap + 1))
        out_ref[tap, :half, :] = block[:, :channels]
        out_ref[tap, half:, :] = pltpu.roll(block, channels, 1)[:, :channels]
        copies.append(pltpu.make_async_copy(out_ref.at[tap], out_hbm.at[tap], sent.at[tap]))
        copies[-1].start()
    for copy in copies:
        copy.wait()


VMEM = pl.BlockSpec(memory_space=pltpu.VMEM)
HBM = pl.BlockSpec(memory_space=pltpu.HBM)


def call(kernel, in_specs, out_shapes, scratch=(), flops=0, name=None, vmem=24 * 2**20, out=None):
    several = isinstance(out_shapes, list)
    return pl.pallas_call(
        kernel,
        in_specs=in_specs,
        out_specs=[VMEM] * len(out_shapes) if several else (out or VMEM),
        out_shape=out_shapes,
        scratch_shapes=list(scratch),
        compiler_params=pltpu.CompilerParams(vmem_limit_bytes=vmem),
        cost_estimate=pl.CostEstimate(flops=flops, bytes_accessed=2**20, transcendentals=0),
        name=name,
    )


def body(tiles, features, cotangent, kernel, neighbours):
    pairs, roles, meetings = make_plan(tiles)
    counts = [len(kind) for kind in pairs]
    bricks, edge = features.shape[1:3]
    width = features.shape[-1]
    channels = kernel.shape[-1]
    rows = edge * edge
    lanes = 2 * channels
    shape = jax.ShapeDtypeStruct
    f = features.reshape(bricks, edge, edge, width)
    c = cotangent.reshape(bricks, edge, edge, width)
    links = neighbours.reshape(bricks, 6)

    near = counts[0] + counts[1]
    *faces, flags = call(
        functools.partial(x_faces_kernel, roles, tiles),
        [HBM, HBM, HBM],
        [pltpu.VMEM((2, bricks, edge, width), BF16)] * counts[0] + [pltpu.VMEM((16, width), F32)],
        [pltpu.SMEM(links.shape, jnp.int32), pltpu.SemaphoreType.DMA((4 * counts[0] + 1,))],
        name="x_faces",
        vmem=None,
    )(f, c, links)
    got = [lax.ppermute(x, ("space", "dp"), one) for x, one in zip(faces, pairs[0])]
    faces = call(
        functools.partial(y_faces_kernel, roles, tiles),
        [VMEM] * 3,
        [pltpu.VMEM((2, edge, width), BF16)] * counts[1],
        name="y_faces",
    )(f, c, flags)
    got += [lax.ppermute(x, ("space", "dp"), one) for x, one in zip(faces, pairs[1])]
    bits = [1 << number for number in range(tiles.bit_length() - 1)]
    orders = [bits, bits]
    wire = BF16 if len(bits) <= 3 else F32
    shared = [bit for bit in bits if meetings == [[(i, i ^ bit) for i in range(tiles)]]]
    joined = bool(shared) and len(bits) == 3
    if joined:
        first, last = (bit for bit in bits if bit not in shared)
        orders = [[first] + shared + [last], shared + [last, first]]
    count = 27 * channels * channels // lanes // 2
    line_rows = 4 * width // lanes
    keep, send, *lines = call(
        functools.partial(kernel_grad_kernel, roles, tiles, channels, joined),
        [VMEM, VMEM] + [VMEM] * near,
        [shape((count, lanes), F32), shape((count + line_rows * joined, lanes), F32)]
        + [shape((line_rows, lanes), BF16)] * (counts[2] if joined else counts[0] + counts[2]),
        [
            pltpu.VMEM((bricks, rows + 2 * edge, width + lanes), F32),
            pltpu.VMEM((bricks, edge, 3 * edge, width), F32),
            pltpu.VMEM((2 * count, lanes), F32),
            pltpu.VMEM((line_rows, lanes), F32),
        ],
        flops=2 * 768 * 384 * 512,
        name="kernel_grad",
    )(f, c, *got)

    forward, backward = call(
        weights_kernel,
        [VMEM],
        [shape((9, 4 * channels, lanes), BF16), shape((9, lanes, 4 * channels), BF16)],
        [pltpu.VMEM((27, channels, lanes), F32)],
        name="weights",
    )(kernel.reshape(27, channels, channels))

    def conv(source, x, weight):
        return call(
            functools.partial(conv_kernel, roles, tiles, channels, source, ready),
            [VMEM] * (2 + len(got)),
            shape((bricks * rows, width), BF16),
            [pltpu.VMEM((bricks, edge + 2, 3 * edge, width + lanes), F32)],
            flops=2 * 512 * 256 * 128 * 9,
            name="response" if source == 0 else "feature_grad",
        )(x, *got, weight)

    cores = lax.axis_size("dp")
    swap = [(0, 1), (1, 0)]
    summed = lax.ppermute(send, "dp", swap)
    part = keep + summed[:count]
    if not joined:
        got += [lax.ppermute(x, ("space", "dp"), one) for x, one in zip(lines, pairs[0])]
        lines = lines[counts[0] :]
    hops = [lax.ppermute(x, ("space", "dp"), one) for x, one in zip(lines, pairs[2])]
    ready = 2 if joined else 1
    for number in range(len(bits)):
        step = [
            tuple(end * cores + half_of(end, half) for end in (tile, tile ^ order[number]))
            for tile in range(tiles)
            for half, order in enumerate(orders)
        ]
        mine = part.astype(wire)
        carries = joined and number < ready
        if carries:
            mine = jnp.concatenate([mine, summed[count:].astype(wire)], axis=0)
        if number == 1:
            mine, hops, forward, backward = lax.optimization_barrier((mine, hops, forward, backward))
        else:
            mine = lax.optimization_barrier(mine)
        if number == ready:
            got += hops
            response = conv(0, f, forward)
            feature_grad = conv(1, c, backward)
        theirs = lax.ppermute(mine, ("space", "dp"), step)
        if carries:
            got.append(theirs)
            mine, theirs = mine[:count], theirs[:count]
        part = mine.astype(F32) + theirs.astype(F32)
    part, response = lax.optimization_barrier((part, response))
    other = lax.ppermute(part, "dp", swap)
    other, feature_grad = lax.optimization_barrier((other, feature_grad))
    response, feature_grad = (x.reshape(features.shape) for x in (response, feature_grad))
    cells = bricks * tiles * lax.axis_size("dp") * edge**3
    kernel_grad = call(
        functools.partial(unpack_kernel, 1.0 / math.sqrt(cells)),
        [VMEM, VMEM],
        shape((9, 3 * channels, channels), F32),
        [pltpu.VMEM((9, 3 * channels, channels), F32), pltpu.SemaphoreType.DMA((9,))],
        name="unpack",
        out=HBM,
    )(part, other).reshape(kernel.shape)
    return response, feature_grad, kernel_grad


def solution(mesh):
    bricks_spec = P(("groups", "dp"), "space", None, None, None)
    return jax.shard_map(
        functools.partial(body, mesh.shape["space"]),
        mesh=mesh,
        in_specs=(bricks_spec, bricks_spec, P(), P(("groups", "dp"), "space", None)),
        out_specs=(bricks_spec, bricks_spec, P("groups", None, None, None, None)),
        check_vma=False,
    )
```

```python
import functools
import math

import jax
import jax.numpy as jnp
from jax import lax
from jax.experimental import pallas as pl
from jax.experimental.pallas import tpu as pltpu
from jax.sharding import PartitionSpec as P

TILES_Y = 4
F32 = jnp.float32
BF16 = jnp.bfloat16


def step_y(tile, sign, tiles):
    column = (tile + TILES_Y // 2) % TILES_Y + sign
    near = tile + sign
    return near if 0 <= column < TILES_Y and 0 <= near < tiles else None


def step_x(tile, sign, tiles):
    near = tile + sign * TILES_Y
    return near if 0 <= near < tiles else None


def rounds(edges):
    found = []
    for low, high in edges:
        for one in found:
            if low not in one and high not in one:
                break
        else:
            one = {}
            found.append(one)
        one[low] = (high, 1)
        one[high] = (low, 0)
    return found


def detours(tiles):
    found = []
    for tile in range(tiles):
        for across in range(2):
            for along in range(2):
                sender = step_y(tile, 2 * along - 1, tiles)
                if sender is None or step_x(sender, 2 * across - 1, tiles) is None:
                    continue
                if step_x(tile, 2 * across - 1, tiles) is not None:
                    continue
                for one in found:
                    if all(hop[0] != sender and hop[1] != tile for hop in one):
                        break
                else:
                    one = []
                    found.append(one)
                one.append((sender, tile, across, along))
    return found


def completed(pairs, tiles):
    idle = [tile for tile in range(tiles) if all(tile != a for a, _ in pairs) and all(tile != b for _, b in pairs)]
    active = [(2 * a + core, 2 * b + core) for a, b in pairs for core in range(2)]
    return sorted(active + [(2 * tile + core, 2 * tile + 1 - core) for tile in idle for core in range(2)])


def make_plan(tiles):
    def edges(step):
        return [(tile, step(tile, 1, tiles)) for tile in range(tiles) if step(tile, 1, tiles) is not None]

    along_x, along_y, hops = rounds(edges(step_x)), rounds(edges(step_y)), detours(tiles)
    pairs = [[[(tile, one[tile][0]) for tile in sorted(one)] for one in kind] for kind in (along_x, along_y)]
    pairs.append([[hop[:2] for hop in one] for one in hops])
    meetings = pairs[0]
    pairs = [[completed(one, tiles) for one in kind] for kind in pairs]
    roles = [[{tile: one[tile][1] for tile in one} for one in kind] for kind in (along_x, along_y)]
    roles.append([{hop[0]: (hop[2], 1 - hop[3]) for hop in one} for one in hops])
    roles.append([{hop[1]: hop[2:] for hop in one} for one in hops])
    return pairs, roles, meetings


class Roles:
    def __init__(self, roles, tiles):
        self.roles, self.tiles = roles, tiles
        self.counts = [len(kind) for kind in roles[:3]]
        self.tile = lax.axis_index("space")

    def any(self, kind, number, test):
        words = []
        for start in range(0, self.tiles, 32):
            here = [t for t in range(start, min(start + 32, self.tiles)) if t in self.roles[kind][number]]
            word = sum(1 << (t - start) for t in here if test(self.roles[kind][number][t]))
            words.append(word - (1 << 32) if word >> 31 else word)
        word = jnp.int32(words[0])
        for number, other in enumerate(words[1:], 1):
            word = jnp.where(self.tile // 32 == number, jnp.int32(other), word)
        return (lax.shift_right_logical(word, self.tile % 32) & 1) == 1

    def side(self, kind, number, side):
        return self.any(kind, number, lambda role: role == side)

    def linked(self, side):
        found = jnp.bool_(False)
        for number in range(self.counts[1]):
            found = found | self.side(1, number, side)
        return found


def half_of(tile, core):
    for shift in (16, 8, 4, 2, 1):
        tile = tile ^ (tile >> shift)
    return core ^ (tile & 1)


def my_half():
    return half_of(lax.axis_index("space"), lax.axis_index("dp"))


def masked(keep, x):
    return jnp.where(keep, x, jnp.zeros_like(x))


def x_faces_kernel(roles, tiles, f_hbm, c_hbm, link_hbm, *refs):
    roles = Roles(roles, tiles)
    *x_refs, f_ref, c_ref, flag_ref, link_ref, arrived = refs
    edge = f_hbm.shape[1]
    copies = [
        pltpu.make_async_copy(source, target, arrived.at[number])
        for number, (source, target) in enumerate(((link_hbm, link_ref), (f_hbm, f_ref), (c_hbm, c_ref)))
    ]
    for number, out in enumerate(x_refs):
        plane = jnp.where(roles.side(0, number, 1), edge - 1, 0)
        for source, ref in enumerate((f_hbm, c_hbm)):
            for brick in range(2):
                at = arrived.at[len(copies)]
                copies.append(pltpu.make_async_copy(ref.at[brick, plane], out.at[source, brick], at))
    for copy in copies:
        copy.start()
    for copy in copies:
        copy.wait()
    linked = [[link_ref[brick, way] >= 0 for way in range(4)] for brick in range(2)]
    for number, out in enumerate(x_refs):
        up = roles.side(0, number, 1)
        for brick in range(2):

            @pl.when(jnp.logical_not(jnp.where(up, linked[brick][1], linked[brick][0])))
            def _():
                out[:, brick] = jnp.zeros_like(out[:, brick])

    for row, flag in enumerate((linked[0][2], linked[1][3])):
        flag_ref[8 * row : 8 * row + 8, :] = jnp.full((8, flag_ref.shape[1]), jnp.where(flag, 1.0, 0.0), F32)


def y_faces_kernel(roles, tiles, f_ref, c_ref, flag_ref, *y_refs):
    roles = Roles(roles, tiles)
    edge = f_ref.shape[1]
    rows = []
    for ref in (f_ref, c_ref):
        low = ref[0].astype(F32)[:, 0, :] * flag_ref[:8]
        high = ref[1].astype(F32)[:, edge - 1, :] * flag_ref[8:]
        rows.append((low, high))
    for number, out in enumerate(y_refs):
        up = roles.side(1, number, 1)
        for source, (low, high) in enumerate(rows):
            out[source] = jnp.where(up, high, low).astype(BF16)


def padded(x, channels):
    zeros = jnp.zeros(x.shape[:-1] + (2 * channels,), F32)
    return pltpu.roll(jnp.concatenate([x, zeros], axis=-1), channels, x.ndim - 1)


def weights_kernel(kernel_ref, forward_ref, backward_ref, wide):
    channels = kernel_ref.shape[-1]
    wide[...] = jnp.zeros_like(wide)
    wide[:, :, :channels] = kernel_ref[...].astype(F32)
    for tap in range(9):
        plain = [wide[3 * tap + d] for d in range(3)]
        moved = [pltpu.roll(x, channels, 1) for x in plain]
        steps = (plain[0], plain[1] + moved[0], plain[2] + moved[1], moved[2])
        for number, block in enumerate(steps):
            forward_ref[tap, channels * number : channels * (number + 1), :] = block.astype(BF16)
        last = 8 - tap
        lanes = 2 * channels
        backward_ref[last, :channels, :lanes] = (plain[2] + moved[1]).astype(BF16)
        backward_ref[last, :channels, lanes:] = plain[0].astype(BF16)
        backward_ref[last, channels:, :lanes] = moved[2].astype(BF16)
        backward_ref[last, channels:, lanes:] = (plain[1] + moved[0]).astype(BF16)


def store_line(lines, number, line):
    lanes = lines.shape[1]
    each = line.shape[1] // lanes
    for k in range(each):
        lines[each * number + k : each * number + k + 1, :] = line[:, lanes * k : lanes * (k + 1)]


def load_line(rows, number, each):
    return jnp.concatenate([rows[each * number + k : each * number + k + 1] for k in range(each)], axis=1)


def stacked(rows, lanes, wide):
    steps = range((rows.shape[1] - wide) // lanes + 1)
    return jnp.concatenate([rows[:, lanes * k : lanes * k + wide] for k in steps], axis=0).astype(BF16)


def outer(left, right):
    return lax.dot_general(left, right, (((0,), (0,)), ((), ())), preferred_element_type=F32)


def local_grad_kernel(channels, f_ref, c_ref, out_ref, wide, tall):
    bricks, edge, _, width = f_ref.shape
    rows = edge * edge
    lanes = 2 * channels
    wide[:, :edge, :] = jnp.zeros_like(wide[:, :edge, :])
    wide[:, edge + rows :, :] = jnp.zeros_like(wide[:, edge + rows :, :])
    wide[:, edge : edge + rows, :] = padded(f_ref[...].astype(F32).reshape(bricks, rows, width), channels)
    own = c_ref[...].astype(F32)
    none = jnp.zeros((edge, 1, width), F32)
    tall[:, :, edge : 2 * edge, :] = own
    tall[0, :, edge - 1 : edge, :] = none
    tall[1, :, edge - 1 : edge, :] = own[0, :, edge - 1 :, :]
    tall[0, :, 2 * edge : 2 * edge + 1, :] = own[1, :, 0:1, :]
    tall[1, :, 2 * edge : 2 * edge + 1, :] = none
    left, right = [], []
    for tap in range(3):
        value = wide[:, edge * tap : edge * tap + rows, :].reshape(bricks * rows, -1)
        left.append(stacked(value, lanes, 2 * lanes))
        value = tall[:, :, edge + 1 - tap : 2 * edge + 1 - tap, :].reshape(bricks * rows, width)
        right.append(stacked(value, lanes, lanes))
    out_ref[...] = outer(jnp.concatenate(left, axis=1), jnp.concatenate(right, axis=1))


def kernel_grad_kernel(roles, tiles, channels, joined, f_ref, c_ref, local_ref, *refs):
    roles = Roles(roles, tiles)
    counts = roles.counts
    x_refs = refs[: counts[0]]
    near = counts[0] + counts[1]
    y_refs = refs[counts[0] : near]
    keep_ref, send_ref = refs[near : near + 2]
    hops_at = near + 2 + (0 if joined else counts[0])
    line_refs = refs[near + 2 : hops_at]
    hop_refs = refs[hops_at : hops_at + counts[2]]
    tall, row_ref, packed, lines = refs[hops_at + counts[2] :]
    count = keep_ref.shape[0]
    bricks, edge, _, width = f_ref.shape
    lanes = 2 * channels
    planes = []
    for side in range(2):
        plane = jnp.zeros((bricks, edge, width), F32)
        for number, ref in enumerate(x_refs):
            plane = jnp.where(roles.side(0, number, side), ref[0].astype(F32), plane)
        planes.append(plane)
    halo = {}
    for side in range(2):
        for source in range(2):
            row = jnp.zeros((edge, width), F32)
            for number, ref in enumerate(y_refs):
                row = jnp.where(roles.side(1, number, side), ref[source].astype(F32), row)
            halo[source, side] = row
    across = []
    for side, plane in enumerate(planes):
        at = (edge - 1) * side
        own = [c_ref[brick, at].astype(F32) for brick in range(bricks)]
        below = (halo[1, 0][at : at + 1], own[0][edge - 1 :])
        above = (own[1][0:1], halo[1, 1][at : at + 1])
        for brick in range(bricks):
            tall[brick, edge : 2 * edge, :] = own[brick]
            tall[brick, edge - 1 : edge, :] = below[brick]
            tall[brick, 2 * edge : 2 * edge + 1, :] = above[brick]
        left = stacked(padded(plane, channels).reshape(bricks * edge, -1), lanes, 2 * lanes)
        right = []
        for tap in range(3):
            value = tall[:, edge + 1 - tap : 2 * edge + 1 - tap, :].reshape(bricks * edge, width)
            right.append(stacked(value, lanes, lanes))
        across.append(outer(left, jnp.concatenate(right, axis=1)))
    along = []
    row_ref[...] = jnp.zeros_like(row_ref)
    for side in range(2):
        row_ref[edge : 2 * edge, :] = padded(f_ref[side].astype(F32)[:, (edge - 1) * side, :], channels)
        left = [stacked(row_ref[edge - 1 + tap : 2 * edge - 1 + tap, :], lanes, 2 * lanes) for tap in range(3)]
        along.append(outer(jnp.concatenate(left, axis=1), stacked(halo[1, side], lanes, lanes)))
    half = 3 * channels // 2
    low = lax.broadcasted_iota(jnp.int32, (half, lanes), 1) < channels
    for row in range(3):
        for col in range(3):
            block = local_ref[2 * lanes * row : 2 * lanes * (row + 1), lanes * col : lanes * (col + 1)]
            if row != 1:
                block = block + across[row // 2][:, lanes * col : lanes * (col + 1)]
            if col != 1:
                block = block + along[1 - col // 2][2 * lanes * row : 2 * lanes * (row + 1)]
            moved = pltpu.roll(block, channels, 1)
            first = block[:half] + moved[channels : channels + half]
            second = moved[half : 2 * half] + block[channels + half :]
            at = half * (3 * row + col)
            packed[at : at + half, :] = jnp.where(low, first, second)
    for number in range(counts[0]):
        up = roles.side(0, number, 1)
        for (source, side), row in halo.items():
            store_line(lines, 2 * source + side, jnp.where(up, row[edge - 1 : edge], row[0:1]))
        if joined:
            send_ref[count:, :] = lines[...]
        else:
            line_refs[number][...] = lines[...].astype(BF16)
    for number, out in enumerate(hop_refs):
        line = jnp.zeros((1, width), F32)
        for across in range(2):
            for side in range(2):
                at = (edge - 1) * side
                hit = roles.any(2, number, lambda role: role == (across, side))
                line = jnp.where(hit, planes[across][side, at : at + 1, :], line)
        store_line(lines, 0, line)
        out[...] = lines[...].astype(BF16)
    own = my_half()
    keep_ref[...] = packed[pl.ds(pl.multiple_of(own * count, 8), count), :]
    send_ref[:count, :] = packed[pl.ds(pl.multiple_of((1 - own) * count, 8), count), :]


def conv_kernel(roles, tiles, channels, source, ways, v_ref, *refs):
    roles = Roles(roles, tiles)
    counts = roles.counts
    x_refs = refs[: counts[0]]
    y_refs = refs[counts[0] : counts[0] + counts[1]]
    near = counts[0] + counts[1]
    hops_at = near + counts[0] * ways
    line_refs = refs[near:hops_at]
    hop_refs = refs[hops_at : hops_at + counts[2]]
    weight_ref, out_ref, ext = refs[hops_at + counts[2] :]
    bricks, edge, _, width = v_ref.shape
    rows = edge * edge
    first, last = edge, 2 * edge - 1
    ext[:, 1 : edge + 1, first : last + 1, :] = padded(v_ref[...].astype(F32), channels)
    for side in range(2):
        plane = jnp.zeros((bricks, edge, width), F32)
        for number, ref in enumerate(x_refs):
            plane = jnp.where(roles.side(0, number, side), ref[source].astype(F32), plane)
        plane = padded(plane, channels)
        for brick in range(bricks):
            ext[brick, side * (edge + 1), first : last + 1, :] = plane[brick]
    each = width // line_refs[0].shape[1]
    arrived = [ref[ref.shape[0] - 4 * each :, :].astype(F32) for ref in line_refs]
    if ways == 2:
        arrived = [jnp.where(my_half() == 1, *arrived)]
    hops = [load_line(ref[...].astype(F32), 0, each) for ref in hop_refs]
    for side in range(2):
        row = jnp.zeros((edge, width), F32)
        for number, ref in enumerate(y_refs):
            row = jnp.where(roles.side(1, number, side), ref[source].astype(F32), row)
        at = last + 1 if side else first - 1
        row = padded(row, channels)
        ext[side, 1 : edge + 1, at : at + 1, :] = row[:, None, :]
        for across in range(2):
            line = jnp.zeros((1, width), F32)
            for number, value in enumerate(arrived):
                line = jnp.where(roles.side(0, number, across), load_line(value, 2 * source + side, each), line)
            if source == 0:
                line = masked(roles.linked(side), line)
                for number, value in enumerate(hops):
                    line = jnp.where(roles.any(3, number, lambda role: role == (across, side)), value, line)
            ext[side, across * (edge + 1), at : at + 1, :] = padded(line, channels)
    ext[1, :, first - 1 : first, :] = ext[0, :, last : last + 1, :]
    ext[0, :, last + 1 : last + 2, :] = ext[1, :, first : first + 1, :]
    lanes = 2 * channels
    pairs = width // lanes
    total = jnp.zeros((pairs * bricks * rows, lanes), F32)
    contract = 0 if source == 0 else 1
    for col in range(3):
        for row in range(3):
            value = ext[:, row : row + edge, first - 1 + col : last + col, :]
            value = value.reshape(bricks * rows, -1).astype(BF16)
            left = jnp.concatenate([value[:, lanes * k : lanes * (k + 2)] for k in range(pairs)], axis=0)
            total = total + lax.dot_general(
                left, weight_ref[3 * row + col], (((1,), (contract,)), ((), ())), preferred_element_type=F32
            )
    for k in range(pairs):
        out_ref[:, lanes * k : lanes * (k + 1)] = total[bricks * rows * k : bricks * rows * (k + 1)].astype(BF16)


def unpack_kernel(factor, own_ref, other_ref, out_hbm, out_ref, sent):
    count = own_ref.shape[0]
    first_half = my_half() == 0
    taps, rows, channels = out_ref.shape
    half = rows // 2

    def packed(start, stop):
        pieces = []
        for low, ref, other in ((0, own_ref, other_ref), (count, other_ref, own_ref)):
            here = slice(max(start - low, 0), min(stop - low, count))
            if here.start < here.stop:
                pieces.append(jnp.where(first_half, ref[here], other[here]))
        return jnp.concatenate(pieces, axis=0) * factor

    copies = []
    for tap in range(taps):
        block = packed(half * tap, half * (tap + 1))
        out_ref[tap, :half, :] = block[:, :channels]
        out_ref[tap, half:, :] = pltpu.roll(block, channels, 1)[:, :channels]
        copies.append(pltpu.make_async_copy(out_ref.at[tap], out_hbm.at[tap], sent.at[tap]))
        copies[-1].start()
    for copy in copies:
        copy.wait()


VMEM = pl.BlockSpec(memory_space=pltpu.VMEM)
HBM = pl.BlockSpec(memory_space=pltpu.HBM)


def call(kernel, in_specs, out_shapes, scratch=(), flops=0, name=None, vmem=24 * 2**20, out=None):
    several = isinstance(out_shapes, list)
    return pl.pallas_call(
        kernel,
        in_specs=in_specs,
        out_specs=[VMEM] * len(out_shapes) if several else (out or VMEM),
        out_shape=out_shapes,
        scratch_shapes=list(scratch),
        compiler_params=pltpu.CompilerParams(vmem_limit_bytes=vmem),
        cost_estimate=pl.CostEstimate(flops=flops, bytes_accessed=2**20, transcendentals=0),
        name=name,
    )


def body(tiles, features, cotangent, kernel, neighbours):
    pairs, roles, meetings = make_plan(tiles)
    counts = [len(kind) for kind in pairs]
    bricks, edge = features.shape[1:3]
    width = features.shape[-1]
    channels = kernel.shape[-1]
    rows = edge * edge
    lanes = 2 * channels
    shape = jax.ShapeDtypeStruct
    f = features.reshape(bricks, edge, edge, width)
    c = cotangent.reshape(bricks, edge, edge, width)
    links = neighbours.reshape(bricks, 6)

    near = counts[0] + counts[1]
    *faces, f, c, flags = call(
        functools.partial(x_faces_kernel, roles, tiles),
        [HBM, HBM, HBM],
        [pltpu.VMEM((2, bricks, edge, width), BF16)] * counts[0]
        + [pltpu.VMEM(f.shape, BF16), pltpu.VMEM(c.shape, BF16), pltpu.VMEM((16, width), F32)],
        [pltpu.SMEM(links.shape, jnp.int32), pltpu.SemaphoreType.DMA((4 * counts[0] + 3,))],
        name="x_faces",
        vmem=None,
    )(f, c, links)
    got = [lax.ppermute(x, ("space", "dp"), one) for x, one in zip(faces, pairs[0])]
    faces = call(
        functools.partial(y_faces_kernel, roles, tiles),
        [VMEM] * 3,
        [pltpu.VMEM((2, edge, width), BF16)] * counts[1],
        name="y_faces",
    )(f, c, flags)
    got += [lax.ppermute(x, ("space", "dp"), one) for x, one in zip(faces, pairs[1])]
    bits = [1 << number for number in range(tiles.bit_length() - 1)]
    orders = [bits, bits]
    wire = BF16 if len(bits) <= 3 else F32
    shared = [bit for bit in bits if meetings == [[(i, i ^ bit) for i in range(tiles)]]]
    joined = bool(shared) and len(bits) == 3
    if joined:
        first, last = (bit for bit in bits if bit not in shared)
        orders = [[first] + shared + [last], shared + [last, first]]
    count = 27 * channels * channels // lanes // 2
    line_rows = 4 * width // lanes
    local = call(
        functools.partial(local_grad_kernel, channels),
        [VMEM, VMEM],
        pltpu.VMEM((6 * lanes, 3 * lanes), F32),
        [
            pltpu.VMEM((bricks, rows + 2 * edge, width + lanes), F32),
            pltpu.VMEM((bricks, edge, 3 * edge, width), F32),
        ],
        flops=2 * 768 * 384 * 512,
        name="local_grad",
    )(f, c)
    keep, send, *lines = call(
        functools.partial(kernel_grad_kernel, roles, tiles, channels, joined),
        [VMEM] * (3 + near),
        [shape((count, lanes), F32), shape((count + line_rows * joined, lanes), F32)]
        + [shape((line_rows, lanes), BF16)] * (counts[2] if joined else counts[0] + counts[2]),
        [
            pltpu.VMEM((bricks, 3 * edge, width), F32),
            pltpu.VMEM((3 * edge, width + lanes), F32),
            pltpu.VMEM((2 * count, lanes), F32),
            pltpu.VMEM((line_rows, lanes), F32),
        ],
        flops=2 * 768 * 384 * 64,
        name="kernel_grad",
    )(f, c, local, *got)

    forward, backward = call(
        weights_kernel,
        [VMEM],
        [shape((9, 4 * channels, lanes), BF16), shape((9, lanes, 4 * channels), BF16)],
        [pltpu.VMEM((27, channels, lanes), F32)],
        name="weights",
    )(kernel.reshape(27, channels, channels))

    def conv(source, x, weight):
        return call(
            functools.partial(conv_kernel, roles, tiles, channels, source, ready),
            [VMEM] * (2 + len(got)),
            shape((bricks * rows, width), BF16),
            [pltpu.VMEM((bricks, edge + 2, 3 * edge, width + lanes), F32)],
            flops=2 * 512 * 256 * 128 * 9,
            name="response" if source == 0 else "feature_grad",
        )(x, *got, weight)

    cores = lax.axis_size("dp")
    swap = [(0, 1), (1, 0)]
    summed = lax.ppermute(send, "dp", swap)
    part = keep + summed[:count]
    if not joined:
        got += [lax.ppermute(x, ("space", "dp"), one) for x, one in zip(lines, pairs[0])]
        lines = lines[counts[0] :]
    hops = [lax.ppermute(x, ("space", "dp"), one) for x, one in zip(lines, pairs[2])]
    ready = 2 if joined else 1
    for number in range(len(bits)):
        step = [
            tuple(end * cores + half_of(end, half) for end in (tile, tile ^ order[number]))
            for tile in range(tiles)
            for half, order in enumerate(orders)
        ]
        mine = part.astype(wire)
        carries = joined and number < ready
        if carries:
            mine = jnp.concatenate([mine, summed[count:].astype(wire)], axis=0)
        if number == ready:
            mine, hops, forward, backward = lax.optimization_barrier((mine, hops, forward, backward))
        else:
            mine = lax.optimization_barrier(mine)
        if number == ready:
            got += hops
            response = conv(0, f, forward)
            feature_grad = conv(1, c, backward)
        theirs = lax.ppermute(mine, ("space", "dp"), step)
        if carries:
            got.append(theirs)
            mine, theirs = mine[:count], theirs[:count]
        part = mine.astype(F32) + theirs.astype(F32)
    part, response = lax.optimization_barrier((part, response))
    other = lax.ppermute(part, "dp", swap)
    other, feature_grad = lax.optimization_barrier((other, feature_grad))
    response, feature_grad = (x.reshape(features.shape) for x in (response, feature_grad))
    cells = bricks * tiles * lax.axis_size("dp") * edge**3
    kernel_grad = call(
        functools.partial(unpack_kernel, 1.0 / math.sqrt(cells)),
        [VMEM, VMEM],
        shape((9, 3 * channels, channels), F32),
        [pltpu.VMEM((9, 3 * channels, channels), F32), pltpu.SemaphoreType.DMA((9,))],
        name="unpack",
        out=HBM,
    )(part, other).reshape(kernel.shape)
    return response, feature_grad, kernel_grad


def solution(mesh):
    bricks_spec = P(("groups", "dp"), "space", None, None, None)
    return jax.shard_map(
        functools.partial(body, mesh.shape["space"]),
        mesh=mesh,
        in_specs=(bricks_spec, bricks_spec, P(), P(("groups", "dp"), "space", None)),
        out_specs=(bricks_spec, bricks_spec, P("groups", None, None, None, None)),
        check_vma=False,
    )
```

```python
import functools
import math

import jax
import jax.numpy as jnp
from jax import lax
from jax.experimental import pallas as pl
from jax.experimental.pallas import tpu as pltpu
from jax.sharding import PartitionSpec as P

TILES_Y = 4
F32 = jnp.float32
BF16 = jnp.bfloat16


def step_y(tile, sign, tiles):
    column = (tile + TILES_Y // 2) % TILES_Y + sign
    near = tile + sign
    return near if 0 <= column < TILES_Y and 0 <= near < tiles else None


def step_x(tile, sign, tiles):
    near = tile + sign * TILES_Y
    return near if 0 <= near < tiles else None


def rounds(edges):
    found = []
    for low, high in edges:
        for one in found:
            if low not in one and high not in one:
                break
        else:
            one = {}
            found.append(one)
        one[low] = (high, 1)
        one[high] = (low, 0)
    return found


def detours(tiles):
    found = []
    for tile in range(tiles):
        for across in range(2):
            for along in range(2):
                sender = step_y(tile, 2 * along - 1, tiles)
                if sender is None or step_x(sender, 2 * across - 1, tiles) is None:
                    continue
                if step_x(tile, 2 * across - 1, tiles) is not None:
                    continue
                for one in found:
                    if all(hop[0] != sender and hop[1] != tile for hop in one):
                        break
                else:
                    one = []
                    found.append(one)
                one.append((sender, tile, across, along))
    return found


def completed(pairs, tiles):
    idle = [tile for tile in range(tiles) if all(tile != a for a, _ in pairs) and all(tile != b for _, b in pairs)]
    active = [(2 * a + core, 2 * b + core) for a, b in pairs for core in range(2)]
    return sorted(active + [(2 * tile + core, 2 * tile + 1 - core) for tile in idle for core in range(2)])


def make_plan(tiles):
    def edges(step):
        return [(tile, step(tile, 1, tiles)) for tile in range(tiles) if step(tile, 1, tiles) is not None]

    along_x, along_y, hops = rounds(edges(step_x)), rounds(edges(step_y)), detours(tiles)
    pairs = [[[(tile, one[tile][0]) for tile in sorted(one)] for one in kind] for kind in (along_x, along_y)]
    pairs.append([[hop[:2] for hop in one] for one in hops])
    meetings = pairs[0]
    pairs = [[completed(one, tiles) for one in kind] for kind in pairs]
    roles = [[{tile: one[tile][1] for tile in one} for one in kind] for kind in (along_x, along_y)]
    roles.append([{hop[0]: (hop[2], 1 - hop[3]) for hop in one} for one in hops])
    roles.append([{hop[1]: hop[2:] for hop in one} for one in hops])
    return pairs, roles, meetings


class Roles:
    def __init__(self, roles, tiles):
        self.roles, self.tiles = roles, tiles
        self.counts = [len(kind) for kind in roles[:3]]
        self.tile = lax.axis_index("space")

    def any(self, kind, number, test):
        words = []
        for start in range(0, self.tiles, 32):
            here = [t for t in range(start, min(start + 32, self.tiles)) if t in self.roles[kind][number]]
            word = sum(1 << (t - start) for t in here if test(self.roles[kind][number][t]))
            words.append(word - (1 << 32) if word >> 31 else word)
        word = jnp.int32(words[0])
        for number, other in enumerate(words[1:], 1):
            word = jnp.where(self.tile // 32 == number, jnp.int32(other), word)
        return (lax.shift_right_logical(word, self.tile % 32) & 1) == 1

    def side(self, kind, number, side):
        return self.any(kind, number, lambda role: role == side)

    def linked(self, side):
        found = jnp.bool_(False)
        for number in range(self.counts[1]):
            found = found | self.side(1, number, side)
        return found


def half_of(tile, core):
    for shift in (16, 8, 4, 2, 1):
        tile = tile ^ (tile >> shift)
    return core ^ (tile & 1)


def my_half():
    return half_of(lax.axis_index("space"), lax.axis_index("dp"))


def masked(keep, x):
    return jnp.where(keep, x, jnp.zeros_like(x))


def faces_kernel(roles, tiles, f_hbm, c_hbm, link_hbm, *refs):
    roles = Roles(roles, tiles)
    *out_refs, f_ref, c_ref, link_ref, arrived = refs
    x_refs, y_refs = out_refs[: roles.counts[0]], out_refs[roles.counts[0] :]
    edge = f_hbm.shape[1]
    copies = [
        pltpu.make_async_copy(source, target, arrived.at[number])
        for number, (source, target) in enumerate(((link_hbm, link_ref), (f_hbm, f_ref), (c_hbm, c_ref)))
    ]
    for copy in copies:
        copy.start()
    for copy in copies:
        copy.wait()
    linked = [[link_ref[brick, way] >= 0 for way in range(4)] for brick in range(2)]
    for number, out in enumerate(x_refs):
        up = roles.side(0, number, 1)
        plane = jnp.where(up, edge - 1, 0)
        for brick in range(2):
            keep = jnp.where(up, linked[brick][1], linked[brick][0])
            for source, ref in enumerate((f_ref, c_ref)):
                out[source, brick] = masked(keep, ref[brick, plane])

    rows = []
    for ref in (f_ref, c_ref):
        low = masked(linked[0][2], ref[0].astype(F32)[:, 0, :])
        high = masked(linked[1][3], ref[1].astype(F32)[:, edge - 1, :])
        rows.append((low, high))
    for number, out in enumerate(y_refs):
        up = roles.side(1, number, 1)
        for source, (low, high) in enumerate(rows):
            out[source] = jnp.where(up, high, low).astype(BF16)


def padded(x, channels):
    zeros = jnp.zeros(x.shape[:-1] + (2 * channels,), F32)
    return pltpu.roll(jnp.concatenate([x, zeros], axis=-1), channels, x.ndim - 1)


def weights_kernel(kernel_ref, forward_ref, backward_ref, wide):
    channels = kernel_ref.shape[-1]
    wide[...] = jnp.zeros_like(wide)
    wide[:, :, :channels] = kernel_ref[...].astype(F32)
    for tap in range(9):
        plain = [wide[3 * tap + d] for d in range(3)]
        moved = [pltpu.roll(x, channels, 1) for x in plain]
        steps = (plain[0], plain[1] + moved[0], plain[2] + moved[1], moved[2])
        for number, block in enumerate(steps):
            forward_ref[tap, channels * number : channels * (number + 1), :] = block.astype(BF16)
        last = 8 - tap
        lanes = 2 * channels
        backward_ref[last, :channels, :lanes] = (plain[2] + moved[1]).astype(BF16)
        backward_ref[last, :channels, lanes:] = plain[0].astype(BF16)
        backward_ref[last, channels:, :lanes] = moved[2].astype(BF16)
        backward_ref[last, channels:, lanes:] = (plain[1] + moved[0]).astype(BF16)


def store_line(lines, number, line):
    lanes = lines.shape[1]
    each = line.shape[1] // lanes
    for k in range(each):
        lines[each * number + k : each * number + k + 1, :] = line[:, lanes * k : lanes * (k + 1)]


def load_line(rows, number, each):
    return jnp.concatenate([rows[each * number + k : each * number + k + 1] for k in range(each)], axis=1)


def stacked(rows, lanes, wide):
    steps = range((rows.shape[1] - wide) // lanes + 1)
    return jnp.concatenate([rows[:, lanes * k : lanes * k + wide] for k in steps], axis=0).astype(BF16)


def outer(left, right):
    return lax.dot_general(left, right, (((0,), (0,)), ((), ())), preferred_element_type=F32)


def local_grad_kernel(channels, f_ref, c_ref, out_ref, wide, tall):
    bricks, edge, _, width = f_ref.shape
    rows = edge * edge
    lanes = 2 * channels
    wide[:, :edge, :] = jnp.zeros_like(wide[:, :edge, :])
    wide[:, edge + rows :, :] = jnp.zeros_like(wide[:, edge + rows :, :])
    wide[:, edge : edge + rows, :] = padded(f_ref[...].astype(F32).reshape(bricks, rows, width), channels)
    own = c_ref[...].astype(F32)
    none = jnp.zeros((edge, 1, width), F32)
    tall[:, :, edge : 2 * edge, :] = own
    tall[0, :, edge - 1 : edge, :] = none
    tall[1, :, edge - 1 : edge, :] = own[0, :, edge - 1 :, :]
    tall[0, :, 2 * edge : 2 * edge + 1, :] = own[1, :, 0:1, :]
    tall[1, :, 2 * edge : 2 * edge + 1, :] = none
    left, right = [], []
    for tap in range(3):
        value = wide[:, edge * tap : edge * tap + rows, :].reshape(bricks * rows, -1)
        left.append(stacked(value, lanes, 2 * lanes))
        value = tall[:, :, edge + 1 - tap : 2 * edge + 1 - tap, :].reshape(bricks * rows, width)
        right.append(stacked(value, lanes, lanes))
    out_ref[...] = outer(jnp.concatenate(left, axis=1), jnp.concatenate(right, axis=1))


def kernel_grad_kernel(roles, tiles, channels, joined, f_ref, c_ref, local_ref, *refs):
    roles = Roles(roles, tiles)
    counts = roles.counts
    x_refs = refs[: counts[0]]
    near = counts[0] + counts[1]
    y_refs = refs[counts[0] : near]
    keep_ref, send_ref = refs[near : near + 2]
    hops_at = near + 2 + (0 if joined else counts[0])
    line_refs = refs[near + 2 : hops_at]
    hop_refs = refs[hops_at : hops_at + counts[2]]
    tall, row_ref, packed, lines = refs[hops_at + counts[2] :]
    count = keep_ref.shape[0]
    bricks, edge, _, width = f_ref.shape
    lanes = 2 * channels
    planes = []
    for side in range(2):
        plane = jnp.zeros((bricks, edge, width), F32)
        for number, ref in enumerate(x_refs):
            plane = jnp.where(roles.side(0, number, side), ref[0].astype(F32), plane)
        planes.append(plane)
    halo = {}
    for side in range(2):
        for source in range(2):
            row = jnp.zeros((edge, width), F32)
            for number, ref in enumerate(y_refs):
                row = jnp.where(roles.side(1, number, side), ref[source].astype(F32), row)
            halo[source, side] = row
    across = []
    for side, plane in enumerate(planes):
        at = (edge - 1) * side
        own = [c_ref[brick, at].astype(F32) for brick in range(bricks)]
        below = (halo[1, 0][at : at + 1], own[0][edge - 1 :])
        above = (own[1][0:1], halo[1, 1][at : at + 1])
        for brick in range(bricks):
            tall[brick, edge : 2 * edge, :] = own[brick]
            tall[brick, edge - 1 : edge, :] = below[brick]
            tall[brick, 2 * edge : 2 * edge + 1, :] = above[brick]
        left = stacked(padded(plane, channels).reshape(bricks * edge, -1), lanes, 2 * lanes)
        right = []
        for tap in range(3):
            value = tall[:, edge + 1 - tap : 2 * edge + 1 - tap, :].reshape(bricks * edge, width)
            right.append(stacked(value, lanes, lanes))
        across.append(outer(left, jnp.concatenate(right, axis=1)))
    along = []
    row_ref[...] = jnp.zeros_like(row_ref)
    for side in range(2):
        row_ref[edge : 2 * edge, :] = padded(f_ref[side].astype(F32)[:, (edge - 1) * side, :], channels)
        left = [stacked(row_ref[edge - 1 + tap : 2 * edge - 1 + tap, :], lanes, 2 * lanes) for tap in range(3)]
        along.append(outer(jnp.concatenate(left, axis=1), stacked(halo[1, side], lanes, lanes)))
    half = 3 * channels // 2
    low = lax.broadcasted_iota(jnp.int32, (half, lanes), 1) < channels
    for row in range(3):
        for col in range(3):
            block = local_ref[2 * lanes * row : 2 * lanes * (row + 1), lanes * col : lanes * (col + 1)]
            if row != 1:
                block = block + across[row // 2][:, lanes * col : lanes * (col + 1)]
            if col != 1:
                block = block + along[1 - col // 2][2 * lanes * row : 2 * lanes * (row + 1)]
            moved = pltpu.roll(block, channels, 1)
            first = block[:half] + moved[channels : channels + half]
            second = moved[half : 2 * half] + block[channels + half :]
            at = half * (3 * row + col)
            packed[at : at + half, :] = jnp.where(low, first, second)
    for number in range(counts[0]):
        up = roles.side(0, number, 1)
        for (source, side), row in halo.items():
            store_line(lines, 2 * source + side, jnp.where(up, row[edge - 1 : edge], row[0:1]))
        if joined:
            send_ref[count:, :] = lines[...]
        else:
            line_refs[number][...] = lines[...].astype(BF16)
    for number, out in enumerate(hop_refs):
        line = jnp.zeros((1, width), F32)
        for across in range(2):
            for side in range(2):
                at = (edge - 1) * side
                hit = roles.any(2, number, lambda role: role == (across, side))
                line = jnp.where(hit, planes[across][side, at : at + 1, :], line)
        store_line(lines, 0, line)
        out[...] = lines[...].astype(BF16)
    own = my_half()
    keep_ref[...] = packed[pl.ds(pl.multiple_of(own * count, 8), count), :]
    send_ref[:count, :] = packed[pl.ds(pl.multiple_of((1 - own) * count, 8), count), :]


def conv_kernel(roles, tiles, channels, source, ways, v_ref, *refs):
    roles = Roles(roles, tiles)
    counts = roles.counts
    x_refs = refs[: counts[0]]
    y_refs = refs[counts[0] : counts[0] + counts[1]]
    near = counts[0] + counts[1]
    hops_at = near + counts[0] * ways
    line_refs = refs[near:hops_at]
    hop_refs = refs[hops_at : hops_at + counts[2]]
    weight_ref, out_ref, ext = refs[hops_at + counts[2] :]
    bricks, edge, _, width = v_ref.shape
    rows = edge * edge
    first, last = edge, 2 * edge - 1
    ext[:, 1 : edge + 1, first : last + 1, :] = padded(v_ref[...].astype(F32), channels)
    for side in range(2):
        plane = jnp.zeros((bricks, edge, width), F32)
        for number, ref in enumerate(x_refs):
            plane = jnp.where(roles.side(0, number, side), ref[source].astype(F32), plane)
        plane = padded(plane, channels)
        for brick in range(bricks):
            ext[brick, side * (edge + 1), first : last + 1, :] = plane[brick]
    each = width // line_refs[0].shape[1]
    arrived = [ref[ref.shape[0] - 4 * each :, :].astype(F32) for ref in line_refs]
    if ways == 2:
        arrived = [jnp.where(my_half() == 0, *arrived)]
    hops = [load_line(ref[...].astype(F32), 0, each) for ref in hop_refs]
    for side in range(2):
        row = jnp.zeros((edge, width), F32)
        for number, ref in enumerate(y_refs):
            row = jnp.where(roles.side(1, number, side), ref[source].astype(F32), row)
        at = last + 1 if side else first - 1
        row = padded(row, channels)
        ext[side, 1 : edge + 1, at : at + 1, :] = row[:, None, :]
        for across in range(2):
            line = jnp.zeros((1, width), F32)
            for number, value in enumerate(arrived):
                line = jnp.where(roles.side(0, number, across), load_line(value, 2 * source + side, each), line)
            if source == 0:
                line = masked(roles.linked(side), line)
                for number, value in enumerate(hops):
                    line = jnp.where(roles.any(3, number, lambda role: role == (across, side)), value, line)
            ext[side, across * (edge + 1), at : at + 1, :] = padded(line, channels)
    ext[1, :, first - 1 : first, :] = ext[0, :, last : last + 1, :]
    ext[0, :, last + 1 : last + 2, :] = ext[1, :, first : first + 1, :]
    lanes = 2 * channels
    pairs = width // lanes
    total = jnp.zeros((pairs * bricks * rows, lanes), F32)
    contract = 0 if source == 0 else 1
    for col in range(3):
        for row in range(3):
            value = ext[:, row : row + edge, first - 1 + col : last + col, :]
            value = value.reshape(bricks * rows, -1).astype(BF16)
            left = jnp.concatenate([value[:, lanes * k : lanes * (k + 2)] for k in range(pairs)], axis=0)
            total = total + lax.dot_general(
                left, weight_ref[3 * row + col], (((1,), (contract,)), ((), ())), preferred_element_type=F32
            )
    for k in range(pairs):
        out_ref[:, lanes * k : lanes * (k + 1)] = total[bricks * rows * k : bricks * rows * (k + 1)].astype(BF16)


def unpack_kernel(factor, own_ref, other_ref, out_hbm, out_ref, sent):
    count = own_ref.shape[0]
    first_half = my_half() == 0
    taps, rows, channels = out_ref.shape
    half = rows // 2

    def packed(start, stop):
        pieces = []
        for low, ref, other in ((0, own_ref, other_ref), (count, other_ref, own_ref)):
            here = slice(max(start - low, 0), min(stop - low, count))
            if here.start < here.stop:
                pieces.append(jnp.where(first_half, ref[here], other[here]))
        return jnp.concatenate(pieces, axis=0) * factor

    copies = []
    for tap in range(taps):
        block = packed(half * tap, half * (tap + 1))
        out_ref[tap, :half, :] = block[:, :channels]
        out_ref[tap, half:, :] = pltpu.roll(block, channels, 1)[:, :channels]
        copies.append(pltpu.make_async_copy(out_ref.at[tap], out_hbm.at[tap], sent.at[tap]))
        copies[-1].start()
    for copy in copies:
        copy.wait()


VMEM = pl.BlockSpec(memory_space=pltpu.VMEM)
HBM = pl.BlockSpec(memory_space=pltpu.HBM)


def call(kernel, in_specs, out_shapes, scratch=(), flops=0, name=None, vmem=24 * 2**20, out=None):
    several = isinstance(out_shapes, list)
    return pl.pallas_call(
        kernel,
        in_specs=in_specs,
        out_specs=[VMEM] * len(out_shapes) if several else (out or VMEM),
        out_shape=out_shapes,
        scratch_shapes=list(scratch),
        compiler_params=pltpu.CompilerParams(vmem_limit_bytes=vmem),
        cost_estimate=pl.CostEstimate(flops=flops, bytes_accessed=2**20, transcendentals=0),
        name=name,
    )


def body(tiles, features, cotangent, kernel, neighbours):
    pairs, roles, meetings = make_plan(tiles)
    counts = [len(kind) for kind in pairs]
    bricks, edge = features.shape[1:3]
    width = features.shape[-1]
    channels = kernel.shape[-1]
    rows = edge * edge
    lanes = 2 * channels
    shape = jax.ShapeDtypeStruct
    f = features.reshape(bricks, edge, edge, width)
    c = cotangent.reshape(bricks, edge, edge, width)
    links = neighbours.reshape(bricks, 6)

    near = counts[0] + counts[1]
    *faces, f, c = call(
        functools.partial(faces_kernel, roles, tiles),
        [HBM, HBM, HBM],
        [pltpu.VMEM((2, bricks, edge, width), BF16)] * counts[0]
        + [pltpu.VMEM((2, edge, width), BF16)] * counts[1]
        + [pltpu.VMEM(f.shape, BF16), pltpu.VMEM(c.shape, BF16)],
        [pltpu.SMEM(links.shape, jnp.int32), pltpu.SemaphoreType.DMA((3,))],
        name="faces",
        vmem=None,
    )(f, c, links)
    got = [lax.ppermute(x, ("space", "dp"), one) for x, one in zip(faces, pairs[0] + pairs[1])]
    bits = [1 << number for number in range(tiles.bit_length() - 1)]
    orders = [bits, bits]
    wire = BF16 if len(bits) <= 3 else F32
    shared = [bit for bit in bits if meetings == [[(i, i ^ bit) for i in range(tiles)]]]
    joined = bool(shared) and len(bits) == 3
    if joined:
        first, last = (bit for bit in bits if bit not in shared)
        orders = [shared + [last, first], [first] + shared + [last]]
    count = 27 * channels * channels // lanes // 2
    line_rows = 4 * width // lanes
    local = call(
        functools.partial(local_grad_kernel, channels),
        [VMEM, VMEM],
        pltpu.VMEM((6 * lanes, 3 * lanes), F32),
        [
            pltpu.VMEM((bricks, rows + 2 * edge, width + lanes), F32),
            pltpu.VMEM((bricks, edge, 3 * edge, width), F32),
        ],
        flops=2 * 768 * 384 * 512,
        name="local_grad",
    )(f, c)
    keep, send, *lines = call(
        functools.partial(kernel_grad_kernel, roles, tiles, channels, joined),
        [VMEM] * (3 + near),
        [shape((count, lanes), F32), shape((count + line_rows * joined, lanes), F32)]
        + [shape((line_rows, lanes), BF16)] * (counts[2] if joined else counts[0] + counts[2]),
        [
            pltpu.VMEM((bricks, 3 * edge, width), F32),
            pltpu.VMEM((3 * edge, width + lanes), F32),
            pltpu.VMEM((2 * count, lanes), F32),
            pltpu.VMEM((line_rows, lanes), F32),
        ],
        flops=2 * 768 * 384 * 64,
        name="kernel_grad",
    )(f, c, local, *got)

    forward, backward = call(
        weights_kernel,
        [VMEM],
        [shape((9, 4 * channels, lanes), BF16), shape((9, lanes, 4 * channels), BF16)],
        [pltpu.VMEM((27, channels, lanes), F32)],
        name="weights",
    )(kernel.reshape(27, channels, channels))

    def conv(source, x, weight):
        return call(
            functools.partial(conv_kernel, roles, tiles, channels, source, ready),
            [VMEM] * (2 + len(got)),
            shape((bricks * rows, width), BF16),
            [pltpu.VMEM((bricks, edge + 2, 3 * edge, width + lanes), F32)],
            flops=2 * 512 * 256 * 128 * 9,
            name="response" if source == 0 else "feature_grad",
        )(x, *got, weight)

    cores = lax.axis_size("dp")
    swap = [(0, 1), (1, 0)]
    summed = lax.ppermute(send, "dp", swap)
    part = keep + summed[:count]
    if not joined:
        got += [lax.ppermute(x, ("space", "dp"), one) for x, one in zip(lines, pairs[0])]
        lines = lines[counts[0] :]
    hops = [lax.ppermute(x, ("space", "dp"), one) for x, one in zip(lines, pairs[2])]
    ready = 2 if joined else 1
    for number in range(len(bits)):
        step = [
            tuple(end * cores + half_of(end, half) for end in (tile, tile ^ order[number]))
            for tile in range(tiles)
            for half, order in enumerate(orders)
        ]
        mine = part.astype(wire)
        carries = joined and number < ready
        if carries:
            mine = jnp.concatenate([mine, summed[count:].astype(wire)], axis=0)
        if number == ready:
            mine, hops, forward, backward = lax.optimization_barrier((mine, hops, forward, backward))
        else:
            mine = lax.optimization_barrier(mine)
        if number == ready:
            got += hops
            response = conv(0, f, forward)
            feature_grad = conv(1, c, backward)
        theirs = lax.ppermute(mine, ("space", "dp"), step)
        if carries:
            got.append(theirs)
            mine, theirs = mine[:count], theirs[:count]
        part = mine.astype(F32) + theirs.astype(F32)
    part, response = lax.optimization_barrier((part, response))
    other = lax.ppermute(part, "dp", swap)
    other, feature_grad = lax.optimization_barrier((other, feature_grad))
    response, feature_grad = (x.reshape(features.shape) for x in (response, feature_grad))
    cells = bricks * tiles * lax.axis_size("dp") * edge**3
    kernel_grad = call(
        functools.partial(unpack_kernel, 1.0 / math.sqrt(cells)),
        [VMEM, VMEM],
        shape((9, 3 * channels, channels), F32),
        [pltpu.VMEM((9, 3 * channels, channels), F32), pltpu.SemaphoreType.DMA((9,))],
        name="unpack",
        out=HBM,
    )(part, other).reshape(kernel.shape)
    return response, feature_grad, kernel_grad


def solution(mesh):
    bricks_spec = P(("groups", "dp"), "space", None, None, None)
    return jax.shard_map(
        functools.partial(body, mesh.shape["space"]),
        mesh=mesh,
        in_specs=(bricks_spec, bricks_spec, P(), P(("groups", "dp"), "space", None)),
        out_specs=(bricks_spec, bricks_spec, P("groups", None, None, None, None)),
        check_vma=False,
    )
```

```python
import functools
import math

import jax
import jax.numpy as jnp
from jax import lax
from jax.experimental import pallas as pl
from jax.experimental.pallas import tpu as pltpu
from jax.sharding import PartitionSpec as P

TILES_Y = 4
F32 = jnp.float32
BF16 = jnp.bfloat16


def step_y(tile, sign, tiles):
    column = (tile + TILES_Y // 2) % TILES_Y + sign
    near = tile + sign
    return near if 0 <= column < TILES_Y and 0 <= near < tiles else None


def step_x(tile, sign, tiles):
    near = tile + sign * TILES_Y
    return near if 0 <= near < tiles else None


def rounds(edges):
    found = []
    for low, high in edges:
        for one in found:
            if low not in one and high not in one:
                break
        else:
            one = {}
            found.append(one)
        one[low] = (high, 1)
        one[high] = (low, 0)
    return found


def detours(tiles):
    found = []
    for tile in range(tiles):
        for across in range(2):
            for along in range(2):
                sender = step_y(tile, 2 * along - 1, tiles)
                if sender is None or step_x(sender, 2 * across - 1, tiles) is None:
                    continue
                if step_x(tile, 2 * across - 1, tiles) is not None:
                    continue
                for one in found:
                    if all(hop[0] != sender and hop[1] != tile for hop in one):
                        break
                else:
                    one = []
                    found.append(one)
                one.append((sender, tile, across, along))
    return found


def completed(pairs, tiles):
    idle = [tile for tile in range(tiles) if all(tile != a for a, _ in pairs) and all(tile != b for _, b in pairs)]
    active = [(2 * a + core, 2 * b + core) for a, b in pairs for core in range(2)]
    return sorted(active + [(2 * tile + core, 2 * tile + 1 - core) for tile in idle for core in range(2)])


def make_plan(tiles):
    def edges(step):
        return [(tile, step(tile, 1, tiles)) for tile in range(tiles) if step(tile, 1, tiles) is not None]

    along_x, along_y, hops = rounds(edges(step_x)), rounds(edges(step_y)), detours(tiles)
    pairs = [[[(tile, one[tile][0]) for tile in sorted(one)] for one in kind] for kind in (along_x, along_y)]
    pairs.append([[hop[:2] for hop in one] for one in hops])
    meetings = pairs[0]
    pairs = [[completed(one, tiles) for one in kind] for kind in pairs]
    roles = [[{tile: one[tile][1] for tile in one} for one in kind] for kind in (along_x, along_y)]
    roles.append([{hop[0]: (hop[2], 1 - hop[3]) for hop in one} for one in hops])
    roles.append([{hop[1]: hop[2:] for hop in one} for one in hops])
    return pairs, roles, meetings


class Roles:
    def __init__(self, roles, tiles):
        self.roles, self.tiles = roles, tiles
        self.counts = [len(kind) for kind in roles[:3]]
        self.tile = lax.axis_index("space")

    def any(self, kind, number, test):
        words = []
        for start in range(0, self.tiles, 32):
            here = [t for t in range(start, min(start + 32, self.tiles)) if t in self.roles[kind][number]]
            word = sum(1 << (t - start) for t in here if test(self.roles[kind][number][t]))
            words.append(word - (1 << 32) if word >> 31 else word)
        word = jnp.int32(words[0])
        for number, other in enumerate(words[1:], 1):
            word = jnp.where(self.tile // 32 == number, jnp.int32(other), word)
        return (lax.shift_right_logical(word, self.tile % 32) & 1) == 1

    def side(self, kind, number, side):
        return self.any(kind, number, lambda role: role == side)

    def linked(self, side):
        found = jnp.bool_(False)
        for number in range(self.counts[1]):
            found = found | self.side(1, number, side)
        return found


def half_of(tile, core):
    for shift in (16, 8, 4, 2, 1):
        tile = tile ^ (tile >> shift)
    return core ^ (tile & 1)


def my_half():
    return half_of(lax.axis_index("space"), lax.axis_index("dp"))


def masked(keep, x):
    return jnp.where(keep, x, jnp.zeros_like(x))


def faces_kernel(roles, tiles, f_hbm, c_hbm, link_hbm, *refs):
    roles = Roles(roles, tiles)
    *out_refs, f_ref, c_ref, link_ref, arrived = refs
    x_refs, y_refs = out_refs[: roles.counts[0]], out_refs[roles.counts[0] :]
    edge = f_hbm.shape[1]
    copies = [
        pltpu.make_async_copy(source, target, arrived.at[number])
        for number, (source, target) in enumerate(((link_hbm, link_ref), (f_hbm, f_ref), (c_hbm, c_ref)))
    ]
    for copy in copies:
        copy.start()
    for copy in copies:
        copy.wait()
    linked = [[link_ref[brick, way] >= 0 for way in range(4)] for brick in range(2)]
    for number, out in enumerate(x_refs):
        up = roles.side(0, number, 1)
        plane = jnp.where(up, edge - 1, 0)
        for brick in range(2):
            keep = jnp.where(up, linked[brick][1], linked[brick][0])
            for source, ref in enumerate((f_ref, c_ref)):
                out[source, brick] = masked(keep, ref[brick, plane])

    rows = []
    for ref in (f_ref, c_ref):
        low = masked(linked[0][2], ref[0].astype(F32)[:, 0, :])
        high = masked(linked[1][3], ref[1].astype(F32)[:, edge - 1, :])
        rows.append((low, high))
    for number, out in enumerate(y_refs):
        up = roles.side(1, number, 1)
        for source, (low, high) in enumerate(rows):
            out[source] = jnp.where(up, high, low).astype(BF16)


def padded(x, channels):
    zeros = jnp.zeros(x.shape[:-1] + (2 * channels,), F32)
    return pltpu.roll(jnp.concatenate([x, zeros], axis=-1), channels, x.ndim - 1)


def weights_kernel(kernel_ref, forward_ref, backward_ref, wide):
    channels = kernel_ref.shape[-1]
    wide[...] = jnp.zeros_like(wide)
    wide[:, :, :channels] = kernel_ref[...].astype(F32)
    for tap in range(9):
        plain = [wide[3 * tap + d] for d in range(3)]
        moved = [pltpu.roll(x, channels, 1) for x in plain]
        steps = (plain[0], plain[1] + moved[0], plain[2] + moved[1], moved[2])
        for number, block in enumerate(steps):
            forward_ref[tap, channels * number : channels * (number + 1), :] = block.astype(BF16)
        last = 8 - tap
        lanes = 2 * channels
        backward_ref[last, :channels, :lanes] = (plain[2] + moved[1]).astype(BF16)
        backward_ref[last, :channels, lanes:] = plain[0].astype(BF16)
        backward_ref[last, channels:, :lanes] = moved[2].astype(BF16)
        backward_ref[last, channels:, lanes:] = (plain[1] + moved[0]).astype(BF16)


def store_line(lines, number, line):
    lanes = lines.shape[1]
    each = line.shape[1] // lanes
    for k in range(each):
        lines[each * number + k : each * number + k + 1, :] = line[:, lanes * k : lanes * (k + 1)]


def load_line(rows, number, each):
    return jnp.concatenate([rows[each * number + k : each * number + k + 1] for k in range(each)], axis=1)


def stacked(rows, lanes, wide):
    steps = range((rows.shape[1] - wide) // lanes + 1)
    return jnp.concatenate([rows[:, lanes * k : lanes * k + wide] for k in steps], axis=0).astype(BF16)


def outer(left, right):
    return lax.dot_general(left, right, (((0,), (0,)), ((), ())), preferred_element_type=F32)


def local_grad_kernel(channels, f_ref, c_ref, out_ref, wide, tall):
    bricks, edge, _, width = f_ref.shape
    rows = edge * edge
    lanes = 2 * channels
    wide[:, :edge, :] = jnp.zeros_like(wide[:, :edge, :])
    wide[:, edge + rows :, :] = jnp.zeros_like(wide[:, edge + rows :, :])
    wide[:, edge : edge + rows, :] = padded(f_ref[...].astype(F32).reshape(bricks, rows, width), channels)
    own = c_ref[...].astype(F32)
    none = jnp.zeros((edge, 1, width), F32)
    tall[:, :, edge : 2 * edge, :] = own
    tall[0, :, edge - 1 : edge, :] = none
    tall[1, :, edge - 1 : edge, :] = own[0, :, edge - 1 :, :]
    tall[0, :, 2 * edge : 2 * edge + 1, :] = own[1, :, 0:1, :]
    tall[1, :, 2 * edge : 2 * edge + 1, :] = none
    left, right = [], []
    for tap in range(3):
        value = wide[:, edge * tap : edge * tap + rows, :].reshape(bricks * rows, -1)
        left.append(stacked(value, lanes, 2 * lanes))
        value = tall[:, :, edge + 1 - tap : 2 * edge + 1 - tap, :].reshape(bricks * rows, width)
        right.append(stacked(value, lanes, lanes))
    out_ref[...] = outer(jnp.concatenate(left, axis=1), jnp.concatenate(right, axis=1))


def kernel_grad_kernel(roles, tiles, channels, joined, f_ref, c_ref, local_ref, *refs):
    roles = Roles(roles, tiles)
    counts = roles.counts
    x_refs = refs[: counts[0]]
    near = counts[0] + counts[1]
    y_refs = refs[counts[0] : near]
    keep_ref, send_ref = refs[near : near + 2]
    hops_at = near + 2 + (0 if joined else counts[0])
    line_refs = refs[near + 2 : hops_at]
    hop_refs = refs[hops_at : hops_at + counts[2]]
    tall, row_ref, packed, lines = refs[hops_at + counts[2] :]
    count = keep_ref.shape[0]
    bricks, edge, _, width = f_ref.shape
    lanes = 2 * channels
    planes = []
    for side in range(2):
        plane = jnp.zeros((bricks, edge, width), F32)
        for number, ref in enumerate(x_refs):
            plane = jnp.where(roles.side(0, number, side), ref[0].astype(F32), plane)
        planes.append(plane)
    halo = {}
    for side in range(2):
        for source in range(2):
            row = jnp.zeros((edge, width), F32)
            for number, ref in enumerate(y_refs):
                row = jnp.where(roles.side(1, number, side), ref[source].astype(F32), row)
            halo[source, side] = row
    across = []
    for side, plane in enumerate(planes):
        at = (edge - 1) * side
        own = [c_ref[brick, at].astype(F32) for brick in range(bricks)]
        below = (halo[1, 0][at : at + 1], own[0][edge - 1 :])
        above = (own[1][0:1], halo[1, 1][at : at + 1])
        for brick in range(bricks):
            tall[brick, edge : 2 * edge, :] = own[brick]
            tall[brick, edge - 1 : edge, :] = below[brick]
            tall[brick, 2 * edge : 2 * edge + 1, :] = above[brick]
        left = stacked(padded(plane, channels).reshape(bricks * edge, -1), lanes, 2 * lanes)
        right = []
        for tap in range(3):
            value = tall[:, edge + 1 - tap : 2 * edge + 1 - tap, :].reshape(bricks * edge, width)
            right.append(stacked(value, lanes, lanes))
        across.append(outer(left, jnp.concatenate(right, axis=1)))
    along = []
    row_ref[...] = jnp.zeros_like(row_ref)
    for side in range(2):
        row_ref[edge : 2 * edge, :] = padded(f_ref[side].astype(F32)[:, (edge - 1) * side, :], channels)
        left = [stacked(row_ref[edge - 1 + tap : 2 * edge - 1 + tap, :], lanes, 2 * lanes) for tap in range(3)]
        along.append(outer(jnp.concatenate(left, axis=1), stacked(halo[1, side], lanes, lanes)))
    half = 3 * channels // 2
    low = lax.broadcasted_iota(jnp.int32, (half, lanes), 1) < channels
    for row in range(3):
        for col in range(3):
            block = local_ref[2 * lanes * row : 2 * lanes * (row + 1), lanes * col : lanes * (col + 1)]
            if row != 1:
                block = block + across[row // 2][:, lanes * col : lanes * (col + 1)]
            if col != 1:
                block = block + along[1 - col // 2][2 * lanes * row : 2 * lanes * (row + 1)]
            moved = pltpu.roll(block, channels, 1)
            first = block[:half] + moved[channels : channels + half]
            second = moved[half : 2 * half] + block[channels + half :]
            at = half * (3 * row + col)
            packed[at : at + half, :] = jnp.where(low, first, second)
    for number in range(counts[0]):
        up = roles.side(0, number, 1)
        for (source, side), row in halo.items():
            store_line(lines, 2 * source + side, jnp.where(up, row[edge - 1 : edge], row[0:1]))
        if joined:
            send_ref[count:, :] = lines[...].astype(send_ref.dtype)
        else:
            line_refs[number][...] = lines[...].astype(BF16)
    for number, out in enumerate(hop_refs):
        line = jnp.zeros((1, width), F32)
        for across in range(2):
            for side in range(2):
                at = (edge - 1) * side
                hit = roles.any(2, number, lambda role: role == (across, side))
                line = jnp.where(hit, planes[across][side, at : at + 1, :], line)
        store_line(lines, 0, line)
        out[...] = lines[...].astype(BF16)
    own = my_half()
    keep_ref[...] = packed[pl.ds(pl.multiple_of(own * count, 8), count), :]
    send_ref[:count, :] = packed[pl.ds(pl.multiple_of((1 - own) * count, 8), count), :].astype(send_ref.dtype)


def conv_kernel(roles, tiles, channels, source, ways, v_ref, *refs):
    roles = Roles(roles, tiles)
    counts = roles.counts
    x_refs = refs[: counts[0]]
    y_refs = refs[counts[0] : counts[0] + counts[1]]
    near = counts[0] + counts[1]
    hops_at = near + counts[0] * ways
    line_refs = refs[near:hops_at]
    hop_refs = refs[hops_at : hops_at + counts[2]]
    weight_ref, out_ref, ext = refs[hops_at + counts[2] :]
    bricks, edge, _, width = v_ref.shape
    rows = edge * edge
    first, last = edge, 2 * edge - 1
    ext[:, 1 : edge + 1, first : last + 1, :] = padded(v_ref[...].astype(F32), channels)
    for side in range(2):
        plane = jnp.zeros((bricks, edge, width), F32)
        for number, ref in enumerate(x_refs):
            plane = jnp.where(roles.side(0, number, side), ref[source].astype(F32), plane)
        plane = padded(plane, channels)
        for brick in range(bricks):
            ext[brick, side * (edge + 1), first : last + 1, :] = plane[brick]
    each = width // line_refs[0].shape[1]
    arrived = [ref[ref.shape[0] - 4 * each :, :].astype(F32) for ref in line_refs]
    if ways == 2:
        arrived = [jnp.where(my_half() == 0, *arrived)]
    hops = [load_line(ref[...].astype(F32), 0, each) for ref in hop_refs]
    for side in range(2):
        row = jnp.zeros((edge, width), F32)
        for number, ref in enumerate(y_refs):
            row = jnp.where(roles.side(1, number, side), ref[source].astype(F32), row)
        at = last + 1 if side else first - 1
        row = padded(row, channels)
        ext[side, 1 : edge + 1, at : at + 1, :] = row[:, None, :]
        for across in range(2):
            line = jnp.zeros((1, width), F32)
            for number, value in enumerate(arrived):
                line = jnp.where(roles.side(0, number, across), load_line(value, 2 * source + side, each), line)
            if source == 0:
                line = masked(roles.linked(side), line)
                for number, value in enumerate(hops):
                    line = jnp.where(roles.any(3, number, lambda role: role == (across, side)), value, line)
            ext[side, across * (edge + 1), at : at + 1, :] = padded(line, channels)
    ext[1, :, first - 1 : first, :] = ext[0, :, last : last + 1, :]
    ext[0, :, last + 1 : last + 2, :] = ext[1, :, first : first + 1, :]
    lanes = 2 * channels
    pairs = width // lanes
    total = jnp.zeros((pairs * bricks * rows, lanes), F32)
    contract = 0 if source == 0 else 1
    for col in range(3):
        for row in range(3):
            value = ext[:, row : row + edge, first - 1 + col : last + col, :]
            value = value.reshape(bricks * rows, -1).astype(BF16)
            left = jnp.concatenate([value[:, lanes * k : lanes * (k + 2)] for k in range(pairs)], axis=0)
            total = total + lax.dot_general(
                left, weight_ref[3 * row + col], (((1,), (contract,)), ((), ())), preferred_element_type=F32
            )
    for k in range(pairs):
        out_ref[:, lanes * k : lanes * (k + 1)] = total[bricks * rows * k : bricks * rows * (k + 1)].astype(BF16)


def unpack_kernel(factor, own_ref, other_ref, out_hbm, out_ref, sent):
    count = own_ref.shape[0]
    first_half = my_half() == 0
    taps, rows, channels = out_ref.shape
    half = rows // 2

    def packed(start, stop):
        pieces = []
        for low, ref, other in ((0, own_ref, other_ref), (count, other_ref, own_ref)):
            here = slice(max(start - low, 0), min(stop - low, count))
            if here.start < here.stop:
                pieces.append(jnp.where(first_half, ref[here], other[here]))
        return jnp.concatenate(pieces, axis=0) * factor

    copies = []
    for tap in range(taps):
        block = packed(half * tap, half * (tap + 1))
        out_ref[tap, :half, :] = block[:, :channels]
        out_ref[tap, half:, :] = pltpu.roll(block, channels, 1)[:, :channels]
        copies.append(pltpu.make_async_copy(out_ref.at[tap], out_hbm.at[tap], sent.at[tap]))
        copies[-1].start()
    for copy in copies:
        copy.wait()


VMEM = pl.BlockSpec(memory_space=pltpu.VMEM)
HBM = pl.BlockSpec(memory_space=pltpu.HBM)


def call(kernel, in_specs, out_shapes, scratch=(), flops=0, name=None, vmem=24 * 2**20, out=None):
    several = isinstance(out_shapes, list)
    return pl.pallas_call(
        kernel,
        in_specs=in_specs,
        out_specs=[VMEM] * len(out_shapes) if several else (out or VMEM),
        out_shape=out_shapes,
        scratch_shapes=list(scratch),
        compiler_params=pltpu.CompilerParams(vmem_limit_bytes=vmem),
        cost_estimate=pl.CostEstimate(flops=flops, bytes_accessed=2**20, transcendentals=0),
        name=name,
    )


def body(tiles, features, cotangent, kernel, neighbours):
    pairs, roles, meetings = make_plan(tiles)
    counts = [len(kind) for kind in pairs]
    bricks, edge = features.shape[1:3]
    width = features.shape[-1]
    channels = kernel.shape[-1]
    rows = edge * edge
    lanes = 2 * channels
    shape = jax.ShapeDtypeStruct
    f = features.reshape(bricks, edge, edge, width)
    c = cotangent.reshape(bricks, edge, edge, width)
    links = neighbours.reshape(bricks, 6)

    near = counts[0] + counts[1]
    *faces, f, c = call(
        functools.partial(faces_kernel, roles, tiles),
        [HBM, HBM, HBM],
        [pltpu.VMEM((2, bricks, edge, width), BF16)] * counts[0]
        + [pltpu.VMEM((2, edge, width), BF16)] * counts[1]
        + [pltpu.VMEM(f.shape, BF16), pltpu.VMEM(c.shape, BF16)],
        [pltpu.SMEM(links.shape, jnp.int32), pltpu.SemaphoreType.DMA((3,))],
        name="faces",
        vmem=None,
    )(f, c, links)
    got = [lax.ppermute(x, ("space", "dp"), one) for x, one in zip(faces, pairs[0] + pairs[1])]
    bits = [1 << number for number in range(tiles.bit_length() - 1)]
    orders = [bits, bits]
    wire = BF16 if len(bits) <= 3 else F32
    shared = [bit for bit in bits if meetings == [[(i, i ^ bit) for i in range(tiles)]]]
    joined = bool(shared) and len(bits) == 3
    if joined:
        first, last = (bit for bit in bits if bit not in shared)
        orders = [shared + [last, first], [first] + shared + [last]]
    count = 27 * channels * channels // lanes // 2
    line_rows = 4 * width // lanes
    local = call(
        functools.partial(local_grad_kernel, channels),
        [VMEM, VMEM],
        pltpu.VMEM((6 * lanes, 3 * lanes), F32),
        [
            pltpu.VMEM((bricks, rows + 2 * edge, width + lanes), F32),
            pltpu.VMEM((bricks, edge, 3 * edge, width), F32),
        ],
        flops=2 * 768 * 384 * 512,
        name="local_grad",
    )(f, c)
    keep, send, *lines = call(
        functools.partial(kernel_grad_kernel, roles, tiles, channels, joined),
        [VMEM] * (3 + near),
        [shape((count, lanes), F32), shape((count + line_rows * joined, lanes), wire)]
        + [shape((line_rows, lanes), BF16)] * (counts[2] if joined else counts[0] + counts[2]),
        [
            pltpu.VMEM((bricks, 3 * edge, width), F32),
            pltpu.VMEM((3 * edge, width + lanes), F32),
            pltpu.VMEM((2 * count, lanes), F32),
            pltpu.VMEM((line_rows, lanes), F32),
        ],
        flops=2 * 768 * 384 * 64,
        name="kernel_grad",
    )(f, c, local, *got)

    forward, backward = call(
        weights_kernel,
        [VMEM],
        [shape((9, 4 * channels, lanes), BF16), shape((9, lanes, 4 * channels), BF16)],
        [pltpu.VMEM((27, channels, lanes), F32)],
        name="weights",
    )(kernel.reshape(27, channels, channels))

    def conv(source, x, weight):
        return call(
            functools.partial(conv_kernel, roles, tiles, channels, source, ready),
            [VMEM] * (2 + len(got)),
            shape((bricks * rows, width), BF16),
            [pltpu.VMEM((bricks, edge + 2, 3 * edge, width + lanes), F32)],
            flops=2 * 512 * 256 * 128 * 9,
            name="response" if source == 0 else "feature_grad",
        )(x, *got, weight)

    cores = lax.axis_size("dp")
    swap = [(0, 1), (1, 0)]
    summed = lax.ppermute(send, "dp", swap)
    part = keep + summed[:count].astype(F32)
    if not joined:
        got += [lax.ppermute(x, ("space", "dp"), one) for x, one in zip(lines, pairs[0])]
        lines = lines[counts[0] :]
    hops = [lax.ppermute(x, ("space", "dp"), one) for x, one in zip(lines, pairs[2])]
    ready = 2 if joined else 1
    for number in range(len(bits)):
        step = [
            tuple(end * cores + half_of(end, half) for end in (tile, tile ^ order[number]))
            for tile in range(tiles)
            for half, order in enumerate(orders)
        ]
        mine = part.astype(wire)
        carries = joined and number < ready
        if carries:
            mine = jnp.concatenate([mine, summed[count:].astype(wire)], axis=0)
        if number == ready:
            mine, hops, forward, backward = lax.optimization_barrier((mine, hops, forward, backward))
        else:
            mine = lax.optimization_barrier(mine)
        if number == ready:
            got += hops
            response = conv(0, f, forward)
            feature_grad = conv(1, c, backward)
        theirs = lax.ppermute(mine, ("space", "dp"), step)
        if carries:
            got.append(theirs)
            mine, theirs = mine[:count], theirs[:count]
        part = mine.astype(F32) + theirs.astype(F32)
    part, response = lax.optimization_barrier((part, response))
    other = lax.ppermute(part, "dp", swap)
    other, feature_grad = lax.optimization_barrier((other, feature_grad))
    response, feature_grad = (x.reshape(features.shape) for x in (response, feature_grad))
    cells = bricks * tiles * lax.axis_size("dp") * edge**3
    kernel_grad = call(
        functools.partial(unpack_kernel, 1.0 / math.sqrt(cells)),
        [VMEM, VMEM],
        shape((9, 3 * channels, channels), F32),
        [pltpu.VMEM((9, 3 * channels, channels), F32), pltpu.SemaphoreType.DMA((9,))],
        name="unpack",
        out=HBM,
    )(part, other).reshape(kernel.shape)
    return response, feature_grad, kernel_grad


def solution(mesh):
    bricks_spec = P(("groups", "dp"), "space", None, None, None)
    return jax.shard_map(
        functools.partial(body, mesh.shape["space"]),
        mesh=mesh,
        in_specs=(bricks_spec, bricks_spec, P(), P(("groups", "dp"), "space", None)),
        out_specs=(bricks_spec, bricks_spec, P("groups", None, None, None, None)),
        check_vma=False,
    )
```
